256 devices in a mesh: grp: 16 (over z, core), blk: 16 (over y, x).
Axes of the slice: x: 4, y: 4, z: 8, core: 2. Of those that a mesh axis runs over, the one named last changes fastest.
Arguments:
- solid_fraction: float32 [384, 128, 2048], P('grp', 'blk'), may hold values from 0.2 to 1
- thermal_state: float32 [384, 128, 2048], P('grp', 'blk'), may hold values from -6 to 6
- target_heat_sensitivity: float32 [384, 128, 2048], P('grp', 'blk'), may hold values from -6 to 6
- coolant_coupling: float32 [384, 128, 2048], P('grp', 'blk'), may hold values from 0.25 to 2
- design_switch: int32 [16, 16, 8], P('grp', 'blk'), may hold values from 0 to 1, as said below
Outputs:
- sensitivity: float32 [384, 128, 2048], P('grp', 'blk')
The draws below stay inside these ranges and needn't reach their ends.
Inputs may be any that keep to these rules, and one draw needn't show every extreme that they name: `design_switch`: every device's 8 blocks hold at least one active block, and on some device all 8 are active.
All inputs are finite; a program needn't handle non-finite values.
Results may differ from the reference program's by a relative error of at most 0.0001.
Values sent between devices are 32-bit elements; how exact they have to be, the bound alone decides.
No kernel may reach another device: no remote copies, remote signals or barrier semaphores. Data moves between devices by JAX's collectives and lax.ppermute only.
A program may use at most 128 MiB of HBM per device.

```python
import math
import jax
import jax.numpy as jnp
from jax import lax

GRID_LENGTH_Z = 2048
BX = 256
RADIUS = 48
SWEEPS = 4
GRID_LENGTH_X = 384
GRID_LENGTH_Y = 128
NBX = 8
ZBLOCKS = 16
YBLOCKS = 16


def draw_design_switch(key, part):
    key_counts, key_full, key_order = jax.random.split(key, 3)
    devices_total = ZBLOCKS * YBLOCKS
    counts = jax.random.randint(key_counts, (devices_total,), 1, NBX + 1)
    full_device = jax.random.randint(key_full, (), 0, devices_total)
    counts = jnp.where(jnp.arange(devices_total) == full_device, NBX, counts)
    orders = jax.vmap(lambda single: jax.random.permutation(single, NBX))(jax.random.split(key_order, devices_total))
    marks = (orders < counts[:, None]).astype(jnp.int32)
    return marks.reshape(ZBLOCKS, YBLOCKS, NBX)


def steps_of(key, shape, pieces, low, high):
    loudness = 1.0
    for position, blocks in pieces:
        heights = jax.random.uniform(jax.random.fold_in(jax.random.fold_in(key, 6), position), (blocks,), jnp.float32, low / len(pieces), high / len(pieces))
        loudness = loudness * jnp.repeat(jnp.exp(heights), shape[position] // blocks).reshape((-1,) + (1,) * (len(shape) - 1 - position))
    return loudness


def gaussian(key, shape, scale, reach, cuts=(), kind=jnp.bfloat16):
    loudness = steps_of(key, shape, cuts, -0.22, 0.18) if cuts else 1.0
    array = jax.random.normal(key, shape, jnp.float32) * scale * loudness
    return jnp.minimum(jnp.maximum(array, -reach), reach).astype(kind)


def setup_inputs(seed: int = 0) -> dict:
    seeds = jax.random.split(jax.random.key(seed), 6)
    return {
        "solid_fraction": jnp.clip(0.2 + 0.8 * jax.random.uniform(seeds[0], (GRID_LENGTH_X, GRID_LENGTH_Y, GRID_LENGTH_Z), jnp.float32) ** steps_of(seeds[0], (GRID_LENGTH_X, GRID_LENGTH_Y, GRID_LENGTH_Z), ((0, 16), (1, 16)), -0.2, 0.2), 0.2, 1.0),
        "thermal_state": gaussian(seeds[1], (GRID_LENGTH_X, GRID_LENGTH_Y, GRID_LENGTH_Z), 1.0, 6.0, ((0, 16), (1, 16)), jnp.float32),
        "target_heat_sensitivity": gaussian(seeds[2], (GRID_LENGTH_X, GRID_LENGTH_Y, GRID_LENGTH_Z), 1.0, 6.0, ((0, 16), (1, 16)), jnp.float32),
        "coolant_coupling": jnp.clip(jnp.exp(math.log(2.0) - 2.0794415 * jax.random.uniform(seeds[3], (GRID_LENGTH_X, GRID_LENGTH_Y, GRID_LENGTH_Z), jnp.float32) ** steps_of(seeds[3], (GRID_LENGTH_X, GRID_LENGTH_Y, GRID_LENGTH_Z), ((0, 16), (1, 16)), -0.2, 0.2)), 0.25, 2.0),
        "design_switch": draw_design_switch(jax.random.fold_in(seeds[5], 71), 0),
    }


COND_FLOOR = 0.001
DAMPING_WEIGHT = 2.0 / 3.0
REPORT_SCALE = 100.0


def cone_weight(distance):
    return jnp.maximum(RADIUS + 1 - jnp.abs(distance), 0).astype(jnp.float32)


def coverage(positions, length):
    offsets = jnp.arange(-RADIUS, RADIUS + 1, dtype=jnp.int32)
    reached = positions[:, None] + offsets[None, :]
    inside = (reached >= 0) & (reached < length)
    return jnp.sum(jnp.where(inside, cone_weight(offsets)[None, :], jnp.float32(0.0)), axis=1)


def nearby_voxels(padded):
    return [padded[2:, 1:-1, 1:-1], padded[:-2, 1:-1, 1:-1],
            padded[1:-1, 2:, 1:-1], padded[1:-1, :-2, 1:-1],
            padded[1:-1, 1:-1, 2:], padded[1:-1, 1:-1, :-2]]


def apply_mask(values, design_switch):
    depth = values.shape[0] // design_switch.shape[0]
    span = values.shape[1] // design_switch.shape[1]
    shaped = values.reshape(design_switch.shape[0], depth, design_switch.shape[1], span, design_switch.shape[2], BX)
    gating = design_switch.astype(jnp.float32)[:, None, :, None, :, None]
    return (shaped * gating).reshape(values.shape)


def filter_x(values):
    extent = values.shape[2]
    count_blocks = extent // BX
    scaled = values / coverage(jnp.arange(extent, dtype=jnp.int32), extent)[None, None, :]
    blocks = scaled.reshape(-1, count_blocks, BX)
    padded = jnp.pad(blocks, ((0, 0), (1, 1), (0, 0)))
    positions = jnp.arange(BX, dtype=jnp.int32)
    result_sum = jnp.zeros(blocks.shape, jnp.float32)
    for block_step in (-1, 0, 1):
        weights_table = cone_weight(block_step * BX + positions[:, None] - positions[None, :])
        result_sum = result_sum + jnp.einsum("rbi,ij->rbj", padded[:, 1 + block_step:1 + block_step + count_blocks], weights_table, precision=lax.Precision.HIGHEST)
    return result_sum.reshape(values.shape)


def filter_y(values):
    extent = values.shape[1]
    positions = jnp.arange(extent, dtype=jnp.int32)
    scaled = values / coverage(positions, extent)[None, :, None]
    weights_table = cone_weight(positions[:, None] - positions[None, :])
    return jnp.einsum("zyx,yw->zwx", scaled, weights_table, precision=lax.Precision.HIGHEST)


def filter_z(values):
    extent = values.shape[0]
    positions = jnp.arange(extent, dtype=jnp.int32)
    scaled = values / coverage(positions, extent)[:, None, None]
    weights_table = cone_weight(positions[:, None] - positions[None, :])
    return jnp.einsum("zyx,zw->wyx", scaled, weights_table, precision=lax.Precision.HIGHEST)


def reference(solid_fraction, thermal_state, target_heat_sensitivity, coolant_coupling, design_switch):
    interface_flux_factor = COND_FLOOR + (1.0 - COND_FLOOR) * solid_fraction ** 3
    face_conduct = [0.5 * (interface_flux_factor + beside) for beside in nearby_voxels(jnp.pad(interface_flux_factor, 1))]
    matrix_main_entry = coolant_coupling + sum(face_conduct)
    lagrange_multiplier = target_heat_sensitivity / matrix_main_entry
    for iteration in range(SWEEPS):
        incoming_flux = sum(weight_face * beside for weight_face, beside in zip(face_conduct, nearby_voxels(jnp.pad(lagrange_multiplier, 1))))
        lagrange_multiplier = lagrange_multiplier + DAMPING_WEIGHT * (target_heat_sensitivity - matrix_main_entry * lagrange_multiplier + incoming_flux) / matrix_main_entry
    couple_multiplied = sum((lagrange_multiplier - nearby_multiplier) * (thermal_state - nearby_heat_level)
                   for nearby_multiplier, nearby_heat_level in zip(nearby_voxels(jnp.pad(lagrange_multiplier, 1)), nearby_voxels(jnp.pad(thermal_state, 1))))
    stiff_slope = 3.0 * (1.0 - COND_FLOOR) * solid_fraction ** 2
    raw = apply_mask(-0.5 * couple_multiplied * stiff_slope, design_switch)
    along_z = filter_z(filter_y(filter_x(raw)))
    return apply_mask(REPORT_SCALE * along_z, design_switch)
```

```python
import jax
import jax.numpy as jnp
from jax import lax
from jax.experimental import pallas as pl
from jax.experimental.pallas import tpu as pltpu
from jax.sharding import PartitionSpec as P

RADIUS = 48
COND_FLOOR = 0.001
REPORT_SCALE = 100.0
D, S, X = 24, 8, 2048
NK = X // 128
E = D + 6
F32 = jnp.float32
BF16 = jnp.bfloat16
MIB = 1024 * 1024


def rows_of(shape):
    return lax.broadcasted_iota(jnp.int32, shape, 0)


def rot(tile, shift):
    shift = shift % 8
    return tile if shift == 0 else pltpu.roll(tile, shift, 0)


def conduct_of(solid):
    return COND_FLOOR + (1.0 - COND_FLOOR) * (solid * solid * solid)


def pack_first(s_ref, t_ref, b_ref, k_ref, ylo, yhi, zlo, zhi, dll, dlh, dhl, dhh):
    r = rows_of((8, X))

    def plane(z, carry):
        c = conduct_of(s_ref[z])
        b, k, t = b_ref[z], k_ref[z], t_ref[z]
        ylo[z] = jnp.where(r < 3, c, jnp.where(r < 5, rot(b, 3), jnp.where(r < 7, rot(k, 5), rot(t, 7))))
        yhi[z] = jnp.where(r > 4, c, jnp.where(r > 2, rot(b, -3), jnp.where(r > 0, rot(k, -5), rot(t, -7))))
        return carry

    lax.fori_loop(0, D, plane, 0)
    for dst, lo, hi, at in ((zlo, dll, dlh, lambda j: j), (zhi, dhl, dhh, lambda j: D - 1 - j)):
        for j in range(3):
            dst[j] = conduct_of(s_ref[at(j)])
        for j in range(2):
            dst[3 + j] = b_ref[at(j)]
            dst[5 + j] = k_ref[at(j)]
        dst[7] = t_ref[at(0)]
        c1, c2, b1, k1 = conduct_of(s_ref[at(0)]), conduct_of(s_ref[at(1)]), b_ref[at(0)], k_ref[at(0)]
        lo[...] = jnp.where(r < 2, c1, jnp.where(r == 2, rot(c2, 2), jnp.where(r == 3, rot(b1, 3), rot(k1, 4))))
        hi[...] = jnp.where(r > 5, c1, jnp.where(r == 5, rot(c2, -2), jnp.where(r == 4, rot(b1, -3), rot(k1, -4))))


def assemble(s_ref, b_ref, k_ref, yhi, ylo, zlo, zhi, dll, dlh, dhl, dhh, C, B, K):
    r = rows_of((8, X))
    zero = jnp.zeros((8, X), F32)

    def plane(z, carry):
        p = z + 3
        C[p, 0:8] = conduct_of(s_ref[z])
        B[p, 0:8] = b_ref[z]
        K[p, 0:8] = k_ref[z]
        h, l = yhi[z], ylo[z]
        C[p, 8:16] = jnp.where(r < 3, h, jnp.where(r > 4, l, 0.0))
        B[p, 8:16] = jnp.where(r < 2, rot(h, -3), jnp.where(r > 5, rot(l, 3), 0.0))
        K[p, 8:16] = jnp.where(r < 2, rot(h, -5), jnp.where(r > 5, rot(l, 5), 0.0))
        return carry

    lax.fori_loop(0, D, plane, 0)
    for src, h_ref, l_ref, at in ((zlo, dlh, dll, lambda j: 2 - j), (zhi, dhh, dhl, lambda j: 27 + j)):
        h, l = h_ref[...], l_ref[...]
        for j in range(3):
            C[at(j), 0:8] = src[j]
        for j in range(2):
            B[at(j), 0:8] = src[3 + j]
            K[at(j), 0:8] = src[5 + j]
        C[at(0), 8:16] = jnp.where(r < 2, h, jnp.where(r > 5, l, 0.0))
        C[at(1), 8:16] = jnp.where(r == 0, rot(h, -2), jnp.where(r == 7, rot(l, 2), 0.0))
        C[at(2), 8:16] = zero
        B[at(0), 8:16] = jnp.where(r == 0, rot(h, -3), jnp.where(r == 7, rot(l, 3), 0.0))
        K[at(0), 8:16] = jnp.where(r == 0, rot(h, -4), jnp.where(r == 7, rot(l, 4), 0.0))
        B[at(1), 8:16] = zero
        K[at(1), 8:16] = zero


def tile_at(k):
    return slice(128 * k, 128 * k + 128)


def left_shift(load, k, lane, rots):
    for m in (k, (k + 1) % NK):
        if m not in rots:
            rots[m] = pltpu.roll(load(m), 127, 1)
    return jnp.where(lane == 127, rots[(k + 1) % NK], rots[k])


def build(C, B, K, A, A0, RD, FX, FY, FZ):
    lane = lax.broadcasted_iota(jnp.int32, (16, 128), 1)

    def plane(p, carry):
        rots, prev = {}, None
        last = None
        for k in range(NK):
            sl = tile_at(k)
            c = C[p, :, sl]
            nxt = left_shift(lambda m: C[p, :, tile_at(m)], k, lane, rots)
            if k == NK - 1:
                nxt = jnp.where(lane == 127, 0.0, nxt)
            fx = c + nxt
            if k == NK - 1:
                fx = jnp.where(lane == 127, 0.0, fx)
            back = pltpu.roll(c, 1, 1)
            before = jnp.where(lane == 0, 0.0 if last is None else last, back)
            last = back
            up = pltpu.roll(c, 15, 0)
            down = pltpu.roll(c, 1, 0)
            cz = C[p + 1, :, sl]
            FX[p, :, sl] = fx
            FY[p, :, sl] = c + up
            FZ[p, :, sl] = c + cz
            coup = K[p, :, sl]
            diag = coup + (3.0 * c + 0.5 * (nxt + before + up + down + cz + C[p - 1, :, sl]))
            rd = jnp.where(coup > 0.0, 1.0 / jnp.where(coup > 0.0, diag, 1.0), 0.0)
            a = B[p, :, sl] * rd
            if A is not None:
                A[p, :, sl] = a
            A0[p, :, sl] = (2.0 / 3.0) * a
            RD[p, :, sl] = (1.0 / 3.0) * rd
        return carry

    lax.fori_loop(1, E - 1, plane, 0)

    def edge(i, carry):
        FZ[0, :, pl.ds(pl.multiple_of(i * 128, 128), 128)] = (
            C[0, :, pl.ds(pl.multiple_of(i * 128, 128), 128)] + C[1, :, pl.ds(pl.multiple_of(i * 128, 128), 128)]
        )
        return carry

    lax.fori_loop(0, NK, edge, 0)


def sweep(A, OUT, A0, RD, FX, FY, FZ, low, high):
    lane = lax.broadcasted_iota(jnp.int32, (16, 128), 1)

    def plane(p, carry):
        rots = {}
        last = pltpu.roll(FX[p, :, tile_at(NK - 1)] * A[p, :, tile_at(NK - 1)], 1, 1)
        for k in range(NK):
            sl = tile_at(k)
            a = A[p, :, sl]
            fx, fy = FX[p, :, sl], FY[p, :, sl]
            nxt = left_shift(lambda m: A[p, :, tile_at(m)], k, lane, rots)
            back = pltpu.roll(fx * a, 1, 1)
            flux = fx * nxt + jnp.where(lane == 0, last, back)
            last = back
            flux = flux + (fy * pltpu.roll(a, 15, 0) + pltpu.roll(fy * a, 1, 0))
            flux = flux + (FZ[p, :, sl] * A[p + 1, :, sl] + FZ[p - 1, :, sl] * A[p - 1, :, sl])
            OUT[p, :, sl] = (1.0 / 3.0) * a + (A0[p, :, sl] + RD[p, :, sl] * flux)
        return carry

    lax.fori_loop(low, high, plane, 0)


def pieces(first, rows):
    out, done = [], 0
    while done < rows:
        n = first + done
        take = min(rows - done, 8 - n % 8)
        out.append((n // 8, n % 8, done, take))
        done += take
    return out


def sweeps_first(s_ref, b_ref, k_ref, yhi, ylo, zlo, zhi, dll, dlh, dhl, dhh,
                 a_out, y2lo, y2hi, z2lo, z2hi, e_ll, e_lh, e_hl, e_hh,
                 C, B, K, A, A0, RD, FX, FY, FZ):
    assemble(s_ref, b_ref, k_ref, yhi, ylo, zlo, zhi, dll, dlh, dhl, dhh, C, B, K)
    build(C, B, K, A, A0, RD, FX, FY, FZ)
    sweep(A, B, A0, RD, FX, FY, FZ, 2, E - 2)
    sweep(B, A, A0, RD, FX, FY, FZ, 3, E - 3)
    r = rows_of((8, X))

    def copy(z, carry):
        a_out[z] = A[z + 3, 0:8]
        return carry

    lax.fori_loop(0, D, copy, 0)

    def group(g, carry):
        low, high = [None] * 3, [None] * 3
        for j in range(8):
            a = A[8 * g + j + 3, 0:8]
            for tile, at, row, take in pieces(3 * j, 3):
                mask = (r >= at) & (r < at + take)
                for msg, src in ((low, row), (high, 5 + row)):
                    moved = rot(a, at - src)
                    msg[tile] = moved if msg[tile] is None else jnp.where(mask, moved, msg[tile])
        for i in range(3):
            y2lo[3 * g + i] = low[i]
            y2hi[3 * g + i] = high[i]
        return carry

    lax.fori_loop(0, 3, group, 0)
    for dst, lo, hi, at in ((z2lo, e_ll, e_lh, lambda j: 3 + j), (z2hi, e_hl, e_hh, lambda j: 26 - j)):
        for j in range(3):
            dst[j] = A[at(j), 0:8]
        a1, a2 = A[at(0), 0:8], A[at(1), 0:8]
        lo[...] = jnp.where(r < 2, a1, rot(a2, 2))
        hi[...] = jnp.where(r > 5, a1, rot(a2, -2))


def tri(u):
    m = jnp.maximum(RADIUS - u, 0)
    return m * (m + 1) // 2


def inv_cover(position, length):
    total = (RADIUS + 1) ** 2 - tri(position) - tri(length - 1 - position)
    return 1.0 / total.astype(F32)


def sweeps_second(info, s_ref, t_ref, b_ref, k_ref, yhi, ylo, zlo, zhi, dll, dlh, dhl, dhh,
                  a_in, y2hi, y2lo, z2lo, z2hi, e_ll, e_lh, e_hl, e_hh,
                  send, C, B, K, A, A0, RD, FX, FY, FZ, R):
    assemble(s_ref, b_ref, k_ref, yhi, ylo, zlo, zhi, dll, dlh, dhl, dhh, C, B, K)
    build(C, B, K, None, A0, RD, FX, FY, FZ)
    r = rows_of((8, X))
    zero = jnp.zeros((8, X), F32)

    def group(g, carry):
        for j in range(8):
            z = 8 * g + j
            A[z + 3, 0:8] = a_in[z]
            side = zero
            for tile, at, row, take in pieces(3 * j, 3):
                side = jnp.where((r >= row) & (r < row + take), rot(y2hi[3 * g + tile], row - at), side)
                side = jnp.where((r >= 5 + row) & (r < 5 + row + take), rot(y2lo[3 * g + tile], 5 + row - at), side)
            A[z + 3, 8:16] = side
        return carry

    lax.fori_loop(0, 3, group, 0)
    for src, h_ref, l_ref, at in ((z2lo, e_lh, e_ll, lambda j: 2 - j), (z2hi, e_hh, e_hl, lambda j: 27 + j)):
        h, l = h_ref[...], l_ref[...]
        for j in range(3):
            A[at(j), 0:8] = src[j]
        A[at(0), 8:16] = jnp.where(r < 2, h, jnp.where(r > 5, l, 0.0))
        A[at(1), 8:16] = jnp.where(r == 0, rot(h, -2), jnp.where(r == 7, rot(l, 2), 0.0))
        A[at(2), 8:16] = zero
    sweep(A, B, A0, RD, FX, FY, FZ, 1, E - 1)
    sweep(B, A, A0, RD, FX, FY, FZ, 2, E - 2)

    T = C

    def plane_t(z, carry):
        T[z + 3, 0:8] = t_ref[z]
        T[z + 3, 8:16] = jnp.where(r == 0, rot(yhi[z], -7), rot(ylo[z], 7))
        return carry

    lax.fori_loop(0, D, plane_t, 0)
    T[2, 0:8] = zlo[7]
    T[27, 0:8] = zhi[7]

    lane = lax.broadcasted_iota(jnp.int32, (16, 128), 1)
    lane8 = lax.broadcasted_iota(jnp.int32, (8, 128), 1)
    row8 = lax.broadcasted_iota(jnp.int32, (8, 128), 0)
    cover_y = inv_cover(info[1] * S + row8, 16 * S)
    factor = -0.5 * 3.0 * (1.0 - COND_FLOOR)

    def plane_raw(z, carry):
        p = z + 3
        base = cover_y * inv_cover(info[0] * D + z + jnp.zeros((8, 128), jnp.int32), 16 * D) * factor
        ra, rt = {}, {}
        last = None
        for k in range(NK):
            sl = tile_at(k)
            a16, t16 = A[p, :, sl], T[p, :, sl]
            a, t = a16[0:8], t16[0:8]
            an = left_shift(lambda m: A[p, 0:8, tile_at(m)], k, lane8, ra)
            tn = left_shift(lambda m: T[p, 0:8, tile_at(m)], k, lane8, rt)
            if k == NK - 1:
                an = jnp.where(lane8 == 127, 0.0, an)
                tn = jnp.where(lane8 == 127, 0.0, tn)
            px = (a - an) * (t - tn)
            back = pltpu.roll(px, 1, 1)
            pair = px + jnp.where(lane8 == 0, a * t if last is None else last, back)
            last = back
            au, tu = pltpu.roll(a16, 15, 0)[0:8], pltpu.roll(t16, 15, 0)[0:8]
            ad, td = pltpu.roll(a16, 1, 0)[0:8], pltpu.roll(t16, 1, 0)[0:8]
            pair = pair + ((a - au) * (t - tu) + (a - ad) * (t - td))
            pair = pair + (a - A[p + 1, 0:8, sl]) * (t - T[p + 1, 0:8, sl])
            pair = pair + (a - A[p - 1, 0:8, sl]) * (t - T[p - 1, 0:8, sl])
            s = s_ref[z, :, sl]
            switch = info[2 + k // 2].astype(F32)
            scale = base * switch
            if k in (0, NK - 1):
                scale = scale * inv_cover(lane8 + 128 * k, X)
            else:
                scale = scale * (1.0 / float((RADIUS + 1) ** 2))
            R[pl.ds(pl.multiple_of(z * 8, 8), 8), sl] = pair * (s * s) * scale
        return carry

    lax.fori_loop(0, D, plane_raw, 0)

    i = lax.broadcasted_iota(jnp.int32, (512, 256), 0) - 128
    j = lax.broadcasted_iota(jnp.int32, (512, 256), 1)
    weights = jnp.maximum(RADIUS + 1 - jnp.abs(i - j), 0).astype(F32).astype(BF16)
    for n in range(X // 256):
        low, high = max(256 * n - 128, 0), min(256 * n + 384, X)
        x = R[:, low:high]
        w = weights[low - (256 * n - 128) : high - (256 * n - 128)]
        xh = x.astype(BF16)
        xl = (x - xh.astype(F32)).astype(BF16)
        y = jnp.dot(xh, w, preferred_element_type=F32) + jnp.dot(xl, w, preferred_element_type=F32)
        send[2 * n] = y[:, 0:128]
        send[2 * n + 1] = y[:, 128:256]


def filter_y(x_ref, out, s0, s1):
    i = lax.broadcasted_iota(jnp.int32, (128, 128), 0)
    j = lax.broadcasted_iota(jnp.int32, (128, 128), 1)
    w = jnp.maximum(RADIUS + 1 - jnp.abs(i - j), 0).astype(F32).astype(BF16)
    acc0 = jnp.zeros((128, 128), F32)
    acc1 = jnp.zeros((128, 128), F32)
    s0[...] = jnp.zeros((128, 128), F32)
    s1[...] = jnp.zeros((128, 128), F32)
    for z in range(D):
        x = x_ref[:, 8 * z : 8 * z + 8, :].reshape(128, 128)
        xh = x.astype(BF16)
        xl = (x - xh.astype(F32)).astype(BF16)
        y = jnp.dot(w, xh, preferred_element_type=F32) + jnp.dot(w, xl, preferred_element_type=F32)
        out[:, 8 * z : 8 * z + 8, :] = y.reshape(16, 8, 128)
        s0[...] += y
        if z:
            s1[...] += float(z) * y


def filter_z(own, up0, up1, down0, down1, up2, down2, out):
    def chunk(m, carry):
        def load(ref, z):
            return ref[m, 8 * z : 8 * z + 8, :]

        sl = pl.ds(pl.multiple_of(m * 8, 8), 8)
        u0, u1, d0, d1 = up0[sl, :], up1[sl, :], down0[sl, :], down1[sl, :]
        suffix = load(down2, D - 1)
        total = suffix
        far = [None] * D
        far[D - 1] = total
        for z in range(D - 2, -1, -1):
            suffix = suffix + load(down2, z)
            total = total + suffix
            far[z] = total
        sum_own = load(own, 0)
        first = jnp.zeros_like(sum_own)
        for z in range(1, D):
            x = load(own, z)
            sum_own = sum_own + x
            first = first + float(z) * x
        distance = first
        near = (25.0 * (u0 + d0) + (d1 - u1)) + float(RADIUS + 1) * sum_own
        slope = u0 - d0
        prefix_own = jnp.zeros_like(sum_own)
        prefix_up = jnp.zeros_like(sum_own)
        total_up = jnp.zeros_like(sum_own)
        for z in range(D):
            prefix_up = prefix_up + load(up2, z)
            total_up = total_up + prefix_up
            out[m, 8 * z : 8 * z + 8, :] = (near - distance) + (total_up + far[z])
            prefix_own = prefix_own + load(own, z)
            distance = distance + (2.0 * prefix_own - sum_own)
            near = near + slope
        return carry

    lax.fori_loop(0, 16, chunk, 0)


def finish(info, x_ref, out):
    for k in range(NK):
        scale = REPORT_SCALE * info[2 + k // 2].astype(F32)
        for z in range(D):
            out[z, :, tile_at(k)] = x_ref[k, 8 * z : 8 * z + 8, :] * scale


def kernel_call(body, ins, outs, scratch=(), scalars=0, limit=60):
    vmem = pl.BlockSpec(memory_space=pltpu.VMEM)
    smem = pl.BlockSpec(memory_space=pltpu.SMEM)
    return pl.pallas_call(
        body,
        out_shape=[jax.ShapeDtypeStruct(s, F32) for s in outs],
        in_specs=[smem] * scalars + [vmem] * (len(ins) - scalars),
        out_specs=[vmem] * len(outs),
        scratch_shapes=[pltpu.VMEM(s, F32) for s in scratch],
        compiler_params=pltpu.CompilerParams(vmem_limit_bytes=limit * MIB),
    )(*ins)


def moved(x, dz, dy):
    pairs = []
    for g in range(16):
        for b in range(16):
            if 0 <= g + dz < 16 and 0 <= b + dy < 16:
                pairs.append(((g + dz) * 16 + b + dy, g * 16 + b))
    return lax.ppermute(x, ("grp", "blk"), pairs)


def local(solid, thermal, target, coolant, switch):
    info = jnp.concatenate(
        [jnp.stack([lax.axis_index("grp"), lax.axis_index("blk")]).astype(jnp.int32), switch.reshape(8)]
    )
    block, tile = (D, 8, X), (8, X)
    ylo, yhi, zlo, zhi, dll, dlh, dhl, dhh = kernel_call(
        pack_first, (solid, thermal, target, coolant), [block, block, tile_shape(8), tile_shape(8)] + [tile] * 4
    )
    first = (
        moved(ylo, 0, 1), moved(yhi, 0, -1), moved(zhi, -1, 0), moved(zlo, 1, 0),
        moved(dhh, -1, -1), moved(dhl, -1, 1), moved(dlh, 1, -1), moved(dll, 1, 1),
    )
    ext = [(E, 16, X)] * 9
    a, ylo, yhi, zlo, zhi, dll, dlh, dhl, dhh = kernel_call(
        sweeps_first, (solid, target, coolant) + first,
        [block, tile_shape(9), tile_shape(9), tile_shape(3), tile_shape(3)] + [tile] * 4, ext,
    )
    second = (
        moved(ylo, 0, 1), moved(yhi, 0, -1), moved(zhi, -1, 0), moved(zlo, 1, 0),
        moved(dhh, -1, -1), moved(dhl, -1, 1), moved(dlh, 1, -1), moved(dll, 1, 1),
    )
    parts = (16, D * 8, 128)
    (send,) = kernel_call(
        sweeps_second, (info, solid, thermal, target, coolant) + first + (a,) + second,
        [parts], ext + [(D * 8, X)], scalars=1,
    )
    columns = lax.all_to_all(send, "blk", split_axis=0, concat_axis=0, tiled=True)
    along_y, s0, s1 = kernel_call(filter_y, (columns,), [parts, (128, 128), (128, 128)], limit=30)
    sums = jnp.stack([s0, s1])
    up2, down2 = moved(along_y, 2, 0), moved(along_y, -2, 0)
    up, down = moved(sums, 1, 0), moved(sums, -1, 0)
    (along_z,) = kernel_call(
        filter_z, (along_y, up[0], up[1], down[0], down[1], up2, down2), [parts], limit=30
    )
    back = lax.all_to_all(along_z, "blk", split_axis=0, concat_axis=0, tiled=True)
    (out,) = kernel_call(finish, (info, back), [block], scalars=1, limit=30)
    return out


def tile_shape(n):
    return (n, 8, X)


def solution(mesh):
    spec = P("grp", "blk", None)
    return jax.shard_map(
        local, mesh=mesh, in_specs=(spec,) * 5, out_specs=spec, check_vma=False
    )
```

```python
import jax
import jax.numpy as jnp
from jax import lax
from jax.experimental import pallas as pl
from jax.experimental.pallas import tpu as pltpu
from jax.sharding import PartitionSpec as P

RADIUS = 48
COND_FLOOR = 0.001
REPORT_SCALE = 100.0
D, S, X = 24, 8, 2048
NK = X // 128
E = D + 6
STEP = 4
F32 = jnp.float32
BF16 = jnp.bfloat16
MIB = 1024 * 1024


def rows_of(shape):
    return lax.broadcasted_iota(jnp.int32, shape, 0)


def rot(tile, shift):
    shift = shift % 8
    return tile if shift == 0 else pltpu.roll(tile, shift, 0)


def conduct_of(solid):
    return COND_FLOOR + (1.0 - COND_FLOOR) * (solid * solid * solid)


def pack_first(s_ref, t_ref, b_ref, k_ref, ylo, yhi, zlo, zhi):
    r = rows_of((8, X))
    for z in range(STEP):
        c = conduct_of(s_ref[z])
        b, k, t = b_ref[z], k_ref[z], t_ref[z]
        ylo[z] = jnp.where(r < 3, c, jnp.where(r < 5, rot(b, 3), jnp.where(r < 7, rot(k, 5), rot(t, 7))))
        yhi[z] = jnp.where(r > 4, c, jnp.where(r > 2, rot(b, -3), jnp.where(r > 0, rot(k, -5), rot(t, -7))))

    def edge(dst, at):
        for j in range(3):
            dst[j] = conduct_of(s_ref[at(j)])
        for j in range(2):
            dst[3 + j] = b_ref[at(j)]
            dst[5 + j] = k_ref[at(j)]
        dst[7] = t_ref[at(0)]

    @pl.when(pl.program_id(0) == 0)
    def _():
        edge(zlo, lambda j: j)

    @pl.when(pl.program_id(0) == D // STEP - 1)
    def _():
        edge(zhi, lambda j: STEP - 1 - j)


def pack_corners(zlo, zhi, lo, hi):
    r = rows_of((8, X))
    for i, src in enumerate((zlo, zhi)):
        c1, c2, b1, k1 = src[0], src[1], src[3], src[5]
        lo[i] = jnp.where(r < 2, c1, jnp.where(r == 2, rot(c2, 2), jnp.where(r == 3, rot(b1, 3), rot(k1, 4))))
        hi[i] = jnp.where(r > 5, c1, jnp.where(r == 5, rot(c2, -2), jnp.where(r == 4, rot(b1, -3), rot(k1, -4))))


def pack_corners_second(zlo, zhi, lo, hi):
    r = rows_of((8, X))
    for i, src in enumerate((zlo, zhi)):
        lo[i] = jnp.where(r < 2, src[0], rot(src[1], 2))
        hi[i] = jnp.where(r > 5, src[0], rot(src[1], -2))


def assemble(s_ref, b_ref, k_ref, yhi, ylo, zlo, zhi, chi, clo, C, B, K):
    r = rows_of((8, X))
    zero = jnp.zeros((8, X), F32)

    def plane(z, carry):
        p = z + 3
        C[p, 0:8] = conduct_of(s_ref[z])
        B[p, 0:8] = b_ref[z]
        K[p, 0:8] = k_ref[z]
        h, l = yhi[z], ylo[z]
        C[p, 8:16] = jnp.where(r < 3, h, jnp.where(r > 4, l, 0.0))
        B[p, 8:16] = jnp.where(r < 2, rot(h, -3), jnp.where(r > 5, rot(l, 3), 0.0))
        K[p, 8:16] = jnp.where(r < 2, rot(h, -5), jnp.where(r > 5, rot(l, 5), 0.0))
        return carry

    lax.fori_loop(0, D, plane, 0)
    for i, src, at in ((0, zlo, lambda j: 2 - j), (1, zhi, lambda j: 27 + j)):
        h, l = chi[i], clo[i]
        for j in range(3):
            C[at(j), 0:8] = src[j]
        for j in range(2):
            B[at(j), 0:8] = src[3 + j]
            K[at(j), 0:8] = src[5 + j]
        C[at(0), 8:16] = jnp.where(r < 2, h, jnp.where(r > 5, l, 0.0))
        C[at(1), 8:16] = jnp.where(r == 0, rot(h, -2), jnp.where(r == 7, rot(l, 2), 0.0))
        C[at(2), 8:16] = zero
        B[at(0), 8:16] = jnp.where(r == 0, rot(h, -3), jnp.where(r == 7, rot(l, 3), 0.0))
        K[at(0), 8:16] = jnp.where(r == 0, rot(h, -4), jnp.where(r == 7, rot(l, 4), 0.0))
        B[at(1), 8:16] = zero
        K[at(1), 8:16] = zero


def tile_at(k):
    return slice(128 * k, 128 * k + 128)


def left_shift(load, k, lane, rots):
    for m in (k, (k + 1) % NK):
        if m not in rots:
            rots[m] = pltpu.roll(load(m), 127, 1)
    return jnp.where(lane == 127, rots[(k + 1) % NK], rots[k])


def build(C, A, A0, RD, FX, FY, FZ):
    lane = lax.broadcasted_iota(jnp.int32, (16, 128), 1)

    def plane(p, carry):
        rots, prev = {}, None
        last = None
        for k in range(NK):
            sl = tile_at(k)
            c = C[p, :, sl]
            nxt = left_shift(lambda m: C[p, :, tile_at(m)], k, lane, rots)
            if k == NK - 1:
                nxt = jnp.where(lane == 127, 0.0, nxt)
            fx = c + nxt
            if k == NK - 1:
                fx = jnp.where(lane == 127, 0.0, fx)
            back = pltpu.roll(c, 1, 1)
            before = jnp.where(lane == 0, 0.0 if last is None else last, back)
            last = back
            up = pltpu.roll(c, 15, 0)
            down = pltpu.roll(c, 1, 0)
            cz = C[p + 1, :, sl]
            FX[p, :, sl] = fx
            FY[p, :, sl] = c + up
            FZ[p, :, sl] = c + cz
            coup = RD[p, :, sl]
            diag = coup + (3.0 * c + 0.5 * (nxt + before + up + down + cz + C[p - 1, :, sl]))
            rd = jnp.where(coup > 0.0, 1.0 / jnp.where(coup > 0.0, diag, 1.0), 0.0)
            a = A[p, :, sl] * rd
            A[p, :, sl] = a
            A0[p, :, sl] = (2.0 / 3.0) * a
            RD[p, :, sl] = (1.0 / 3.0) * rd
        return carry

    lax.fori_loop(1, E - 1, plane, 0)

    def edge(i, carry):
        FZ[0, :, pl.ds(pl.multiple_of(i * 128, 128), 128)] = (
            C[0, :, pl.ds(pl.multiple_of(i * 128, 128), 128)] + C[1, :, pl.ds(pl.multiple_of(i * 128, 128), 128)]
        )
        return carry

    lax.fori_loop(0, NK, edge, 0)


def sweep(A, OUT, A0, RD, FX, FY, FZ, low, high):
    lane = lax.broadcasted_iota(jnp.int32, (16, 128), 1)

    def plane(p, carry):
        rots = {}
        last = pltpu.roll(FX[p, :, tile_at(NK - 1)] * A[p, :, tile_at(NK - 1)], 1, 1)
        for k in range(NK):
            sl = tile_at(k)
            a = A[p, :, sl]
            fx, fy = FX[p, :, sl], FY[p, :, sl]
            nxt = left_shift(lambda m: A[p, :, tile_at(m)], k, lane, rots)
            back = pltpu.roll(fx * a, 1, 1)
            flux = fx * nxt + jnp.where(lane == 0, last, back)
            last = back
            flux = flux + (fy * pltpu.roll(a, 15, 0) + pltpu.roll(fy * a, 1, 0))
            flux = flux + (FZ[p, :, sl] * A[p + 1, :, sl] + FZ[p - 1, :, sl] * A[p - 1, :, sl])
            OUT[p, :, sl] = (1.0 / 3.0) * a + (A0[p, :, sl] + RD[p, :, sl] * flux)
        return carry

    lax.fori_loop(low, high, plane, 0)


def pieces(first, rows):
    out, done = [], 0
    while done < rows:
        n = first + done
        take = min(rows - done, 8 - n % 8)
        out.append((n // 8, n % 8, done, take))
        done += take
    return out


def sweeps_first(s_ref, b_ref, k_ref, yhi, ylo, zlo, zhi, chi, clo,
                 a_out, y2lo, y2hi, z2lo, z2hi, A0, RD, FX, FY, FZ, C, A):
    assemble(s_ref, b_ref, k_ref, yhi, ylo, zlo, zhi, chi, clo, C, A, RD)
    build(C, A, A0, RD, FX, FY, FZ)
    sweep(A, C, A0, RD, FX, FY, FZ, 2, E - 2)
    sweep(C, A, A0, RD, FX, FY, FZ, 3, E - 3)
    r = rows_of((8, X))

    def copy(z, carry):
        a_out[z] = A[z + 3, 0:8]
        return carry

    lax.fori_loop(0, D, copy, 0)

    def group(g, carry):
        low, high = [None] * 3, [None] * 3
        for j in range(8):
            a = A[8 * g + j + 3, 0:8]
            for tile, at, row, take in pieces(3 * j, 3):
                mask = (r >= at) & (r < at + take)
                for msg, src in ((low, row), (high, 5 + row)):
                    moved = rot(a, at - src)
                    msg[tile] = moved if msg[tile] is None else jnp.where(mask, moved, msg[tile])
        for i in range(3):
            y2lo[3 * g + i] = low[i]
            y2hi[3 * g + i] = high[i]
        return carry

    lax.fori_loop(0, 3, group, 0)
    for j in range(3):
        z2lo[j] = A[3 + j, 0:8]
        z2hi[j] = A[26 - j, 0:8]


def tri(u):
    m = jnp.maximum(RADIUS - u, 0)
    return m * (m + 1) // 2


def inv_cover(position, length):
    total = (RADIUS + 1) ** 2 - tri(position) - tri(length - 1 - position)
    return 1.0 / total.astype(F32)


def sweeps_second(info, s_ref, t_ref, yhi, ylo, zlo, zhi, a_in, A0, RD, FX, FY, FZ,
                  y2hi, y2lo, z2lo, z2hi, e_hi, e_lo, send, A, B, T, R):
    r = rows_of((8, X))
    zero = jnp.zeros((8, X), F32)

    def group(g, carry):
        for j in range(8):
            z = 8 * g + j
            A[z + 3, 0:8] = a_in[z]
            side = zero
            for tile, at, row, take in pieces(3 * j, 3):
                side = jnp.where((r >= row) & (r < row + take), rot(y2hi[3 * g + tile], row - at), side)
                side = jnp.where((r >= 5 + row) & (r < 5 + row + take), rot(y2lo[3 * g + tile], 5 + row - at), side)
            A[z + 3, 8:16] = side
        return carry

    lax.fori_loop(0, 3, group, 0)
    for i, src, at in ((0, z2lo, lambda j: 2 - j), (1, z2hi, lambda j: 27 + j)):
        h, l = e_hi[i], e_lo[i]
        for j in range(3):
            A[at(j), 0:8] = src[j]
        A[at(0), 8:16] = jnp.where(r < 2, h, jnp.where(r > 5, l, 0.0))
        A[at(1), 8:16] = jnp.where(r == 0, rot(h, -2), jnp.where(r == 7, rot(l, 2), 0.0))
        A[at(2), 8:16] = zero
    sweep(A, B, A0, RD, FX, FY, FZ, 1, E - 1)
    sweep(B, A, A0, RD, FX, FY, FZ, 2, E - 2)

    def plane_t(z, carry):
        T[z + 1] = t_ref[z]
        return carry

    lax.fori_loop(0, D, plane_t, 0)
    T[0] = zlo[7]
    T[D + 1] = zhi[7]

    lane8 = lax.broadcasted_iota(jnp.int32, (8, 128), 1)
    row8 = lax.broadcasted_iota(jnp.int32, (8, 128), 0)
    cover_y = inv_cover(info[1] * S + row8, 16 * S)
    factor = -0.5 * 3.0 * (1.0 - COND_FLOOR)

    def plane_raw(z, carry):
        p = z + 3
        base = cover_y * inv_cover(info[0] * D + z + jnp.zeros((8, 128), jnp.int32), 16 * D) * factor
        ra, rt = {}, {}
        last = None
        for k in range(NK):
            sl = tile_at(k)
            a16 = A[p, :, sl]
            a, t = a16[0:8], T[z + 1, :, sl]
            an = left_shift(lambda m: A[p, 0:8, tile_at(m)], k, lane8, ra)
            tn = left_shift(lambda m: T[z + 1, :, tile_at(m)], k, lane8, rt)
            if k == NK - 1:
                an = jnp.where(lane8 == 127, 0.0, an)
                tn = jnp.where(lane8 == 127, 0.0, tn)
            px = (a - an) * (t - tn)
            back = pltpu.roll(px, 1, 1)
            pair = px + jnp.where(lane8 == 0, a * t if last is None else last, back)
            last = back
            au, tu = pltpu.roll(a16, 15, 0)[0:8], jnp.where(row8 == 7, yhi[z, :, sl], rot(t, -1))
            ad, td = pltpu.roll(a16, 1, 0)[0:8], jnp.where(row8 == 0, ylo[z, :, sl], rot(t, 1))
            pair = pair + ((a - au) * (t - tu) + (a - ad) * (t - td))
            pair = pair + (a - A[p + 1, 0:8, sl]) * (t - T[z + 2, :, sl])
            pair = pair + (a - A[p - 1, 0:8, sl]) * (t - T[z, :, sl])
            s = s_ref[z, :, sl]
            switch = info[2 + k // 2].astype(F32)
            scale = base * switch
            if k in (0, NK - 1):
                scale = scale * inv_cover(lane8 + 128 * k, X)
            else:
                scale = scale * (1.0 / float((RADIUS + 1) ** 2))
            R[pl.ds(pl.multiple_of(z * 8, 8), 8), sl] = pair * (s * s) * scale
        return carry

    lax.fori_loop(0, D, plane_raw, 0)

    i = lax.broadcasted_iota(jnp.int32, (512, 256), 0) - 128
    j = lax.broadcasted_iota(jnp.int32, (512, 256), 1)
    weights = jnp.maximum(RADIUS + 1 - jnp.abs(i - j), 0).astype(F32).astype(BF16)
    for n in range(X // 256):
        low, high = max(256 * n - 128, 0), min(256 * n + 384, X)
        x = R[:, low:high]
        w = weights[low - (256 * n - 128) : high - (256 * n - 128)]
        xh = x.astype(BF16)
        xl = (x - xh.astype(F32)).astype(BF16)
        y = jnp.dot(xh, w, preferred_element_type=F32) + jnp.dot(xl, w, preferred_element_type=F32)
        send[2 * n] = y[:, 0:128]
        send[2 * n + 1] = y[:, 128:256]


def filter_y(x_ref, out, s0, s1):
    i = lax.broadcasted_iota(jnp.int32, (128, 128), 0)
    j = lax.broadcasted_iota(jnp.int32, (128, 128), 1)
    w = jnp.maximum(RADIUS + 1 - jnp.abs(i - j), 0).astype(F32).astype(BF16)
    acc0 = jnp.zeros((128, 128), F32)
    acc1 = jnp.zeros((128, 128), F32)
    s0[...] = jnp.zeros((128, 128), F32)
    s1[...] = jnp.zeros((128, 128), F32)
    for z in range(D):
        x = x_ref[:, 8 * z : 8 * z + 8, :].reshape(128, 128)
        xh = x.astype(BF16)
        xl = (x - xh.astype(F32)).astype(BF16)
        y = jnp.dot(w, xh, preferred_element_type=F32) + jnp.dot(w, xl, preferred_element_type=F32)
        out[:, 8 * z : 8 * z + 8, :] = y.reshape(16, 8, 128)
        s0[...] += y
        if z:
            s1[...] += float(z) * y


def filter_z(own, up0, up1, down0, down1, up2, down2, out):
    def chunk(m, carry):
        def load(ref, z):
            return ref[m, 8 * z : 8 * z + 8, :]

        sl = pl.ds(pl.multiple_of(m * 8, 8), 8)
        u0, u1, d0, d1 = up0[sl, :], up1[sl, :], down0[sl, :], down1[sl, :]
        suffix = load(down2, D - 1)
        total = suffix
        far = [None] * D
        far[D - 1] = total
        for z in range(D - 2, -1, -1):
            suffix = suffix + load(down2, z)
            total = total + suffix
            far[z] = total
        sum_own = load(own, 0)
        first = jnp.zeros_like(sum_own)
        for z in range(1, D):
            x = load(own, z)
            sum_own = sum_own + x
            first = first + float(z) * x
        distance = first
        near = (25.0 * (u0 + d0) + (d1 - u1)) + float(RADIUS + 1) * sum_own
        slope = u0 - d0
        prefix_own = jnp.zeros_like(sum_own)
        prefix_up = jnp.zeros_like(sum_own)
        total_up = jnp.zeros_like(sum_own)
        for z in range(D):
            prefix_up = prefix_up + load(up2, z)
            total_up = total_up + prefix_up
            out[m, 8 * z : 8 * z + 8, :] = (near - distance) + (total_up + far[z])
            prefix_own = prefix_own + load(own, z)
            distance = distance + (2.0 * prefix_own - sum_own)
            near = near + slope
        return carry

    lax.fori_loop(0, 16, chunk, 0)


def finish(info, x_ref, out):
    for k in range(NK):
        scale = REPORT_SCALE * info[2 + k // 2].astype(F32)
        for z in range(D):
            out[z, :, tile_at(k)] = x_ref[k, 8 * z : 8 * z + 8, :] * scale


def kernel_call(body, ins, outs, scratch=(), scalars=0, limit=60):
    vmem = pl.BlockSpec(memory_space=pltpu.VMEM)
    smem = pl.BlockSpec(memory_space=pltpu.SMEM)
    return pl.pallas_call(
        body,
        out_shape=[jax.ShapeDtypeStruct(s, F32) for s in outs],
        in_specs=[smem] * scalars + [vmem] * (len(ins) - scalars),
        out_specs=[vmem] * len(outs),
        scratch_shapes=[pltpu.VMEM(s, F32) for s in scratch],
        compiler_params=pltpu.CompilerParams(vmem_limit_bytes=limit * MIB),
    )(*ins)


def moved(x, dz, dy):
    pairs = []
    for g in range(16):
        for b in range(16):
            if 0 <= g + dz < 16 and 0 <= b + dy < 16:
                pairs.append(((g + dz) * 16 + b + dy, g * 16 + b))
    return lax.ppermute(x, ("grp", "blk"), pairs)


def local(solid, thermal, target, coolant, switch):
    info = jnp.concatenate(
        [jnp.stack([lax.axis_index("grp"), lax.axis_index("blk")]).astype(jnp.int32), switch.reshape(8)]
    )
    block, pair = (D, 8, X), tile_shape(2)
    step = pl.BlockSpec((STEP, 8, X), lambda i: (i, 0, 0))
    whole = pl.BlockSpec((8, 8, X), lambda i: (0, 0, 0))
    ylo, yhi, zlo, zhi = pl.pallas_call(
        pack_first,
        grid=(D // STEP,),
        out_shape=[jax.ShapeDtypeStruct(shape, F32) for shape in (block, block, tile_shape(8), tile_shape(8))],
        in_specs=[step] * 4,
        out_specs=[step, step, whole, whole],
        compiler_params=pltpu.CompilerParams(vmem_limit_bytes=12 * MIB),
    )(solid, thermal, target, coolant)
    yhi, ylo = moved(ylo, 0, 1), moved(yhi, 0, -1)
    zlo, zhi = moved(zhi, -1, 0), moved(zlo, 1, 0)
    clo, chi = kernel_call(pack_corners, (zlo, zhi), [pair, pair], limit=8)
    chi, clo = moved(clo, 0, 1), moved(chi, 0, -1)
    ext = (E, 16, X)
    a, y2lo, y2hi, z2lo, z2hi, *fields = kernel_call(
        sweeps_first, (solid, target, coolant, yhi, ylo, zlo, zhi, chi, clo),
        [block, tile_shape(9), tile_shape(9), tile_shape(3), tile_shape(3)] + [ext] * 5, [ext, ext], limit=12,
    )
    y2hi, y2lo = moved(y2lo, 0, 1), moved(y2hi, 0, -1)
    z2lo, z2hi = moved(z2hi, -1, 0), moved(z2lo, 1, 0)
    clo, chi = kernel_call(pack_corners_second, (z2lo, z2hi), [pair, pair], limit=8)
    e_hi, e_lo = moved(clo, 0, 1), moved(chi, 0, -1)
    parts = (16, D * 8, 128)
    (send,) = kernel_call(
        sweeps_second,
        (info, solid, thermal, yhi, ylo, zlo, zhi, a, *fields, y2hi, y2lo, z2lo, z2hi, e_hi, e_lo),
        [parts], [ext, ext, (D + 2, 8, X), (D * 8, X)], scalars=1, limit=16,
    )
    columns = lax.all_to_all(send, "blk", split_axis=0, concat_axis=0, tiled=True)
    along_y, s0, s1 = kernel_call(filter_y, (columns,), [parts, (128, 128), (128, 128)], limit=30)
    sums = jnp.stack([s0, s1])
    up2, down2 = moved(along_y, 2, 0), moved(along_y, -2, 0)
    up, down = moved(sums, 1, 0), moved(sums, -1, 0)
    (along_z,) = kernel_call(
        filter_z, (along_y, up[0], up[1], down[0], down[1], up2, down2), [parts], limit=30
    )
    back = lax.all_to_all(along_z, "blk", split_axis=0, concat_axis=0, tiled=True)
    (out,) = kernel_call(finish, (info, back), [block], scalars=1, limit=30)
    return out


def tile_shape(n):
    return (n, 8, X)


def solution(mesh):
    spec = P("grp", "blk", None)
    return jax.shard_map(
        local, mesh=mesh, in_specs=(spec,) * 5, out_specs=spec, check_vma=False
    )
```

```python
import jax
import jax.numpy as jnp
from jax import lax
from jax.experimental import pallas as pl
from jax.experimental.pallas import tpu as pltpu
from jax.sharding import PartitionSpec as P

RADIUS = 48
COND_FLOOR = 0.001
REPORT_SCALE = 100.0
D, S, X = 24, 8, 2048
NK = X // 128
E = D + 6
STEP = 8
F32 = jnp.float32
BF16 = jnp.bfloat16
MIB = 1024 * 1024


def rows_of(shape):
    return lax.broadcasted_iota(jnp.int32, shape, 0)


def rot(tile, shift):
    shift = shift % 8
    return tile if shift == 0 else pltpu.roll(tile, shift, 0)


def conduct_of(solid):
    return COND_FLOOR + (1.0 - COND_FLOOR) * (solid * solid * solid)


def pack_first(s_hbm, t_hbm, b_hbm, k_hbm, ylo, yhi, zlo, zhi, s_ref, t_ref, b_ref, k_ref, sems):
    pairs = ((s_hbm, s_ref), (b_hbm, b_ref), (k_hbm, k_ref), (t_hbm, t_ref))
    copies = [
        [
            pltpu.make_async_copy(src.at[pl.ds(i * STEP, STEP)], dst.at[pl.ds(i * STEP, STEP)], sems.at[n, i])
            for n, (src, dst) in enumerate(pairs)
        ]
        for i in range(D // STEP)
    ]
    for group in copies:
        for copy in group:
            copy.start()
    r = rows_of((8, X))
    for i, group in enumerate(copies):
        for copy in group:
            copy.wait()

        def plane(z, carry):
            c = conduct_of(s_ref[z])
            b, k, t = b_ref[z], k_ref[z], t_ref[z]
            ylo[z] = jnp.where(r < 3, c, jnp.where(r < 5, rot(b, 3), jnp.where(r < 7, rot(k, 5), rot(t, 7))))
            yhi[z] = jnp.where(r > 4, c, jnp.where(r > 2, rot(b, -3), jnp.where(r > 0, rot(k, -5), rot(t, -7))))
            return carry

        lax.fori_loop(i * STEP, (i + 1) * STEP, plane, 0)
    for dst, at in ((zlo, lambda j: j), (zhi, lambda j: D - 1 - j)):
        for j in range(3):
            dst[j] = conduct_of(s_ref[at(j)])
        for j in range(2):
            dst[3 + j] = b_ref[at(j)]
            dst[5 + j] = k_ref[at(j)]
        dst[7] = t_ref[at(0)]


def pack_corners(zlo, zhi, lo, hi):
    r = rows_of((8, X))
    for i, src in enumerate((zlo, zhi)):
        c1, c2, b1, k1 = src[0], src[1], src[3], src[5]
        lo[i] = jnp.where(r < 2, c1, jnp.where(r == 2, rot(c2, 2), jnp.where(r == 3, rot(b1, 3), rot(k1, 4))))
        hi[i] = jnp.where(r > 5, c1, jnp.where(r == 5, rot(c2, -2), jnp.where(r == 4, rot(b1, -3), rot(k1, -4))))


def pack_corners_second(zlo, zhi, lo, hi):
    r = rows_of((8, X))
    for i, src in enumerate((zlo, zhi)):
        lo[i] = jnp.where(r < 2, src[0], rot(src[1], 2))
        hi[i] = jnp.where(r > 5, src[0], rot(src[1], -2))


def assemble(s_ref, b_ref, k_ref, yhi, ylo, zlo, zhi, chi, clo, C, B, K):
    r = rows_of((8, X))
    zero = jnp.zeros((8, X), F32)

    def plane(z, carry):
        p = z + 3
        C[p, 0:8] = conduct_of(s_ref[z])
        B[p, 0:8] = b_ref[z]
        K[p, 0:8] = k_ref[z]
        h, l = yhi[z], ylo[z]
        C[p, 8:16] = jnp.where(r < 3, h, jnp.where(r > 4, l, 0.0))
        B[p, 8:16] = jnp.where(r < 2, rot(h, -3), jnp.where(r > 5, rot(l, 3), 0.0))
        K[p, 8:16] = jnp.where(r < 2, rot(h, -5), jnp.where(r > 5, rot(l, 5), 0.0))
        return carry

    lax.fori_loop(0, D, plane, 0)
    for i, src, at in ((0, zlo, lambda j: 2 - j), (1, zhi, lambda j: 27 + j)):
        h, l = chi[i], clo[i]
        for j in range(3):
            C[at(j), 0:8] = src[j]
        for j in range(2):
            B[at(j), 0:8] = src[3 + j]
            K[at(j), 0:8] = src[5 + j]
        C[at(0), 8:16] = jnp.where(r < 2, h, jnp.where(r > 5, l, 0.0))
        C[at(1), 8:16] = jnp.where(r == 0, rot(h, -2), jnp.where(r == 7, rot(l, 2), 0.0))
        C[at(2), 8:16] = zero
        B[at(0), 8:16] = jnp.where(r == 0, rot(h, -3), jnp.where(r == 7, rot(l, 3), 0.0))
        K[at(0), 8:16] = jnp.where(r == 0, rot(h, -4), jnp.where(r == 7, rot(l, 4), 0.0))
        B[at(1), 8:16] = zero
        K[at(1), 8:16] = zero


def tile_at(k):
    return slice(128 * k, 128 * k + 128)


def left_shift(load, k, lane, rots):
    for m in (k, (k + 1) % NK):
        if m not in rots:
            rots[m] = pltpu.roll(load(m), 127, 1)
    return jnp.where(lane == 127, rots[(k + 1) % NK], rots[k])


def build(C, A, A0, RD, FX, FY, FZ):
    lane = lax.broadcasted_iota(jnp.int32, (16, 128), 1)

    def plane(p, carry):
        rots, prev = {}, None
        last = None
        for k in range(NK):
            sl = tile_at(k)
            c = C[p, :, sl]
            nxt = left_shift(lambda m: C[p, :, tile_at(m)], k, lane, rots)
            if k == NK - 1:
                nxt = jnp.where(lane == 127, 0.0, nxt)
            fx = c + nxt
            if k == NK - 1:
                fx = jnp.where(lane == 127, 0.0, fx)
            back = pltpu.roll(c, 1, 1)
            before = jnp.where(lane == 0, 0.0 if last is None else last, back)
            last = back
            up = pltpu.roll(c, 15, 0)
            down = pltpu.roll(c, 1, 0)
            cz = C[p + 1, :, sl]
            FX[p, :, sl] = fx
            FY[p, :, sl] = c + up
            FZ[p, :, sl] = c + cz
            coup = RD[p, :, sl]
            diag = coup + (3.0 * c + 0.5 * (nxt + before + up + down + cz + C[p - 1, :, sl]))
            rd = jnp.where(coup > 0.0, 1.0 / jnp.where(coup > 0.0, diag, 1.0), 0.0)
            a = A[p, :, sl] * rd
            A[p, :, sl] = a
            A0[p, :, sl] = (2.0 / 3.0) * a
            RD[p, :, sl] = (1.0 / 3.0) * rd
        return carry

    lax.fori_loop(1, E - 1, plane, 0)

    def edge(i, carry):
        FZ[0, :, pl.ds(pl.multiple_of(i * 128, 128), 128)] = (
            C[0, :, pl.ds(pl.multiple_of(i * 128, 128), 128)] + C[1, :, pl.ds(pl.multiple_of(i * 128, 128), 128)]
        )
        return carry

    lax.fori_loop(0, NK, edge, 0)


def sweep(A, OUT, A0, RD, FX, FY, FZ, both):
    lane = lax.broadcasted_iota(jnp.int32, (8, 128), 1)
    row = lax.broadcasted_iota(jnp.int32, (8, 128), 0)
    first, last, top, bottom = lane == 0, lane == 127, row == 0, row == 7

    def plane(p, halves):
        ahead, back = {}, {}

        def shift(m):
            if m in ahead:
                return
            sl = tile_at(m)
            a = [A[p, 8 * h : 8 * h + 8, sl] for h in range(halves)]
            ahead[m] = [pltpu.roll(x, 127, 1) for x in a]
            back[m] = [pltpu.roll(FX[p, 8 * h : 8 * h + 8, sl] * a[h], 1, 1) for h in range(halves)]

        shift(NK - 1)
        shift(0)
        for k in range(NK):
            sl = tile_at(k)
            shift((k + 1) % NK)
            a = [A[p, 8 * h : 8 * h + 8, sl] for h in (0, 1)]
            fy = [FY[p, 8 * h : 8 * h + 8, sl] for h in (0, 1)]
            up = [pltpu.roll(x, 7, 0) for x in a]
            down = [pltpu.roll(f * x, 1, 0) for f, x in zip(fy, a)]
            for h in range(halves):
                hs = slice(8 * h, 8 * h + 8)
                flux = FX[p, hs, sl] * jnp.where(last, ahead[(k + 1) % NK][h], ahead[k][h])
                flux = flux + jnp.where(first, back[(k - 1) % NK][h], back[k][h])
                flux = flux + (fy[h] * jnp.where(bottom, up[1 - h], up[h]) + jnp.where(top, down[1 - h], down[h]))
                flux = flux + (FZ[p, hs, sl] * A[p + 1, hs, sl] + FZ[p - 1, hs, sl] * A[p - 1, hs, sl])
                OUT[p, hs, sl] = (1.0 / 3.0) * a[h] + (A0[p, hs, sl] + RD[p, hs, sl] * flux)

    low, high, halves = both

    def pair(i, carry):
        plane(low + 2 * i, halves)
        plane(low + 2 * i + 1, halves)
        return carry

    lax.fori_loop(0, (high - low) // 2, pair, 0)
    if halves == 2:

        def ends(i, carry):
            plane(low - 1 + i * (high - low + 1), 1)
            return carry

        lax.fori_loop(0, 2, ends, 0)


def pieces(first, rows):
    out, done = [], 0
    while done < rows:
        n = first + done
        take = min(rows - done, 8 - n % 8)
        out.append((n // 8, n % 8, done, take))
        done += take
    return out


def sweeps_first(s_ref, b_ref, k_ref, yhi, ylo, zlo, zhi, chi, clo,
                 a_out, y2lo, y2hi, z2lo, z2hi, A0, RD, FX, FY, FZ, C, A):
    assemble(s_ref, b_ref, k_ref, yhi, ylo, zlo, zhi, chi, clo, C, A, RD)
    build(C, A, A0, RD, FX, FY, FZ)
    sweep(A, C, A0, RD, FX, FY, FZ, (3, E - 3, 2))
    sweep(C, A, A0, RD, FX, FY, FZ, (3, E - 3, 1))
    r = rows_of((8, X))

    def copy(z, carry):
        a_out[z] = A[z + 3, 0:8]
        return carry

    lax.fori_loop(0, D, copy, 0)

    def group(g, carry):
        low, high = [None] * 3, [None] * 3
        for j in range(8):
            a = A[8 * g + j + 3, 0:8]
            for tile, at, row, take in pieces(3 * j, 3):
                mask = (r >= at) & (r < at + take)
                for msg, src in ((low, row), (high, 5 + row)):
                    moved = rot(a, at - src)
                    msg[tile] = moved if msg[tile] is None else jnp.where(mask, moved, msg[tile])
        for i in range(3):
            y2lo[3 * g + i] = low[i]
            y2hi[3 * g + i] = high[i]
        return carry

    lax.fori_loop(0, 3, group, 0)
    for j in range(3):
        z2lo[j] = A[3 + j, 0:8]
        z2hi[j] = A[26 - j, 0:8]


def tri(u):
    m = jnp.maximum(RADIUS - u, 0)
    return m * (m + 1) // 2


def inv_cover(position, length):
    total = (RADIUS + 1) ** 2 - tri(position) - tri(length - 1 - position)
    return 1.0 / total.astype(F32)


def sweeps_second(info, s_ref, t_ref, yhi, ylo, zlo, zhi, a_in, A0, RD, FX, FY, FZ,
                  y2hi, y2lo, z2lo, z2hi, e_hi, e_lo, send, A, B, T, R):
    r = rows_of((8, X))
    zero = jnp.zeros((8, X), F32)

    def group(g, carry):
        for j in range(8):
            z = 8 * g + j
            A[z + 3, 0:8] = a_in[z]
            side = zero
            for tile, at, row, take in pieces(3 * j, 3):
                side = jnp.where((r >= row) & (r < row + take), rot(y2hi[3 * g + tile], row - at), side)
                side = jnp.where((r >= 5 + row) & (r < 5 + row + take), rot(y2lo[3 * g + tile], 5 + row - at), side)
            A[z + 3, 8:16] = side
        return carry

    lax.fori_loop(0, 3, group, 0)
    for i, src, at in ((0, z2lo, lambda j: 2 - j), (1, z2hi, lambda j: 27 + j)):
        h, l = e_hi[i], e_lo[i]
        for j in range(3):
            A[at(j), 0:8] = src[j]
        A[at(0), 8:16] = jnp.where(r < 2, h, jnp.where(r > 5, l, 0.0))
        A[at(1), 8:16] = jnp.where(r == 0, rot(h, -2), jnp.where(r == 7, rot(l, 2), 0.0))
        A[at(2), 8:16] = zero
    sweep(A, B, A0, RD, FX, FY, FZ, (2, E - 2, 2))
    sweep(B, A, A0, RD, FX, FY, FZ, (3, E - 3, 2))

    def plane_t(z, carry):
        T[z + 1] = t_ref[z]
        return carry

    lax.fori_loop(0, D, plane_t, 0)
    T[0] = zlo[7]
    T[D + 1] = zhi[7]

    lane8 = lax.broadcasted_iota(jnp.int32, (8, 128), 1)
    row8 = lax.broadcasted_iota(jnp.int32, (8, 128), 0)
    cover_y = inv_cover(lax.axis_index("blk") * S + row8, 16 * S)
    base_z = lax.axis_index("grp") * D
    factor = -0.5 * 3.0 * (1.0 - COND_FLOOR)

    def plane_raw(z, carry):
        p = z + 3
        base = cover_y * inv_cover(base_z + z + jnp.zeros((8, 128), jnp.int32), 16 * D) * factor
        ra, rt = {}, {}
        last = None
        for k in range(NK):
            sl = tile_at(k)
            a16 = A[p, :, sl]
            a, t = a16[0:8], T[z + 1, :, sl]
            an = left_shift(lambda m: A[p, 0:8, tile_at(m)], k, lane8, ra)
            tn = left_shift(lambda m: T[z + 1, :, tile_at(m)], k, lane8, rt)
            if k == NK - 1:
                an = jnp.where(lane8 == 127, 0.0, an)
                tn = jnp.where(lane8 == 127, 0.0, tn)
            px = (a - an) * (t - tn)
            back = pltpu.roll(px, 1, 1)
            pair = px + jnp.where(lane8 == 0, a * t if last is None else last, back)
            last = back
            au, tu = pltpu.roll(a16, 15, 0)[0:8], jnp.where(row8 == 7, yhi[z, :, sl], rot(t, -1))
            ad, td = pltpu.roll(a16, 1, 0)[0:8], jnp.where(row8 == 0, ylo[z, :, sl], rot(t, 1))
            pair = pair + ((a - au) * (t - tu) + (a - ad) * (t - td))
            pair = pair + (a - A[p + 1, 0:8, sl]) * (t - T[z + 2, :, sl])
            pair = pair + (a - A[p - 1, 0:8, sl]) * (t - T[z, :, sl])
            s = s_ref[z, :, sl]
            switch = info[k // 2].astype(F32)
            scale = base * switch
            if k in (0, NK - 1):
                scale = scale * inv_cover(lane8 + 128 * k, X)
            else:
                scale = scale * (1.0 / float((RADIUS + 1) ** 2))
            R[pl.ds(pl.multiple_of(z * 8, 8), 8), sl] = pair * (s * s) * scale
        return carry

    lax.fori_loop(0, D, plane_raw, 0)

    i = lax.broadcasted_iota(jnp.int32, (512, 256), 0) - 128
    j = lax.broadcasted_iota(jnp.int32, (512, 256), 1)
    weights = jnp.maximum(RADIUS + 1 - jnp.abs(i - j), 0).astype(F32).astype(BF16)
    for n in range(X // 256):
        low, high = max(256 * n - 128, 0), min(256 * n + 384, X)
        x = R[:, low:high]
        w = weights[low - (256 * n - 128) : high - (256 * n - 128)]
        xh = x.astype(BF16)
        xl = (x - xh.astype(F32)).astype(BF16)
        y = jnp.dot(xh, w, preferred_element_type=F32) + jnp.dot(xl, w, preferred_element_type=F32)
        send[2 * n] = y[:, 0:128]
        send[2 * n + 1] = y[:, 128:256]


def filter_y(x_ref, out, sums):
    i = lax.broadcasted_iota(jnp.int32, (128, 128), 0)
    j = lax.broadcasted_iota(jnp.int32, (128, 128), 1)
    w = jnp.maximum(RADIUS + 1 - jnp.abs(i - j), 0).astype(F32).astype(BF16)
    sums[...] = jnp.zeros((2, 128, 128), F32)
    for z in range(D):
        x = x_ref[:, 8 * z : 8 * z + 8, :].reshape(128, 128)
        xh = x.astype(BF16)
        xl = (x - xh.astype(F32)).astype(BF16)
        y = jnp.dot(w, xh, preferred_element_type=F32) + jnp.dot(w, xl, preferred_element_type=F32)
        out[:, 8 * z : 8 * z + 8, :] = y.reshape(16, 8, 128)
        sums[0] += y
        if z:
            sums[1] += float(z) * y


def filter_z(own, up, down, up2, down2, out):
    def chunk(m, carry):
        def load(ref, z):
            return ref[m, 8 * z : 8 * z + 8, :]

        sl = pl.ds(pl.multiple_of(m * 8, 8), 8)
        u0, u1, d0, d1 = up[0, sl, :], up[1, sl, :], down[0, sl, :], down[1, sl, :]
        suffix = load(down2, D - 1)
        total = suffix
        far = [None] * D
        far[D - 1] = total
        for z in range(D - 2, -1, -1):
            suffix = suffix + load(down2, z)
            total = total + suffix
            far[z] = total
        sum_own = load(own, 0)
        first = jnp.zeros_like(sum_own)
        for z in range(1, D):
            x = load(own, z)
            sum_own = sum_own + x
            first = first + float(z) * x
        distance = first
        near = (25.0 * (u0 + d0) + (d1 - u1)) + float(RADIUS + 1) * sum_own
        slope = u0 - d0
        prefix_own = jnp.zeros_like(sum_own)
        prefix_up = jnp.zeros_like(sum_own)
        total_up = jnp.zeros_like(sum_own)
        for z in range(D):
            prefix_up = prefix_up + load(up2, z)
            total_up = total_up + prefix_up
            out[m, 8 * z : 8 * z + 8, :] = (near - distance) + (total_up + far[z])
            prefix_own = prefix_own + load(own, z)
            distance = distance + (2.0 * prefix_own - sum_own)
            near = near + slope
        return carry

    lax.fori_loop(0, 16, chunk, 0)


def finish(info, x_ref, out):
    for k in range(NK):
        scale = REPORT_SCALE * info[k // 2].astype(F32)
        for z in range(D):
            out[z, :, tile_at(k)] = x_ref[k, 8 * z : 8 * z + 8, :] * scale


def kernel_call(body, ins, outs, scratch=(), scalars=0, limit=60):
    vmem = pl.BlockSpec(memory_space=pltpu.VMEM)
    smem = pl.BlockSpec(memory_space=pltpu.SMEM)
    return pl.pallas_call(
        body,
        out_shape=[jax.ShapeDtypeStruct(s, F32) for s in outs],
        in_specs=[smem] * scalars + [vmem] * (len(ins) - scalars),
        out_specs=[vmem] * len(outs),
        scratch_shapes=[pltpu.VMEM(s, F32) for s in scratch],
        compiler_params=pltpu.CompilerParams(vmem_limit_bytes=limit * MIB),
    )(*ins)


def moved(x, dz, dy):
    pairs = []
    for g in range(16):
        for b in range(16):
            if 0 <= g + dz < 16 and 0 <= b + dy < 16:
                pairs.append(((g + dz) * 16 + b + dy, g * 16 + b))
    return lax.ppermute(x, ("grp", "blk"), pairs)


def local(solid, thermal, target, coolant, switch):
    info = switch.reshape(8)
    block, pair = (D, 8, X), tile_shape(2)
    ylo, yhi, zlo, zhi = pl.pallas_call(
        pack_first,
        out_shape=[jax.ShapeDtypeStruct(shape, F32) for shape in (block, block, tile_shape(8), tile_shape(8))],
        in_specs=[pl.BlockSpec(memory_space=pltpu.HBM)] * 4,
        out_specs=[pl.BlockSpec(memory_space=pltpu.VMEM)] * 4,
        scratch_shapes=[pltpu.VMEM(block, F32)] * 4 + [pltpu.SemaphoreType.DMA((4, D // STEP))],
        compiler_params=pltpu.CompilerParams(vmem_limit_bytes=9 * MIB),
    )(solid, thermal, target, coolant)
    yhi, ylo = moved(ylo, 0, 1), moved(yhi, 0, -1)
    zlo, zhi = moved(zhi, -1, 0), moved(zlo, 1, 0)
    clo, chi = kernel_call(pack_corners, (zlo, zhi), [pair, pair], limit=8)
    chi, clo = moved(clo, 0, 1), moved(chi, 0, -1)
    ext = (E, 16, X)
    a, y2lo, y2hi, z2lo, z2hi, *fields = kernel_call(
        sweeps_first, (solid, target, coolant, yhi, ylo, zlo, zhi, chi, clo),
        [block, tile_shape(9), tile_shape(9), tile_shape(3), tile_shape(3)] + [ext] * 5, [ext, ext], limit=12,
    )
    y2hi, y2lo = moved(y2lo, 0, 1), moved(y2hi, 0, -1)
    z2lo, z2hi = moved(z2hi, -1, 0), moved(z2lo, 1, 0)
    clo, chi = kernel_call(pack_corners_second, (z2lo, z2hi), [pair, pair], limit=8)
    e_hi, e_lo = moved(clo, 0, 1), moved(chi, 0, -1)
    parts = (16, D * 8, 128)
    (send,) = kernel_call(
        sweeps_second,
        (info, solid, thermal, yhi, ylo, zlo, zhi, a, *fields, y2hi, y2lo, z2lo, z2hi, e_hi, e_lo),
        [parts], [ext, ext, (D + 2, 8, X), (D * 8, X)], scalars=1, limit=16,
    )
    columns = lax.all_to_all(send, "blk", split_axis=0, concat_axis=0, tiled=True)
    along_y, sums = kernel_call(filter_y, (columns,), [parts, (2, 128, 128)], limit=8)
    up2, down2 = moved(along_y, 2, 0), moved(along_y, -2, 0)
    up, down = moved(sums, 1, 0), moved(sums, -1, 0)
    (along_z,) = kernel_call(
        filter_z, (along_y, up, down, up2, down2), [parts], limit=8
    )
    back = lax.all_to_all(along_z, "blk", split_axis=0, concat_axis=0, tiled=True)
    (out,) = kernel_call(finish, (info, back), [block], scalars=1, limit=8)
    return out


def tile_shape(n):
    return (n, 8, X)


def solution(mesh):
    spec = P("grp", "blk", None)
    return jax.shard_map(
        local, mesh=mesh, in_specs=(spec,) * 5, out_specs=spec, check_vma=False
    )
```

```python
import jax
import jax.numpy as jnp
from jax import lax
from jax.experimental import pallas as pl
from jax.experimental.pallas import tpu as pltpu
from jax.sharding import PartitionSpec as P

RADIUS = 48
COND_FLOOR = 0.001
REPORT_SCALE = 100.0
D, S, X = 24, 8, 2048
NK = X // 128
E = D + 6
STEP = 8
HALF = NK // 2
F32 = jnp.float32
BF16 = jnp.bfloat16
MIB = 1024 * 1024


def rows_of(shape):
    return lax.broadcasted_iota(jnp.int32, shape, 0)


def rot(tile, shift):
    shift = shift % 8
    return tile if shift == 0 else pltpu.roll(tile, shift, 0)


def conduct_of(solid):
    return COND_FLOOR + (1.0 - COND_FLOOR) * (solid * solid * solid)


def pack_first(s_hbm, t_hbm, b_hbm, k_hbm, ylo_hbm, yhi_hbm, zlo_hbm, zhi_hbm,
               s_ref, t_ref, b_ref, k_ref, ylo, yhi, zlo, zhi, sems, out_sems):
    pairs = ((s_hbm, s_ref), (b_hbm, b_ref), (k_hbm, k_ref), (t_hbm, t_ref))
    copies = [
        [
            pltpu.make_async_copy(src.at[pl.ds(i * STEP, STEP)], dst.at[pl.ds(i * STEP, STEP)], sems.at[n, i])
            for n, (src, dst) in enumerate(pairs)
        ]
        for i in range(D // STEP)
    ]
    for group in copies:
        for copy in group:
            copy.start()
    r = rows_of((8, X))
    outs = []
    for i, group in enumerate(copies):
        for copy in group:
            copy.wait()

        def plane(z, carry):
            c = conduct_of(s_ref[z])
            b, k, t = b_ref[z], k_ref[z], t_ref[z]
            ylo[z] = jnp.where(r < 3, c, jnp.where(r < 5, rot(b, 3), jnp.where(r < 7, rot(k, 5), rot(t, 7))))
            yhi[z] = jnp.where(r > 4, c, jnp.where(r > 2, rot(b, -3), jnp.where(r > 0, rot(k, -5), rot(t, -7))))
            return carry

        lax.fori_loop(i * STEP, (i + 1) * STEP, plane, 0)
        part = pl.ds(i * STEP, STEP)
        outs += [
            pltpu.make_async_copy(ylo.at[part], ylo_hbm.at[part], out_sems.at[0, i]),
            pltpu.make_async_copy(yhi.at[part], yhi_hbm.at[part], out_sems.at[1, i]),
        ]
        outs[-2].start()
        outs[-1].start()
    for dst, at in ((zlo, lambda j: j), (zhi, lambda j: D - 1 - j)):
        for j in range(3):
            dst[j] = conduct_of(s_ref[at(j)])
        for j in range(2):
            dst[3 + j] = b_ref[at(j)]
            dst[5 + j] = k_ref[at(j)]
        dst[7] = t_ref[at(0)]
    outs += [
        pltpu.make_async_copy(zlo, zlo_hbm, out_sems.at[2, 0]),
        pltpu.make_async_copy(zhi, zhi_hbm, out_sems.at[2, 1]),
    ]
    outs[-2].start()
    outs[-1].start()
    for copy in outs:
        copy.wait()


def pack_corners(zlo, zhi, lo, hi):
    r = rows_of((8, X))
    for i, src in enumerate((zlo, zhi)):
        c1, c2, b1, k1 = src[0], src[1], src[3], src[5]
        lo[i] = jnp.where(r < 2, c1, jnp.where(r == 2, rot(c2, 2), jnp.where(r == 3, rot(b1, 3), rot(k1, 4))))
        hi[i] = jnp.where(r > 5, c1, jnp.where(r == 5, rot(c2, -2), jnp.where(r == 4, rot(b1, -3), rot(k1, -4))))


def pack_corners_second(zlo, zhi, lo, hi):
    r = rows_of((8, X))
    for i, src in enumerate((zlo, zhi)):
        lo[i] = jnp.where(r < 2, src[0], rot(src[1], 2))
        hi[i] = jnp.where(r > 5, src[0], rot(src[1], -2))


def assemble(s_ref, b_ref, k_ref, yhi, ylo, zlo, zhi, chi, clo, C, B, K):
    r = rows_of((8, X))
    zero = jnp.zeros((8, X), F32)

    def plane(z, carry):
        p = z + 3
        C[p, 0:8] = conduct_of(s_ref[z])
        B[p, 0:8] = b_ref[z]
        K[p, 0:8] = k_ref[z]
        h, l = yhi[z], ylo[z]
        C[p, 8:16] = jnp.where(r < 3, h, jnp.where(r > 4, l, 0.0))
        B[p, 8:16] = jnp.where(r < 2, rot(h, -3), jnp.where(r > 5, rot(l, 3), 0.0))
        K[p, 8:16] = jnp.where(r < 2, rot(h, -5), jnp.where(r > 5, rot(l, 5), 0.0))
        return carry

    lax.fori_loop(0, D, plane, 0)
    for i, src, at in ((0, zlo, lambda j: 2 - j), (1, zhi, lambda j: 27 + j)):
        h, l = chi[i], clo[i]
        for j in range(3):
            C[at(j), 0:8] = src[j]
        for j in range(2):
            B[at(j), 0:8] = src[3 + j]
            K[at(j), 0:8] = src[5 + j]
        C[at(0), 8:16] = jnp.where(r < 2, h, jnp.where(r > 5, l, 0.0))
        C[at(1), 8:16] = jnp.where(r == 0, rot(h, -2), jnp.where(r == 7, rot(l, 2), 0.0))
        C[at(2), 8:16] = zero
        B[at(0), 8:16] = jnp.where(r == 0, rot(h, -3), jnp.where(r == 7, rot(l, 3), 0.0))
        K[at(0), 8:16] = jnp.where(r == 0, rot(h, -4), jnp.where(r == 7, rot(l, 4), 0.0))
        B[at(1), 8:16] = zero
        K[at(1), 8:16] = zero


def tile_at(k):
    return slice(128 * k, 128 * k + 128)


def left_shift(load, k, lane, rots):
    for m in (k, (k + 1) % NK):
        if m not in rots:
            rots[m] = pltpu.roll(load(m), 127, 1)
    return jnp.where(lane == 127, rots[(k + 1) % NK], rots[k])


def build(C, A, A0, RD, FX, FY, FZ):
    lane = lax.broadcasted_iota(jnp.int32, (16, 128), 1)

    def plane(p, carry):
        rots, prev = {}, None
        last = None
        for k in range(NK):
            sl = tile_at(k)
            c = C[p, :, sl]
            nxt = left_shift(lambda m: C[p, :, tile_at(m)], k, lane, rots)
            if k == NK - 1:
                nxt = jnp.where(lane == 127, 0.0, nxt)
            fx = c + nxt
            if k == NK - 1:
                fx = jnp.where(lane == 127, 0.0, fx)
            back = pltpu.roll(c, 1, 1)
            before = jnp.where(lane == 0, 0.0 if last is None else last, back)
            last = back
            up = pltpu.roll(c, 15, 0)
            down = pltpu.roll(c, 1, 0)
            cz = C[p + 1, :, sl]
            FX[p, :, sl] = fx
            FY[p, :, sl] = c + up
            FZ[p, :, sl] = c + cz
            coup = RD[p, :, sl]
            diag = coup + (3.0 * c + 0.5 * (nxt + before + up + down + cz + C[p - 1, :, sl]))
            rd = jnp.where(coup > 0.0, 1.0 / jnp.where(coup > 0.0, diag, 1.0), 0.0)
            a = A[p, :, sl] * rd
            A[p, :, sl] = a
            A0[p, :, sl] = (2.0 / 3.0) * a
            RD[p, :, sl] = (1.0 / 3.0) * rd
        return carry

    lax.fori_loop(1, E - 1, plane, 0)

    def edge(i, carry):
        FZ[0, :, pl.ds(pl.multiple_of(i * 128, 128), 128)] = (
            C[0, :, pl.ds(pl.multiple_of(i * 128, 128), 128)] + C[1, :, pl.ds(pl.multiple_of(i * 128, 128), 128)]
        )
        return carry

    lax.fori_loop(0, NK, edge, 0)


def sweep(A, OUT, A0, RD, FX, FY, FZ, both):
    lane = lax.broadcasted_iota(jnp.int32, (8, 128), 1)
    row = lax.broadcasted_iota(jnp.int32, (8, 128), 0)
    first, last, top, bottom = lane == 0, lane == 127, row == 0, row == 7

    def plane(p, halves):
        ahead, back = {}, {}

        def shift(m):
            if m in ahead:
                return
            sl = tile_at(m)
            a = [A[p, 8 * h : 8 * h + 8, sl] for h in range(halves)]
            ahead[m] = [pltpu.roll(x, 127, 1) for x in a]
            back[m] = [pltpu.roll(FX[p, 8 * h : 8 * h + 8, sl] * a[h], 1, 1) for h in range(halves)]

        shift(NK - 1)
        shift(0)
        for k in range(NK):
            sl = tile_at(k)
            shift((k + 1) % NK)
            a = [A[p, 8 * h : 8 * h + 8, sl] for h in (0, 1)]
            fy = [FY[p, 8 * h : 8 * h + 8, sl] for h in (0, 1)]
            up = [pltpu.roll(x, 7, 0) for x in a]
            down = [pltpu.roll(f * x, 1, 0) for f, x in zip(fy, a)]
            for h in range(halves):
                hs = slice(8 * h, 8 * h + 8)
                flux = FX[p, hs, sl] * jnp.where(last, ahead[(k + 1) % NK][h], ahead[k][h])
                flux = flux + jnp.where(first, back[(k - 1) % NK][h], back[k][h])
                flux = flux + (fy[h] * jnp.where(bottom, up[1 - h], up[h]) + jnp.where(top, down[1 - h], down[h]))
                flux = flux + (FZ[p, hs, sl] * A[p + 1, hs, sl] + FZ[p - 1, hs, sl] * A[p - 1, hs, sl])
                OUT[p, hs, sl] = (1.0 / 3.0) * a[h] + (A0[p, hs, sl] + RD[p, hs, sl] * flux)

    low, high, halves = both

    def pair(i, carry):
        plane(low + 2 * i, halves)
        plane(low + 2 * i + 1, halves)
        return carry

    lax.fori_loop(0, (high - low) // 2, pair, 0)
    if halves == 2:

        def ends(i, carry):
            plane(low - 1 + i * (high - low + 1), 1)
            return carry

        lax.fori_loop(0, 2, ends, 0)


def pieces(first, rows):
    out, done = [], 0
    while done < rows:
        n = first + done
        take = min(rows - done, 8 - n % 8)
        out.append((n // 8, n % 8, done, take))
        done += take
    return out


def sweeps_first(s_ref, b_ref, k_ref, yhi, ylo, zlo, zhi, chi, clo,
                 a_out, y2lo, y2hi, z2lo, z2hi, A0, RD, FX, FY, FZ, C, A):
    assemble(s_ref, b_ref, k_ref, yhi, ylo, zlo, zhi, chi, clo, C, A, RD)
    build(C, A, A0, RD, FX, FY, FZ)
    sweep(A, C, A0, RD, FX, FY, FZ, (3, E - 3, 2))
    sweep(C, A, A0, RD, FX, FY, FZ, (3, E - 3, 1))
    r = rows_of((8, X))

    def copy(z, carry):
        a_out[z] = A[z + 3, 0:8]
        return carry

    lax.fori_loop(0, D, copy, 0)

    def group(g, carry):
        low, high = [None] * 3, [None] * 3
        for j in range(8):
            a = A[8 * g + j + 3, 0:8]
            for tile, at, row, take in pieces(3 * j, 3):
                mask = (r >= at) & (r < at + take)
                for msg, src in ((low, row), (high, 5 + row)):
                    moved = rot(a, at - src)
                    msg[tile] = moved if msg[tile] is None else jnp.where(mask, moved, msg[tile])
        for i in range(3):
            y2lo[3 * g + i] = low[i]
            y2hi[3 * g + i] = high[i]
        return carry

    lax.fori_loop(0, 3, group, 0)
    for j in range(3):
        z2lo[j] = A[3 + j, 0:8]
        z2hi[j] = A[26 - j, 0:8]


def tri(u):
    m = jnp.maximum(RADIUS - u, 0)
    return m * (m + 1) // 2


def inv_cover(position, length):
    total = (RADIUS + 1) ** 2 - tri(position) - tri(length - 1 - position)
    return 1.0 / total.astype(F32)


def sweeps_second(info, s_ref, t_ref, yhi, ylo, zlo, zhi, a_in, A0, RD, FX, FY, FZ,
                  y2hi, y2lo, z2lo, z2hi, e_hi, e_lo, send, late, sums, A, B, T, R):
    r = rows_of((8, X))
    zero = jnp.zeros((8, X), F32)

    def group(g, carry):
        for j in range(8):
            z = 8 * g + j
            A[z + 3, 0:8] = a_in[z]
            side = zero
            for tile, at, row, take in pieces(3 * j, 3):
                side = jnp.where((r >= row) & (r < row + take), rot(y2hi[3 * g + tile], row - at), side)
                side = jnp.where((r >= 5 + row) & (r < 5 + row + take), rot(y2lo[3 * g + tile], 5 + row - at), side)
            A[z + 3, 8:16] = side
        return carry

    lax.fori_loop(0, 3, group, 0)
    for i, src, at in ((0, z2lo, lambda j: 2 - j), (1, z2hi, lambda j: 27 + j)):
        h, l = e_hi[i], e_lo[i]
        for j in range(3):
            A[at(j), 0:8] = src[j]
        A[at(0), 8:16] = jnp.where(r < 2, h, jnp.where(r > 5, l, 0.0))
        A[at(1), 8:16] = jnp.where(r == 0, rot(h, -2), jnp.where(r == 7, rot(l, 2), 0.0))
        A[at(2), 8:16] = zero
    sweep(A, B, A0, RD, FX, FY, FZ, (2, E - 2, 2))
    sweep(B, A, A0, RD, FX, FY, FZ, (3, E - 3, 2))

    def plane_t(z, carry):
        T[z + 1] = t_ref[z]
        return carry

    lax.fori_loop(0, D, plane_t, 0)
    T[0] = zlo[7]
    T[D + 1] = zhi[7]

    lane8 = lax.broadcasted_iota(jnp.int32, (8, 128), 1)
    row8 = lax.broadcasted_iota(jnp.int32, (8, 128), 0)
    cover_y = inv_cover(lax.axis_index("blk") * S + row8, 16 * S)
    base_z = lax.axis_index("grp") * D
    factor = -0.5 * 3.0 * (1.0 - COND_FLOOR)

    def plane_raw(z, carry):
        p = z + 3
        base = cover_y * inv_cover(base_z + z + jnp.zeros((8, 128), jnp.int32), 16 * D) * factor
        ra, rt = {}, {}
        last = None
        for k in range(NK):
            sl = tile_at(k)
            a16 = A[p, :, sl]
            a, t = a16[0:8], T[z + 1, :, sl]
            an = left_shift(lambda m: A[p, 0:8, tile_at(m)], k, lane8, ra)
            tn = left_shift(lambda m: T[z + 1, :, tile_at(m)], k, lane8, rt)
            if k == NK - 1:
                an = jnp.where(lane8 == 127, 0.0, an)
                tn = jnp.where(lane8 == 127, 0.0, tn)
            px = (a - an) * (t - tn)
            back = pltpu.roll(px, 1, 1)
            pair = px + jnp.where(lane8 == 0, a * t if last is None else last, back)
            last = back
            au, tu = pltpu.roll(a16, 15, 0)[0:8], jnp.where(row8 == 7, yhi[z, :, sl], rot(t, -1))
            ad, td = pltpu.roll(a16, 1, 0)[0:8], jnp.where(row8 == 0, ylo[z, :, sl], rot(t, 1))
            pair = pair + ((a - au) * (t - tu) + (a - ad) * (t - td))
            pair = pair + (a - A[p + 1, 0:8, sl]) * (t - T[z + 2, :, sl])
            pair = pair + (a - A[p - 1, 0:8, sl]) * (t - T[z, :, sl])
            s = s_ref[z, :, sl]
            switch = info[k // 2].astype(F32)
            scale = base * switch
            if k in (0, NK - 1):
                scale = scale * inv_cover(lane8 + 128 * k, X)
            else:
                scale = scale * (1.0 / float((RADIUS + 1) ** 2))
            R[pl.ds(pl.multiple_of(z * 8, 8), 8), sl] = pair * (s * s) * scale
        return carry

    lax.fori_loop(0, D, plane_raw, 0)

    i = lax.broadcasted_iota(jnp.int32, (512, 256), 0) - 128
    j = lax.broadcasted_iota(jnp.int32, (512, 256), 1)
    weights = jnp.maximum(RADIUS + 1 - jnp.abs(i - j), 0).astype(F32).astype(BF16)
    for n in range(X // 256):
        low, high = max(256 * n - 128, 0), min(256 * n + 384, X)
        x = R[:, low:high]
        w = weights[low - (256 * n - 128) : high - (256 * n - 128)]
        xh = x.astype(BF16)
        xl = (x - xh.astype(F32)).astype(BF16)
        y = jnp.dot(xh, w, preferred_element_type=F32) + jnp.dot(xl, w, preferred_element_type=F32)
        for h in range(2):
            part, m = y[:, 128 * h : 128 * h + 128], (2 * n + h) % HALF
            if n < X // 512:
                send[m] = part[0 : 4 * D]
                send[HALF + m] = part[4 * D :]
            else:
                late[m] = part
                layers = [part[8 * z : 8 * z + 8] for z in range(D)]
                sums[0, 8 * m : 8 * m + 8] = sum(layers)
                sums[1, 8 * m : 8 * m + 8] = sum(float(z) * layers[z] for z in range(1, D))


def filter_y(x_ref, out):
    i = lax.broadcasted_iota(jnp.int32, (128, 128), 0)
    j = lax.broadcasted_iota(jnp.int32, (128, 128), 1)
    w = jnp.maximum(RADIUS + 1 - jnp.abs(i - j), 0).astype(F32).astype(BF16)
    for z in range(D // 2):
        x = x_ref[:, 8 * z : 8 * z + 8, :].reshape(128, 128)
        xh = x.astype(BF16)
        xl = (x - xh.astype(F32)).astype(BF16)
        y = jnp.dot(w, xh, preferred_element_type=F32) + jnp.dot(w, xl, preferred_element_type=F32)
        out[:, 8 * z : 8 * z + 8, :] = y.reshape(16, 8, 128)


def whole_layer(ref, m, z):
    return ref[m, 8 * z : 8 * z + 8, :]


def split_layer(ref, m, z):
    return ref[HALF * (z // (D // 2)) + m, 8 * (z % (D // 2)) : 8 * (z % (D // 2)) + 8, :]


def layer_sums(x_ref, sums):
    def chunk(m, carry):
        layers = [split_layer(x_ref, m, z) for z in range(D)]
        sl = pl.ds(pl.multiple_of(m * 8, 8), 8)
        sums[0, sl] = sum(layers)
        sums[1, sl] = sum(float(z) * layers[z] for z in range(1, D))
        return carry

    lax.fori_loop(0, HALF, chunk, 0)


def filter_z(load, m, own, up, down, up2, down2, store):
    sl = pl.ds(pl.multiple_of(m * 8, 8), 8)
    u0, u1, d0, d1 = up[0, sl, :], up[1, sl, :], down[0, sl, :], down[1, sl, :]
    suffix = load(down2, m, D - 1)
    total = suffix
    far = [None] * D
    far[D - 1] = total
    for z in range(D - 2, -1, -1):
        suffix = suffix + load(down2, m, z)
        total = total + suffix
        far[z] = total
    sum_own = load(own, m, 0)
    distance = jnp.zeros_like(sum_own)
    for z in range(1, D):
        x = load(own, m, z)
        sum_own = sum_own + x
        distance = distance + float(z) * x
    near = (25.0 * (u0 + d0) + (d1 - u1)) + float(RADIUS + 1) * sum_own
    slope = u0 - d0
    prefix_own = jnp.zeros_like(sum_own)
    prefix_up = jnp.zeros_like(sum_own)
    total_up = jnp.zeros_like(sum_own)
    for z in range(D):
        prefix_up = prefix_up + load(up2, m, z)
        total_up = total_up + prefix_up
        store(z, (near - distance) + (total_up + far[z]))
        prefix_own = prefix_own + load(own, m, z)
        distance = distance + (2.0 * prefix_own - sum_own)
        near = near + slope


def filter_z_late(own, up, down, up2, down2, out):
    def chunk(m, carry):
        def store(z, value):
            out[HALF * (z // (D // 2)) + m, 8 * (z % (D // 2)) : 8 * (z % (D // 2)) + 8, :] = value

        filter_z(whole_layer, m, own, up, down, up2, down2, store)
        return carry

    lax.fori_loop(0, HALF, chunk, 0)


def finish(info, own, up, down, up2, down2, late, out):
    def chunk(m, carry):
        column = pl.ds(pl.multiple_of(m * 128, 128), 128)
        scale = REPORT_SCALE * info[m // 2].astype(F32)

        def store(z, value):
            out[z, :, column] = value * scale

        filter_z(split_layer, m, own, up, down, up2, down2, store)
        column = pl.ds(pl.multiple_of(m * 128 + X // 2, 128), 128)
        scale_late = REPORT_SCALE * info[HALF // 2 + m // 2].astype(F32)
        for z in range(D):
            out[z, :, column] = split_layer(late, m, z) * scale_late
        return carry

    lax.fori_loop(0, HALF, chunk, 0)


def kernel_call(body, ins, outs, scratch=(), scalars=0, limit=60):
    vmem = pl.BlockSpec(memory_space=pltpu.VMEM)
    smem = pl.BlockSpec(memory_space=pltpu.SMEM)
    return pl.pallas_call(
        body,
        out_shape=[jax.ShapeDtypeStruct(s, F32) for s in outs],
        in_specs=[smem] * scalars + [vmem] * (len(ins) - scalars),
        out_specs=[vmem] * len(outs),
        scratch_shapes=[pltpu.VMEM(s, F32) for s in scratch],
        compiler_params=pltpu.CompilerParams(vmem_limit_bytes=limit * MIB),
    )(*ins)


def moved(x, dz, dy):
    pairs = []
    for g in range(16):
        for b in range(16):
            if 0 <= g + dz < 16 and 0 <= b + dy < 16:
                pairs.append(((g + dz) * 16 + b + dy, g * 16 + b))
    return lax.ppermute(x, ("grp", "blk"), pairs)


def local(solid, thermal, target, coolant, switch):
    info = switch.reshape(8)
    block, pair = (D, 8, X), tile_shape(2)
    ylo, yhi, zlo, zhi = pl.pallas_call(
        pack_first,
        out_shape=[jax.ShapeDtypeStruct(shape, F32) for shape in (block, block, tile_shape(8), tile_shape(8))],
        in_specs=[pl.BlockSpec(memory_space=pltpu.HBM)] * 4,
        out_specs=[pl.BlockSpec(memory_space=pltpu.HBM)] * 4,
        scratch_shapes=[pltpu.VMEM(block, F32)] * 6
        + [pltpu.VMEM(tile_shape(8), F32)] * 2
        + [pltpu.SemaphoreType.DMA((4, D // STEP)), pltpu.SemaphoreType.DMA((3, D // STEP))],
        compiler_params=pltpu.CompilerParams(vmem_limit_bytes=60 * MIB),
    )(solid, thermal, target, coolant)
    yhi, ylo = moved(ylo, 0, 1), moved(yhi, 0, -1)
    zlo, zhi = moved(zhi, -1, 0), moved(zlo, 1, 0)
    clo, chi = kernel_call(pack_corners, (zlo, zhi), [pair, pair], limit=8)
    chi, clo = moved(clo, 0, 1), moved(chi, 0, -1)
    ext = (E, 16, X)
    a, y2lo, y2hi, z2lo, z2hi, *fields = kernel_call(
        sweeps_first, (solid, target, coolant, yhi, ylo, zlo, zhi, chi, clo),
        [block, tile_shape(9), tile_shape(9), tile_shape(3), tile_shape(3)] + [ext] * 5, [ext, ext], limit=12,
    )
    y2hi, y2lo = moved(y2lo, 0, 1), moved(y2hi, 0, -1)
    z2lo, z2hi = moved(z2hi, -1, 0), moved(z2lo, 1, 0)
    clo, chi = kernel_call(pack_corners_second, (z2lo, z2hi), [pair, pair], limit=8)
    e_hi, e_lo = moved(clo, 0, 1), moved(chi, 0, -1)
    parts, wide, small = (2 * HALF, D * 4, 128), (HALF, D * 8, 128), (2, HALF * 8, 128)
    send, late, sums = kernel_call(
        sweeps_second,
        (info, solid, thermal, yhi, ylo, zlo, zhi, a, *fields, y2hi, y2lo, z2lo, z2hi, e_hi, e_lo),
        [parts, wide, small], [ext, ext, (D + 2, 8, X), (D * 8, X)], scalars=1, limit=16,
    )

    def exchanged(x):
        return lax.all_to_all(x, "blk", split_axis=0, concat_axis=0, tiled=True)

    columns = exchanged(send)
    up2, down2 = moved(late, 2, 0), moved(late, -2, 0)
    up, down = moved(sums, 1, 0), moved(sums, -1, 0)
    (columns,) = kernel_call(filter_y, (columns,), [parts], limit=8)
    early = exchanged(columns)
    (late,) = kernel_call(filter_z_late, (late, up, down, up2, down2), [parts], limit=8)
    late = exchanged(late)
    up2, down2 = moved(early, 2, 0), moved(early, -2, 0)
    (sums,) = kernel_call(layer_sums, (early,), [small], limit=8)
    up, down = moved(sums, 1, 0), moved(sums, -1, 0)
    (late,) = kernel_call(filter_y, (late,), [parts], limit=8)
    late = exchanged(late)
    (out,) = kernel_call(finish, (info, early, up, down, up2, down2, late), [block], scalars=1, limit=8)
    return out


def tile_shape(n):
    return (n, 8, X)


def solution(mesh):
    spec = P("grp", "blk", None)
    return jax.shard_map(
        local, mesh=mesh, in_specs=(spec,) * 5, out_specs=spec, check_vma=False
    )
```

```python
import jax
import jax.numpy as jnp
from jax import lax
from jax.experimental import pallas as pl
from jax.experimental.pallas import tpu as pltpu
from jax.sharding import PartitionSpec as P

RADIUS = 48
COND_FLOOR = 0.001
REPORT_SCALE = 100.0
D, S, X = 24, 8, 2048
NK = X // 128
E = D + 6
STEP = 8
HALF = NK // 2
F32 = jnp.float32
BF16 = jnp.bfloat16
MIB = 1024 * 1024


def rows_of(shape):
    return lax.broadcasted_iota(jnp.int32, shape, 0)


def rot(tile, shift):
    shift = shift % 8
    return tile if shift == 0 else pltpu.roll(tile, shift, 0)


def conduct_of(solid):
    return COND_FLOOR + (1.0 - COND_FLOOR) * (solid * solid * solid)


def pack_first(s_hbm, t_hbm, b_hbm, k_hbm, ylo_hbm, yhi_hbm, zlo_hbm, zhi_hbm,
               s_ref, b_ref, k_ref, ylo, yhi, zlo, zhi, sems, edge_sems, out_sems):
    pairs = ((s_hbm, s_ref), (b_hbm, b_ref), (k_hbm, k_ref))
    copies = [
        [
            pltpu.make_async_copy(src.at[pl.ds(i * STEP, STEP)], dst.at[pl.ds(i * STEP, STEP)], sems.at[n, i])
            for n, (src, dst) in enumerate(pairs)
        ]
        for i in range(D // STEP)
    ]
    edges = [
        pltpu.make_async_copy(t_hbm.at[0], zlo.at[7], edge_sems.at[0]),
        pltpu.make_async_copy(t_hbm.at[D - 1], zhi.at[7], edge_sems.at[1]),
    ]
    for group in copies:
        for copy in group:
            copy.start()
    for copy in edges:
        copy.start()
    r = rows_of((8, X))
    outs = []
    for i, group in enumerate(copies):
        for copy in group:
            copy.wait()

        def two(m, carry):
            ce, co = conduct_of(s_ref[2 * m]), conduct_of(s_ref[2 * m + 1])
            be, bo, ke, ko = b_ref[2 * m], b_ref[2 * m + 1], k_ref[2 * m], k_ref[2 * m + 1]
            even = jnp.where(r < 2, ce, jnp.where(r == 2, rot(be, 2), rot(ke, 3)))
            odd = jnp.where(r < 6, rot(co, 4), jnp.where(r == 6, rot(bo, 6), rot(ko, 7)))
            ylo[m] = jnp.where(r < 4, even, odd)
            even = jnp.where(r > 1, rot(ce, 4), jnp.where(r == 1, rot(be, 2), rot(ke, 1)))
            odd = jnp.where(r > 5, co, jnp.where(r == 5, rot(bo, -2), rot(ko, -3)))
            yhi[m] = jnp.where(r < 4, even, odd)
            return carry

        half = STEP // 2
        lax.fori_loop(i * half, (i + 1) * half, two, 0)
        part = pl.ds(i * half, half)
        outs += [
            pltpu.make_async_copy(ylo.at[part], ylo_hbm.at[part], out_sems.at[0, i]),
            pltpu.make_async_copy(yhi.at[part], yhi_hbm.at[part], out_sems.at[1, i]),
        ]
        outs[-2].start()
        outs[-1].start()
    for copy in edges:
        copy.wait()
    for dst, at in ((zlo, lambda j: j), (zhi, lambda j: D - 1 - j)):
        for j in range(3):
            dst[j] = conduct_of(s_ref[at(j)])
        for j in range(2):
            dst[3 + j] = b_ref[at(j)]
            dst[5 + j] = k_ref[at(j)]
    outs += [
        pltpu.make_async_copy(zlo, zlo_hbm, out_sems.at[2, 0]),
        pltpu.make_async_copy(zhi, zhi_hbm, out_sems.at[2, 1]),
    ]
    outs[-2].start()
    outs[-1].start()
    for copy in outs:
        copy.wait()


def build_own(s_ref, t_ref, b_ref, k_ref, zlo, zhi, C, B, FX, FZ, DP, mlo, mhi, hlo, hhi, RS, AS, FS, TS):
    lane = lax.broadcasted_iota(jnp.int32, (8, 128), 1)
    row = lax.broadcasted_iota(jnp.int32, (8, 128), 0)

    def own(z, carry):
        C[z + 3] = conduct_of(s_ref[z])
        B[z + 3] = b_ref[z]
        DP[z + 3] = k_ref[z]
        for k in range(NK):
            TS[k, pl.ds(pl.multiple_of(z * 8, 8), 8)] = t_ref[z, :, tile_at(k)]
        return carry

    lax.fori_loop(0, D, own, 0)
    for src, at in ((zlo, lambda j: 2 - j), (zhi, lambda j: 27 + j)):
        for j in range(3):
            C[at(j)] = src[j]
        for j in range(2):
            B[at(j)] = src[3 + j]
            DP[at(j)] = src[5 + j]
    FZ[0] = C[0] + C[1]

    def plane(p, inner):
        rots, last = {}, None
        for k in range(NK):
            sl = tile_at(k)
            c = C[p, :, sl]
            nxt = left_shift(lambda m: C[p, :, tile_at(m)], k, lane, rots)
            fx = c + nxt
            if k == NK - 1:
                nxt = jnp.where(lane == 127, 0.0, nxt)
                fx = jnp.where(lane == 127, 0.0, fx)
            back = pltpu.roll(c, 1, 1)
            before = jnp.where(lane == 0, 0.0 if last is None else last, back)
            last = back
            up = jnp.where(row == 7, 0.0, pltpu.roll(c, 7, 0))
            down = jnp.where(row == 0, 0.0, pltpu.roll(c, 1, 0))
            cz = C[p + 1, :, sl]
            FX[p, :, sl] = fx
            FZ[p, :, sl] = c + cz
            coup = DP[p, :, sl]
            diag = coup + (3.0 * c + 0.5 * (nxt + before + up + down + cz + C[p - 1, :, sl]))
            diag = jnp.where(coup > 0.0, diag, 0.0)
            DP[p, :, sl] = diag
            if inner:
                at = pl.ds(pl.multiple_of((p - 3) * 8, 8), 8)
                rd = 1.0 / diag
                RS[k, at] = (1.0 / 3.0) * rd
                AS[k, at] = B[p, :, sl] * rd
                FS[k, at] = c + up

    def inside(p, carry):
        plane(p, True)
        return carry

    def outside(i, carry):
        plane(jnp.where(i < 2, 1 + i, 25 + i), False)
        return carry

    lax.fori_loop(3, E - 3, inside, 0)
    lax.fori_loop(0, 4, outside, 0)
    r = rows_of((8, X))
    for i, src in enumerate((zlo, zhi)):
        c1, c2, b1, k1 = src[0], src[1], src[3], src[5]
        mlo[i] = jnp.where(r < 2, c1, jnp.where(r == 2, rot(c2, 2), jnp.where(r == 3, rot(b1, 3), rot(k1, 4))))
        mhi[i] = jnp.where(r > 5, c1, jnp.where(r == 5, rot(c2, -2), jnp.where(r == 4, rot(b1, -3), rot(k1, -4))))
    for g in range(D // 8):
        for k in range(NK):
            sl = tile_at(k)
            mlo[2 + g, :, sl] = AS[k, pl.ds(64 * g + 1, 8, stride=8), :]
            mhi[2 + g, :, sl] = AS[k, pl.ds(64 * g + 6, 8, stride=8), :]
            for n, (src, low, high) in enumerate(((RS, 1, 6), (FS, 1, 5), (TS, 0, 7))):
                hlo[3 * g + n, :, sl] = src[k, pl.ds(64 * g + low, 8, stride=8), :]
                hhi[3 * g + n, :, sl] = src[k, pl.ds(64 * g + high, 8, stride=8), :]


def pack_corners_second(zlo, zhi, lo, hi):
    r = rows_of((8, X))
    for i, src in enumerate((zlo, zhi)):
        lo[i] = jnp.where(r < 2, src[0], rot(src[1], 2))
        hi[i] = jnp.where(r > 5, src[0], rot(src[1], -2))


def assemble(yhi, ylo, mhi, mlo, C, B, K):
    r = rows_of((8, X))
    zero = jnp.zeros((8, X), F32)

    def two(m, carry):
        h, l = yhi[m], ylo[m]
        p = 2 * m + 3
        C[p] = jnp.where(r < 2, h, jnp.where(r > 5, rot(l, 4), 0.0))
        B[p] = jnp.where(r == 0, rot(h, -2), jnp.where(r == 7, rot(l, 6), 0.0))
        K[p] = jnp.where(r == 0, rot(h, -3), jnp.where(r == 7, rot(l, 7), 0.0))
        C[p + 1] = jnp.where(r < 2, rot(h, -4), jnp.where(r > 5, l, 0.0))
        B[p + 1] = jnp.where(r == 0, rot(h, -6), jnp.where(r == 7, rot(l, 2), 0.0))
        K[p + 1] = jnp.where(r == 0, rot(h, -7), jnp.where(r == 7, rot(l, 3), 0.0))
        return carry

    lax.fori_loop(0, D // 2, two, 0)
    for i, at in ((0, lambda j: 2 - j), (1, lambda j: 27 + j)):
        h, l = mhi[i], mlo[i]
        C[at(0)] = jnp.where(r < 2, h, jnp.where(r > 5, l, 0.0))
        C[at(1)] = jnp.where(r == 0, rot(h, -2), jnp.where(r == 7, rot(l, 2), 0.0))
        C[at(2)] = zero
        B[at(0)] = jnp.where(r == 0, rot(h, -3), jnp.where(r == 7, rot(l, 3), 0.0))
        K[at(0)] = jnp.where(r == 0, rot(h, -4), jnp.where(r == 7, rot(l, 4), 0.0))
        B[at(1)] = zero
        K[at(1)] = zero


def tile_at(k):
    return slice(128 * k, 128 * k + 128)


def left_shift(load, k, lane, rots):
    for m in (k, (k + 1) % NK):
        if m not in rots:
            rots[m] = pltpu.roll(load(m), 127, 1)
    return jnp.where(lane == 127, rots[(k + 1) % NK], rots[k])


def build(C, B, DP, A, A0, RD, FX, FY, FZ):
    lane = lax.broadcasted_iota(jnp.int32, (8, 128), 1)
    row = lax.broadcasted_iota(jnp.int32, (8, 128), 0)
    top, bottom = row == 0, row == 7

    def plane(p, carry):
        rots, last = {}, None
        for k in range(NK):
            sl = tile_at(k)
            own, c = C[0][p, :, sl], C[1][p, :, sl]
            own_up, own_down = pltpu.roll(own, 7, 0), pltpu.roll(own, 1, 0)
            up, down = pltpu.roll(c, 7, 0), pltpu.roll(c, 1, 0)
            FY[0][p, :, sl] = own + jnp.where(bottom, up, own_up)
            beside = jnp.where(bottom, up, jnp.where(top, down, 0.0))
            up, down = jnp.where(bottom, own_up, up), jnp.where(top, own_down, down)
            FY[1][p, :, sl] = c + up
            part = DP[p, :, sl]
            rd = jnp.where(part > 0.0, 1.0 / jnp.where(part > 0.0, part + 0.5 * beside, 1.0), 0.0)
            a = B[p, :, sl] * rd
            A[0][p, :, sl] = a
            A0[0][p, :, sl] = (2.0 / 3.0) * a
            RD[0][p, :, sl] = (1.0 / 3.0) * rd

            nxt = left_shift(lambda m: C[1][p, :, tile_at(m)], k, lane, rots)
            fx = c + nxt
            if k == NK - 1:
                nxt = jnp.where(lane == 127, 0.0, nxt)
                fx = jnp.where(lane == 127, 0.0, fx)
            back = pltpu.roll(c, 1, 1)
            before = jnp.where(lane == 0, 0.0 if last is None else last, back)
            last = back
            cz = C[1][p + 1, :, sl]
            FX[1][p, :, sl] = fx
            FZ[1][p, :, sl] = c + cz
            coup = RD[1][p, :, sl]
            diag = coup + (3.0 * c + 0.5 * (nxt + before + up + down + cz + C[1][p - 1, :, sl]))
            rd = jnp.where(coup > 0.0, 1.0 / jnp.where(coup > 0.0, diag, 1.0), 0.0)
            a = A[1][p, :, sl] * rd
            A[1][p, :, sl] = a
            A0[1][p, :, sl] = (2.0 / 3.0) * a
            RD[1][p, :, sl] = (1.0 / 3.0) * rd
        return carry

    lax.fori_loop(1, E - 1, plane, 0)


def unpack_third(hhi, hlo, RD, FY, RDN, FYN, TH):
    r = rows_of((8, X))

    def group(g, carry):
        for j in range(8):
            p = 3 + 8 * g + j
            RDN[p] = jnp.where(r == 1, rot(hhi[3 * g], 1 - j), jnp.where(r == 6, rot(hlo[3 * g], 6 - j), RD[p]))
            FYN[p] = jnp.where(r == 1, rot(hhi[3 * g + 1], 1 - j), jnp.where(r == 5, rot(hlo[3 * g + 1], 5 - j), FY[p]))
            TH[8 * g + j] = jnp.where(r == 7, rot(hhi[3 * g + 2], 7 - j), rot(hlo[3 * g + 2], -j))
        return carry

    lax.fori_loop(0, D // 8, group, 0)
    for p in (0, 1, 2, 27, 28, 29):
        RDN[p] = RD[p]
        FYN[p] = FY[p]


def sweep(A, OUT, A0, RD, FX, FY, FZ, both):
    lane = lax.broadcasted_iota(jnp.int32, (8, 128), 1)
    row = lax.broadcasted_iota(jnp.int32, (8, 128), 0)
    first, last, top, bottom = lane == 0, lane == 127, row == 0, row == 7

    def plane(p, halves):
        ahead, back = {}, {}

        def shift(m):
            if m in ahead:
                return
            sl = tile_at(m)
            a = [A[h][p, :, sl] for h in range(halves)]
            ahead[m] = [pltpu.roll(x, 127, 1) for x in a]
            back[m] = [pltpu.roll(FX[h][p, :, sl] * a[h], 1, 1) for h in range(halves)]

        shift(NK - 1)
        shift(0)
        for k in range(NK):
            sl = tile_at(k)
            shift((k + 1) % NK)
            a = [A[h][p, :, sl] for h in (0, 1)]
            fy = [FY[h][p, :, sl] for h in (0, 1)]
            up = [pltpu.roll(x, 7, 0) for x in a]
            down = [pltpu.roll(f * x, 1, 0) for f, x in zip(fy, a)]
            for h in range(halves):
                flux = FX[h][p, :, sl] * jnp.where(last, ahead[(k + 1) % NK][h], ahead[k][h])
                flux = flux + jnp.where(first, back[(k - 1) % NK][h], back[k][h])
                flux = flux + (fy[h] * jnp.where(bottom, up[1 - h], up[h]) + jnp.where(top, down[1 - h], down[h]))
                flux = flux + (FZ[h][p, :, sl] * A[h][p + 1, :, sl] + FZ[h][p - 1, :, sl] * A[h][p - 1, :, sl])
                OUT[h][p, :, sl] = (1.0 / 3.0) * a[h] + (A0[h][p, :, sl] + RD[h][p, :, sl] * flux)

    low, high, halves = both

    def pair(i, carry):
        plane(low + 2 * i, halves)
        plane(low + 2 * i + 1, halves)
        return carry

    lax.fori_loop(0, (high - low) // 2, pair, 0)
    if halves == 2:

        def ends(i, carry):
            plane(low - 1 + i * (high - low + 1), 1)
            return carry

        lax.fori_loop(0, 2, ends, 0)


def pieces(first, rows):
    out, done = [], 0
    while done < rows:
        n = first + done
        take = min(rows - done, 8 - n % 8)
        out.append((n // 8, n % 8, done, take))
        done += take
    return out


def sweeps_first(C0, B0, FX0, FZ0, DP, yhi, ylo, mhi, mlo,
                 a_out, y2lo, y2hi, z2lo, z2hi, FY0, RD0, R0, FX1, FY1, FZ1, RD1, R1, C1, A_0, A_1, O_0, O_1):
    FX, FY, FZ, RD, A0, A, OUT = (FX0, FX1), (FY0, FY1), (FZ0, FZ1), (RD0, RD1), (R0, R1), (A_0, A_1), (O_0, O_1)
    assemble(yhi, ylo, mhi, mlo, C1, A_1, RD1)
    build((C0, C1), B0, DP, A, A0, RD, FX, FY, FZ)
    r = rows_of((8, X))

    def second_rows(g, carry):
        for j in range(8):
            p = 3 + 8 * g + j
            a = jnp.where(r == 1, rot(mhi[2 + g], 1 - j), jnp.where(r == 6, rot(mlo[2 + g], 6 - j), A_1[p]))
            A_1[p] = a
            R1[p] = (2.0 / 3.0) * a
        return carry

    lax.fori_loop(0, D // 8, second_rows, 0)
    sweep(A, OUT, A0, RD, FX, FY, FZ, (3, E - 3, 2))
    sweep(OUT, A, A0, RD, FX, FY, FZ, (3, E - 3, 1))
    A = A_0

    def copy(z, carry):
        a_out[z] = A[z + 3]
        return carry

    lax.fori_loop(0, D, copy, 0)

    def group(g, carry):
        low, high = [None] * 3, [None] * 3
        for j in range(8):
            a = A[8 * g + j + 3]
            for tile, at, row, take in pieces(3 * j, 3):
                mask = (r >= at) & (r < at + take)
                for msg, src in ((low, row), (high, 5 + row)):
                    moved = rot(a, at - src)
                    msg[tile] = moved if msg[tile] is None else jnp.where(mask, moved, msg[tile])
        for i in range(3):
            y2lo[3 * g + i] = low[i]
            y2hi[3 * g + i] = high[i]
        return carry

    lax.fori_loop(0, 3, group, 0)
    for j in range(3):
        z2lo[j] = A[3 + j]
        z2hi[j] = A[26 - j]


def tri(u):
    m = jnp.maximum(RADIUS - u, 0)
    return m * (m + 1) // 2


def inv_cover(position, length):
    total = (RADIUS + 1) ** 2 - tri(position) - tri(length - 1 - position)
    return 1.0 / total.astype(F32)


def sweeps_second(info, s_ref, t_ref, TH, zlo, zhi, a_in, FX0, FZ0, FY0, RD0, R0, FX1, FYN, FZ1, RDN, R1,
                  y2hi, y2lo, z2lo, z2hi, e_hi, e_lo, send, late, sums, A_0, A_1, O_0, O_1, T, R):
    r = rows_of((8, X))
    zero = jnp.zeros((8, X), F32)

    def group(g, carry):
        for j in range(8):
            z = 8 * g + j
            A_0[z + 3] = a_in[z]
            side = zero
            for tile, at, row, take in pieces(3 * j, 3):
                side = jnp.where((r >= row) & (r < row + take), rot(y2hi[3 * g + tile], row - at), side)
                side = jnp.where((r >= 5 + row) & (r < 5 + row + take), rot(y2lo[3 * g + tile], 5 + row - at), side)
            A_1[z + 3] = side
        return carry

    lax.fori_loop(0, 3, group, 0)
    for i, src, at in ((0, z2lo, lambda j: 2 - j), (1, z2hi, lambda j: 27 + j)):
        h, l = e_hi[i], e_lo[i]
        for j in range(3):
            A_0[at(j)] = src[j]
        A_1[at(0)] = jnp.where(r < 2, h, jnp.where(r > 5, l, 0.0))
        A_1[at(1)] = jnp.where(r == 0, rot(h, -2), jnp.where(r == 7, rot(l, 2), 0.0))

    FX, FY, FZ, RD, A0, A, B = (FX0, FX1), (FY0, FYN), (FZ0, FZ1), (RD0, RDN), (R0, R1), (A_0, A_1), (O_0, O_1)
    sweep(A, B, A0, RD, FX, FY, FZ, (2, E - 2, 2))
    sweep(B, A, A0, RD, FX, FY, FZ, (3, E - 3, 2))

    def plane_t(z, carry):
        T[z + 1] = t_ref[z]
        return carry

    lax.fori_loop(0, D, plane_t, 0)
    T[0] = zlo[7]
    T[D + 1] = zhi[7]

    lane8 = lax.broadcasted_iota(jnp.int32, (8, 128), 1)
    row8 = lax.broadcasted_iota(jnp.int32, (8, 128), 0)
    cover_y = inv_cover(lax.axis_index("blk") * S + row8, 16 * S)
    base_z = lax.axis_index("grp") * D
    factor = -0.5 * 3.0 * (1.0 - COND_FLOOR)

    def plane_raw(z, carry):
        p = z + 3
        base = cover_y * inv_cover(base_z + z + jnp.zeros((8, 128), jnp.int32), 16 * D) * factor
        ra, rt = {}, {}
        last = None
        for k in range(NK):
            sl = tile_at(k)
            a, side, t = A_0[p, :, sl], A_1[p, :, sl], T[z + 1, :, sl]
            an = left_shift(lambda m: A_0[p, :, tile_at(m)], k, lane8, ra)
            tn = left_shift(lambda m: T[z + 1, :, tile_at(m)], k, lane8, rt)
            if k == NK - 1:
                an = jnp.where(lane8 == 127, 0.0, an)
                tn = jnp.where(lane8 == 127, 0.0, tn)
            px = (a - an) * (t - tn)
            back = pltpu.roll(px, 1, 1)
            pair = px + jnp.where(lane8 == 0, a * t if last is None else last, back)
            last = back
            edge = TH[z, :, sl]
            au, tu = jnp.where(row8 == 7, rot(side, -1), rot(a, -1)), jnp.where(row8 == 7, edge, rot(t, -1))
            ad, td = jnp.where(row8 == 0, rot(side, 1), rot(a, 1)), jnp.where(row8 == 0, edge, rot(t, 1))
            pair = pair + ((a - au) * (t - tu) + (a - ad) * (t - td))
            pair = pair + (a - A_0[p + 1, :, sl]) * (t - T[z + 2, :, sl])
            pair = pair + (a - A_0[p - 1, :, sl]) * (t - T[z, :, sl])
            s = s_ref[z, :, sl]
            switch = info[k // 2].astype(F32)
            scale = base * switch
            if k in (0, NK - 1):
                scale = scale * inv_cover(lane8 + 128 * k, X)
            else:
                scale = scale * (1.0 / float((RADIUS + 1) ** 2))
            R[pl.ds(pl.multiple_of(z * 8, 8), 8), sl] = pair * (s * s) * scale
        return carry

    lax.fori_loop(0, D, plane_raw, 0)

    i = lax.broadcasted_iota(jnp.int32, (512, 256), 0) - 128
    j = lax.broadcasted_iota(jnp.int32, (512, 256), 1)
    weights = jnp.maximum(RADIUS + 1 - jnp.abs(i - j), 0).astype(F32).astype(BF16)
    for n in range(X // 256):
        low, high = max(256 * n - 128, 0), min(256 * n + 384, X)
        x = R[:, low:high]
        w = weights[low - (256 * n - 128) : high - (256 * n - 128)]
        xh = x.astype(BF16)
        xl = (x - xh.astype(F32)).astype(BF16)
        y = jnp.dot(xh, w, preferred_element_type=F32) + jnp.dot(xl, w, preferred_element_type=F32)
        for h in range(2):
            part, m = y[:, 128 * h : 128 * h + 128], (2 * n + h) % HALF
            if n < X // 512:
                send[m] = part[0 : 4 * D]
                send[HALF + m] = part[4 * D :]
            else:
                late[m] = part
                layers = [part[8 * z : 8 * z + 8] for z in range(D)]
                sums[0, 8 * m : 8 * m + 8] = sum(layers)
                sums[1, 8 * m : 8 * m + 8] = sum(float(z) * layers[z] for z in range(1, D))


def filter_y(x_ref, out):
    i = lax.broadcasted_iota(jnp.int32, (128, 128), 0)
    j = lax.broadcasted_iota(jnp.int32, (128, 128), 1)
    w = jnp.maximum(RADIUS + 1 - jnp.abs(i - j), 0).astype(F32).astype(BF16)
    for z in range(D // 2):
        x = x_ref[:, 8 * z : 8 * z + 8, :].reshape(128, 128)
        xh = x.astype(BF16)
        xl = (x - xh.astype(F32)).astype(BF16)
        y = jnp.dot(w, xh, preferred_element_type=F32) + jnp.dot(w, xl, preferred_element_type=F32)
        out[:, 8 * z : 8 * z + 8, :] = y.reshape(16, 8, 128)


def whole_layer(ref, m, z):
    return ref[m, 8 * z : 8 * z + 8, :]


def split_layer(ref, m, z):
    return ref[HALF * (z // (D // 2)) + m, 8 * (z % (D // 2)) : 8 * (z % (D // 2)) + 8, :]


def layer_sums(x_ref, sums):
    def chunk(m, carry):
        layers = [split_layer(x_ref, m, z) for z in range(D)]
        sl = pl.ds(pl.multiple_of(m * 8, 8), 8)
        sums[0, sl] = sum(layers)
        sums[1, sl] = sum(float(z) * layers[z] for z in range(1, D))
        return carry

    lax.fori_loop(0, HALF, chunk, 0)


def filter_z(load, m, own, up, down, up2, down2, store):
    sl = pl.ds(pl.multiple_of(m * 8, 8), 8)
    u0, u1, d0, d1 = up[0, sl, :], up[1, sl, :], down[0, sl, :], down[1, sl, :]
    suffix = load(down2, m, D - 1)
    total = suffix
    far = [None] * D
    far[D - 1] = total
    for z in range(D - 2, -1, -1):
        suffix = suffix + load(down2, m, z)
        total = total + suffix
        far[z] = total
    sum_own = load(own, m, 0)
    distance = jnp.zeros_like(sum_own)
    for z in range(1, D):
        x = load(own, m, z)
        sum_own = sum_own + x
        distance = distance + float(z) * x
    near = (25.0 * (u0 + d0) + (d1 - u1)) + float(RADIUS + 1) * sum_own
    slope = u0 - d0
    prefix_own = jnp.zeros_like(sum_own)
    prefix_up = jnp.zeros_like(sum_own)
    total_up = jnp.zeros_like(sum_own)
    for z in range(D):
        prefix_up = prefix_up + load(up2, m, z)
        total_up = total_up + prefix_up
        store(z, (near - distance) + (total_up + far[z]))
        prefix_own = prefix_own + load(own, m, z)
        distance = distance + (2.0 * prefix_own - sum_own)
        near = near + slope


def filter_z_late(own, up, down, up2, down2, out):
    def chunk(m, carry):
        def store(z, value):
            out[HALF * (z // (D // 2)) + m, 8 * (z % (D // 2)) : 8 * (z % (D // 2)) + 8, :] = value

        filter_z(whole_layer, m, own, up, down, up2, down2, store)
        return carry

    lax.fori_loop(0, HALF, chunk, 0)


def finish(info, own, up, down, up2, down2, late, out):
    def chunk(m, carry):
        column = pl.ds(pl.multiple_of(m * 128, 128), 128)
        scale = REPORT_SCALE * info[m // 2].astype(F32)

        def store(z, value):
            out[z, :, column] = value * scale

        filter_z(split_layer, m, own, up, down, up2, down2, store)
        column = pl.ds(pl.multiple_of(m * 128 + X // 2, 128), 128)
        scale_late = REPORT_SCALE * info[HALF // 2 + m // 2].astype(F32)
        for z in range(D):
            out[z, :, column] = split_layer(late, m, z) * scale_late
        return carry

    lax.fori_loop(0, HALF, chunk, 0)


def kernel_call(body, ins, outs, scratch=(), scalars=0, limit=60):
    vmem = pl.BlockSpec(memory_space=pltpu.VMEM)
    smem = pl.BlockSpec(memory_space=pltpu.SMEM)
    return pl.pallas_call(
        body,
        out_shape=[jax.ShapeDtypeStruct(s, F32) for s in outs],
        in_specs=[smem] * scalars + [vmem] * (len(ins) - scalars),
        out_specs=[vmem] * len(outs),
        scratch_shapes=[pltpu.VMEM(s, F32) for s in scratch],
        compiler_params=pltpu.CompilerParams(vmem_limit_bytes=limit * MIB),
    )(*ins)


def moved(x, dz, dy):
    pairs = []
    for g in range(16):
        for b in range(16):
            if 0 <= g + dz < 16 and 0 <= b + dy < 16:
                pairs.append(((g + dz) * 16 + b + dy, g * 16 + b))
    return lax.ppermute(x, ("grp", "blk"), pairs)


def local(solid, thermal, target, coolant, switch):
    info = switch.reshape(8)
    block, pair = (D, 8, X), tile_shape(2)
    near = tile_shape(D // 2)
    ylo, yhi, zlo, zhi = pl.pallas_call(
        pack_first,
        out_shape=[jax.ShapeDtypeStruct(shape, F32) for shape in (near, near, tile_shape(8), tile_shape(8))],
        in_specs=[pl.BlockSpec(memory_space=pltpu.HBM)] * 4,
        out_specs=[pl.BlockSpec(memory_space=pltpu.HBM)] * 4,
        scratch_shapes=[pltpu.VMEM(block, F32)] * 3
        + [pltpu.VMEM(near, F32)] * 2
        + [pltpu.VMEM(tile_shape(8), F32)] * 2
        + [pltpu.SemaphoreType.DMA((3, D // STEP)), pltpu.SemaphoreType.DMA((2,)), pltpu.SemaphoreType.DMA((3, D // STEP))],
        compiler_params=pltpu.CompilerParams(vmem_limit_bytes=60 * MIB),
    )(solid, thermal, target, coolant)
    yhi, ylo = moved(ylo, 0, 1), moved(yhi, 0, -1)
    zlo, zhi = moved(zhi, -1, 0), moved(zlo, 1, 0)
    ext, flat = (E, 8, X), (D * 8, X)
    c, b, fx, fz, dp, mlo, mhi, hlo, hhi = kernel_call(
        build_own, (solid, thermal, target, coolant, zlo, zhi),
        [ext] * 5 + [tile_shape(5)] * 2 + [tile_shape(9)] * 2, [(NK, D * 8, 128)] * 4, limit=10,
    )
    mhi, mlo = moved(mlo, 0, 1), moved(mhi, 0, -1)
    hlo, hhi, mhi, mlo = lax.optimization_barrier((hlo, hhi, mhi, mlo))
    hhi, hlo = moved(hlo, 0, 1), moved(hhi, 0, -1)
    a, y2lo, y2hi, z2lo, z2hi, *fields = kernel_call(
        sweeps_first, (c, b, fx, fz, dp, yhi, ylo, mhi, mlo),
        [block, tile_shape(9), tile_shape(9), tile_shape(3), tile_shape(3)] + [ext] * 8, [ext] * 5, limit=14,
    )
    y2hi, y2lo = moved(y2lo, 0, 1), moved(y2hi, 0, -1)
    z2lo, z2hi = moved(z2hi, -1, 0), moved(z2lo, 1, 0)
    fy0, rd0, r0, fx1, fy1, fz1, rd1, r1 = fields
    rd1, fy1, th = kernel_call(unpack_third, (hhi, hlo, rd1, fy1), [ext, ext, block], limit=8)
    clo, chi = kernel_call(pack_corners_second, (z2lo, z2hi), [pair, pair], limit=8)
    e_hi, e_lo = moved(clo, 0, 1), moved(chi, 0, -1)
    parts, wide, small = (2 * HALF, D * 4, 128), (HALF, D * 8, 128), (2, HALF * 8, 128)
    send, late, sums = kernel_call(
        sweeps_second,
        (info, solid, thermal, th, zlo, zhi, a, fx, fz, fy0, rd0, r0, fx1, fy1, fz1, rd1, r1,
         y2hi, y2lo, z2lo, z2hi, e_hi, e_lo),
        [parts, wide, small], [ext] * 4 + [(D + 2, 8, X), flat], scalars=1, limit=14,
    )

    def exchanged(x):
        return lax.all_to_all(x, "blk", split_axis=0, concat_axis=0, tiled=True)

    columns = exchanged(send)
    up2, down2 = moved(late, 2, 0), moved(late, -2, 0)
    up, down = moved(sums, 1, 0), moved(sums, -1, 0)
    (columns,) = kernel_call(filter_y, (columns,), [parts], limit=8)
    early = exchanged(columns)
    (late,) = kernel_call(filter_z_late, (late, up, down, up2, down2), [parts], limit=8)
    late = exchanged(late)
    up2, down2 = moved(early, 2, 0), moved(early, -2, 0)
    (sums,) = kernel_call(layer_sums, (early,), [small], limit=8)
    up, down = moved(sums, 1, 0), moved(sums, -1, 0)
    (late,) = kernel_call(filter_y, (late,), [parts], limit=8)
    late = exchanged(late)
    (out,) = kernel_call(finish, (info, early, up, down, up2, down2, late), [block], scalars=1, limit=8)
    return out


def tile_shape(n):
    return (n, 8, X)


def solution(mesh):
    spec = P("grp", "blk", None)
    return jax.shard_map(
        local, mesh=mesh, in_specs=(spec,) * 5, out_specs=spec, check_vma=False
    )
```

```python
import jax
import jax.numpy as jnp
from jax import lax
from jax.experimental import pallas as pl
from jax.experimental.pallas import tpu as pltpu
from jax.sharding import PartitionSpec as P

RADIUS = 48
COND_FLOOR = 0.001
REPORT_SCALE = 100.0
D, S, X = 24, 8, 2048
NK = X // 128
E = D + 6
STEP = 8
HALF = NK // 2
F32 = jnp.float32
BF16 = jnp.bfloat16
MIB = 1024 * 1024


def rows_of(shape):
    return lax.broadcasted_iota(jnp.int32, shape, 0)


def rot(tile, shift):
    shift = shift % 8
    return tile if shift == 0 else pltpu.roll(tile, shift, 0)


def conduct_of(solid):
    return COND_FLOOR + (1.0 - COND_FLOOR) * (solid * solid * solid)


def pack_first(s_hbm, t_hbm, b_hbm, k_hbm, ylo_hbm, yhi_hbm, zlo_hbm, zhi_hbm,
               s_ref, b_ref, k_ref, ylo, yhi, zlo, zhi, sems, edge_sems, out_sems):
    pairs = ((s_hbm, s_ref), (b_hbm, b_ref), (k_hbm, k_ref))
    copies = [
        [
            pltpu.make_async_copy(src.at[pl.ds(i * STEP, STEP)], dst.at[pl.ds(i * STEP, STEP)], sems.at[n, i])
            for n, (src, dst) in enumerate(pairs)
        ]
        for i in range(D // STEP)
    ]
    edges = [
        pltpu.make_async_copy(t_hbm.at[0], zlo.at[7], edge_sems.at[0]),
        pltpu.make_async_copy(t_hbm.at[D - 1], zhi.at[7], edge_sems.at[1]),
    ]
    for group in copies:
        for copy in group:
            copy.start()
    for copy in edges:
        copy.start()
    r = rows_of((8, X))
    outs = []
    for i, group in enumerate(copies):
        for copy in group:
            copy.wait()

        def two(m, carry):
            ce, co = conduct_of(s_ref[2 * m]), conduct_of(s_ref[2 * m + 1])
            be, bo, ke, ko = b_ref[2 * m], b_ref[2 * m + 1], k_ref[2 * m], k_ref[2 * m + 1]
            even = jnp.where(r < 2, ce, jnp.where(r == 2, rot(be, 2), rot(ke, 3)))
            odd = jnp.where(r < 6, rot(co, 4), jnp.where(r == 6, rot(bo, 6), rot(ko, 7)))
            ylo[m] = jnp.where(r < 4, even, odd)
            even = jnp.where(r > 1, rot(ce, 4), jnp.where(r == 1, rot(be, 2), rot(ke, 1)))
            odd = jnp.where(r > 5, co, jnp.where(r == 5, rot(bo, -2), rot(ko, -3)))
            yhi[m] = jnp.where(r < 4, even, odd)
            return carry

        half = STEP // 2
        lax.fori_loop(i * half, (i + 1) * half, two, 0)
        part = pl.ds(i * half, half)
        outs += [
            pltpu.make_async_copy(ylo.at[part], ylo_hbm.at[part], out_sems.at[0, i]),
            pltpu.make_async_copy(yhi.at[part], yhi_hbm.at[part], out_sems.at[1, i]),
        ]
        outs[-2].start()
        outs[-1].start()
    for copy in edges:
        copy.wait()
    for dst, at in ((zlo, lambda j: j), (zhi, lambda j: D - 1 - j)):
        for j in range(3):
            dst[j] = conduct_of(s_ref[at(j)])
        for j in range(2):
            dst[3 + j] = b_ref[at(j)]
            dst[5 + j] = k_ref[at(j)]
    outs += [
        pltpu.make_async_copy(zlo, zlo_hbm, out_sems.at[2, 0]),
        pltpu.make_async_copy(zhi, zhi_hbm, out_sems.at[2, 1]),
    ]
    outs[-2].start()
    outs[-1].start()
    for copy in outs:
        copy.wait()


def build_own(s_ref, t_ref, b_ref, k_ref, zlo, zhi, C, B, FX, FZ, DP, mlo, mhi, hlo, hhi, RS, AS, FS, TS):
    lane = lax.broadcasted_iota(jnp.int32, (8, 128), 1)
    row = lax.broadcasted_iota(jnp.int32, (8, 128), 0)

    def own(z, carry):
        C[z + 3] = conduct_of(s_ref[z])
        B[z + 3] = b_ref[z]
        DP[z + 3] = k_ref[z]
        for k in range(NK):
            TS[k, pl.ds(pl.multiple_of(z * 8, 8), 8)] = t_ref[z, :, tile_at(k)]
        return carry

    lax.fori_loop(0, D, own, 0)
    for src, at in ((zlo, lambda j: 2 - j), (zhi, lambda j: 27 + j)):
        for j in range(3):
            C[at(j)] = src[j]
        for j in range(2):
            B[at(j)] = src[3 + j]
            DP[at(j)] = src[5 + j]
    FZ[0] = C[0] + C[1]

    def plane(p, inner):
        rots, last = {}, None
        for k in range(NK):
            sl = tile_at(k)
            c = C[p, :, sl]
            nxt = left_shift(lambda m: C[p, :, tile_at(m)], k, lane, rots)
            fx = c + nxt
            if k == NK - 1:
                nxt = jnp.where(lane == 127, 0.0, nxt)
                fx = jnp.where(lane == 127, 0.0, fx)
            back = pltpu.roll(c, 1, 1)
            before = jnp.where(lane == 0, 0.0 if last is None else last, back)
            last = back
            up = jnp.where(row == 7, 0.0, pltpu.roll(c, 7, 0))
            down = jnp.where(row == 0, 0.0, pltpu.roll(c, 1, 0))
            cz = C[p + 1, :, sl]
            FX[p, :, sl] = fx
            FZ[p, :, sl] = c + cz
            coup = DP[p, :, sl]
            diag = coup + (3.0 * c + 0.5 * (nxt + before + up + down + cz + C[p - 1, :, sl]))
            diag = jnp.where(coup > 0.0, diag, 0.0)
            DP[p, :, sl] = diag
            if inner:
                at = pl.ds(pl.multiple_of((p - 3) * 8, 8), 8)
                rd = 1.0 / diag
                RS[k, at] = (1.0 / 3.0) * rd
                AS[k, at] = B[p, :, sl] * rd
                FS[k, at] = c + up

    def inside(p, carry):
        plane(p, True)
        return carry

    def outside(i, carry):
        plane(jnp.where(i < 2, 1 + i, 25 + i), False)
        return carry

    lax.fori_loop(3, E - 3, inside, 0)
    lax.fori_loop(0, 4, outside, 0)
    r = rows_of((8, X))
    for i, src in enumerate((zlo, zhi)):
        c1, c2, b1, k1 = src[0], src[1], src[3], src[5]
        mlo[i] = jnp.where(r < 2, c1, jnp.where(r == 2, rot(c2, 2), jnp.where(r == 3, rot(b1, 3), rot(k1, 4))))
        mhi[i] = jnp.where(r > 5, c1, jnp.where(r == 5, rot(c2, -2), jnp.where(r == 4, rot(b1, -3), rot(k1, -4))))
    for g in range(D // 8):
        for k in range(NK):
            sl = tile_at(k)
            mlo[2 + g, :, sl] = AS[k, pl.ds(64 * g + 1, 8, stride=8), :]
            mhi[2 + g, :, sl] = AS[k, pl.ds(64 * g + 6, 8, stride=8), :]
            for n, (src, low, high) in enumerate(((RS, 1, 6), (FS, 1, 5), (TS, 0, 7))):
                hlo[3 * g + n, :, sl] = src[k, pl.ds(64 * g + low, 8, stride=8), :]
                hhi[3 * g + n, :, sl] = src[k, pl.ds(64 * g + high, 8, stride=8), :]


def pack_corners_second(zlo, zhi, w3lo, w3hi, lo, hi):
    r = rows_of((8, X))
    for g in range(D // 8):
        lo[2 + g] = w3lo[g]
        hi[2 + g] = w3hi[g]
    for i, src in enumerate((zlo, zhi)):
        lo[i] = jnp.where(r < 2, src[0], rot(src[1], 2))
        hi[i] = jnp.where(r > 5, src[0], rot(src[1], -2))


def assemble(yhi, ylo, mhi, mlo, C, B, K):
    r = rows_of((8, X))
    zero = jnp.zeros((8, X), F32)

    def two(m, carry):
        h, l = yhi[m], ylo[m]
        p = 2 * m + 3
        C[p] = jnp.where(r < 2, h, jnp.where(r > 5, rot(l, 4), 0.0))
        B[p] = jnp.where(r == 0, rot(h, -2), jnp.where(r == 7, rot(l, 6), 0.0))
        K[p] = jnp.where(r == 0, rot(h, -3), jnp.where(r == 7, rot(l, 7), 0.0))
        C[p + 1] = jnp.where(r < 2, rot(h, -4), jnp.where(r > 5, l, 0.0))
        B[p + 1] = jnp.where(r == 0, rot(h, -6), jnp.where(r == 7, rot(l, 2), 0.0))
        K[p + 1] = jnp.where(r == 0, rot(h, -7), jnp.where(r == 7, rot(l, 3), 0.0))
        return carry

    lax.fori_loop(0, D // 2, two, 0)
    for i, at in ((0, lambda j: 2 - j), (1, lambda j: 27 + j)):
        h, l = mhi[i], mlo[i]
        C[at(0)] = jnp.where(r < 2, h, jnp.where(r > 5, l, 0.0))
        C[at(1)] = jnp.where(r == 0, rot(h, -2), jnp.where(r == 7, rot(l, 2), 0.0))
        C[at(2)] = zero
        B[at(0)] = jnp.where(r == 0, rot(h, -3), jnp.where(r == 7, rot(l, 3), 0.0))
        K[at(0)] = jnp.where(r == 0, rot(h, -4), jnp.where(r == 7, rot(l, 4), 0.0))
        B[at(1)] = zero
        K[at(1)] = zero


def tile_at(k):
    return slice(128 * k, 128 * k + 128)


def left_shift(load, k, lane, rots):
    for m in (k, (k + 1) % NK):
        if m not in rots:
            rots[m] = pltpu.roll(load(m), 127, 1)
    return jnp.where(lane == 127, rots[(k + 1) % NK], rots[k])


def build(C, B, DP, A, A0, RD, FX, FY, FZ):
    lane = lax.broadcasted_iota(jnp.int32, (8, 128), 1)
    row = lax.broadcasted_iota(jnp.int32, (8, 128), 0)
    top, bottom = row == 0, row == 7

    def plane(p, carry):
        rots, last = {}, None
        for k in range(NK):
            sl = tile_at(k)
            own, c = C[0][p, :, sl], C[1][p, :, sl]
            own_up, own_down = pltpu.roll(own, 7, 0), pltpu.roll(own, 1, 0)
            up, down = pltpu.roll(c, 7, 0), pltpu.roll(c, 1, 0)
            FY[0][p, :, sl] = own + jnp.where(bottom, up, own_up)
            beside = jnp.where(bottom, up, jnp.where(top, down, 0.0))
            up, down = jnp.where(bottom, own_up, up), jnp.where(top, own_down, down)
            FY[1][p, :, sl] = c + up
            part = DP[p, :, sl]
            rd = jnp.where(part > 0.0, 1.0 / jnp.where(part > 0.0, part + 0.5 * beside, 1.0), 0.0)
            a = B[p, :, sl] * rd
            A[0][p, :, sl] = a
            A0[0][p, :, sl] = (2.0 / 3.0) * a
            RD[0][p, :, sl] = (1.0 / 3.0) * rd

            nxt = left_shift(lambda m: C[1][p, :, tile_at(m)], k, lane, rots)
            fx = c + nxt
            if k == NK - 1:
                nxt = jnp.where(lane == 127, 0.0, nxt)
                fx = jnp.where(lane == 127, 0.0, fx)
            back = pltpu.roll(c, 1, 1)
            before = jnp.where(lane == 0, 0.0 if last is None else last, back)
            last = back
            cz = C[1][p + 1, :, sl]
            FX[1][p, :, sl] = fx
            FZ[1][p, :, sl] = c + cz
            coup = RD[1][p, :, sl]
            diag = coup + (3.0 * c + 0.5 * (nxt + before + up + down + cz + C[1][p - 1, :, sl]))
            rd = jnp.where(coup > 0.0, 1.0 / jnp.where(coup > 0.0, diag, 1.0), 0.0)
            a = A[1][p, :, sl] * rd
            A[1][p, :, sl] = a
            A0[1][p, :, sl] = (2.0 / 3.0) * a
            RD[1][p, :, sl] = (1.0 / 3.0) * rd
        return carry

    lax.fori_loop(1, E - 1, plane, 0)


def unpack_third(hhi, hlo, RD, FY, RDN, FYN, TH):
    r = rows_of((8, X))

    def group(g, carry):
        for j in range(8):
            p = 3 + 8 * g + j
            RDN[p] = jnp.where(r == 1, rot(hhi[3 * g], 1 - j), jnp.where(r == 6, rot(hlo[3 * g], 6 - j), RD[p]))
            FYN[p] = jnp.where(r == 1, rot(hhi[3 * g + 1], 1 - j), jnp.where(r == 5, rot(hlo[3 * g + 1], 5 - j), FY[p]))
            TH[8 * g + j] = jnp.where(r == 7, rot(hhi[3 * g + 2], 7 - j), rot(hlo[3 * g + 2], -j))
        return carry

    lax.fori_loop(0, D // 8, group, 0)
    for p in (0, 1, 2, 27, 28, 29):
        RDN[p] = RD[p]
        FYN[p] = FY[p]


def sweep(A, OUT, A0, RD, FX, FY, FZ, both):
    lane = lax.broadcasted_iota(jnp.int32, (8, 128), 1)
    row = lax.broadcasted_iota(jnp.int32, (8, 128), 0)
    first, last, top, bottom = lane == 0, lane == 127, row == 0, row == 7

    def plane(p, halves):
        ahead, back = {}, {}

        def shift(m):
            if m in ahead:
                return
            sl = tile_at(m)
            a = [A[h][p, :, sl] for h in range(halves)]
            ahead[m] = [pltpu.roll(x, 127, 1) for x in a]
            back[m] = [pltpu.roll(FX[h][p, :, sl] * a[h], 1, 1) for h in range(halves)]

        shift(NK - 1)
        shift(0)
        for k in range(NK):
            sl = tile_at(k)
            shift((k + 1) % NK)
            a = [A[h][p, :, sl] for h in (0, 1)]
            fy = [FY[h][p, :, sl] for h in (0, 1)]
            up = [pltpu.roll(x, 7, 0) for x in a]
            down = [pltpu.roll(f * x, 1, 0) for f, x in zip(fy, a)]
            for h in range(halves):
                flux = FX[h][p, :, sl] * jnp.where(last, ahead[(k + 1) % NK][h], ahead[k][h])
                flux = flux + jnp.where(first, back[(k - 1) % NK][h], back[k][h])
                flux = flux + (fy[h] * jnp.where(bottom, up[1 - h], up[h]) + jnp.where(top, down[1 - h], down[h]))
                flux = flux + (FZ[h][p, :, sl] * A[h][p + 1, :, sl] + FZ[h][p - 1, :, sl] * A[h][p - 1, :, sl])
                OUT[h][p, :, sl] = (1.0 / 3.0) * a[h] + (A0[h][p, :, sl] + RD[h][p, :, sl] * flux)

    low, high, halves = both

    def pair(i, carry):
        plane(low + 2 * i, halves)
        plane(low + 2 * i + 1, halves)
        return carry

    lax.fori_loop(0, (high - low) // 2, pair, 0)
    if halves == 2:

        def ends(i, carry):
            plane(low - 1 + i * (high - low + 1), 1)
            return carry

        lax.fori_loop(0, 2, ends, 0)


def sweeps_first(C0, B0, FX0, FZ0, DP, yhi, ylo, mhi, mlo,
                 a_out, y2lo, y2hi, w3lo, w3hi, z2lo, z2hi, FY0, RD0, R0, FX1, FY1, FZ1, RD1, R1, C1, A_0, A_1, O_0, O_1):
    FX, FY, FZ, RD, A0, A, OUT = (FX0, FX1), (FY0, FY1), (FZ0, FZ1), (RD0, RD1), (R0, R1), (A_0, A_1), (O_0, O_1)
    assemble(yhi, ylo, mhi, mlo, C1, A_1, RD1)
    build((C0, C1), B0, DP, A, A0, RD, FX, FY, FZ)
    r = rows_of((8, X))

    def second_rows(g, carry):
        for j in range(8):
            p = 3 + 8 * g + j
            a = jnp.where(r == 1, rot(mhi[2 + g], 1 - j), jnp.where(r == 6, rot(mlo[2 + g], 6 - j), A_1[p]))
            A_1[p] = a
            R1[p] = (2.0 / 3.0) * a
        return carry

    lax.fori_loop(0, D // 8, second_rows, 0)
    sweep(A, OUT, A0, RD, FX, FY, FZ, (3, E - 3, 2))
    sweep(OUT, A, A0, RD, FX, FY, FZ, (3, E - 3, 1))
    A = A_0

    def copy(z, carry):
        a_out[z] = A[z + 3]
        return carry

    lax.fori_loop(0, D, copy, 0)

    def group(g, carry):
        for i in range(2):
            low, high = None, None
            for j in range(4):
                a = A[8 * g + 4 * i + j + 3]
                mask = (r >= 2 * j) & (r < 2 * j + 2)
                low = rot(a, 2 * j) if low is None else jnp.where(mask, rot(a, 2 * j), low)
                high = rot(a, 2 * j - 6) if high is None else jnp.where(mask, rot(a, 2 * j - 6), high)
            y2lo[2 * g + i] = low
            y2hi[2 * g + i] = high
        low, high = None, None
        for j in range(8):
            a = A[8 * g + j + 3]
            low = rot(a, j - 2) if low is None else jnp.where(r == j, rot(a, j - 2), low)
            high = rot(a, j - 5) if high is None else jnp.where(r == j, rot(a, j - 5), high)
        w3lo[g] = low
        w3hi[g] = high
        return carry

    lax.fori_loop(0, D // 8, group, 0)
    for j in range(3):
        z2lo[j] = A[3 + j]
        z2hi[j] = A[26 - j]


def tri(u):
    m = jnp.maximum(RADIUS - u, 0)
    return m * (m + 1) // 2


def inv_cover(position, length):
    total = (RADIUS + 1) ** 2 - tri(position) - tri(length - 1 - position)
    return 1.0 / total.astype(F32)


def sweeps_second(info, s_ref, t_ref, TH, zlo, zhi, a_in, FX0, FZ0, FY0, RD0, R0, FX1, FYN, FZ1, RDN, R1,
                  y2hi, y2lo, z2lo, z2hi, e_hi, e_lo, send, late, sums, A_0, A_1, O_0, O_1, T, R):
    r = rows_of((8, X))

    def group(g, carry):
        for j in range(8):
            z = 8 * g + j
            A_0[z + 3] = a_in[z]
            tile, at = 2 * g + j // 4, 2 * (j % 4)
            side = jnp.where(r < 2, rot(y2hi[tile], -at), jnp.where(r > 5, rot(y2lo[tile], 6 - at), 0.0))
            side = jnp.where(r == 2, rot(e_hi[2 + g], 2 - j), jnp.where(r == 5, rot(e_lo[2 + g], 5 - j), side))
            A_1[z + 3] = side
        return carry

    lax.fori_loop(0, 3, group, 0)
    for i, src, at in ((0, z2lo, lambda j: 2 - j), (1, z2hi, lambda j: 27 + j)):
        h, l = e_hi[i], e_lo[i]
        for j in range(3):
            A_0[at(j)] = src[j]
        A_1[at(0)] = jnp.where(r < 2, h, jnp.where(r > 5, l, 0.0))
        A_1[at(1)] = jnp.where(r == 0, rot(h, -2), jnp.where(r == 7, rot(l, 2), 0.0))

    FX, FY, FZ, RD, A0, A, B = (FX0, FX1), (FY0, FYN), (FZ0, FZ1), (RD0, RDN), (R0, R1), (A_0, A_1), (O_0, O_1)
    sweep(A, B, A0, RD, FX, FY, FZ, (2, E - 2, 2))
    sweep(B, A, A0, RD, FX, FY, FZ, (3, E - 3, 2))

    def plane_t(z, carry):
        T[z + 1] = t_ref[z]
        return carry

    lax.fori_loop(0, D, plane_t, 0)
    T[0] = zlo[7]
    T[D + 1] = zhi[7]

    lane8 = lax.broadcasted_iota(jnp.int32, (8, 128), 1)
    row8 = lax.broadcasted_iota(jnp.int32, (8, 128), 0)
    cover_y = inv_cover(lax.axis_index("blk") * S + row8, 16 * S)
    base_z = lax.axis_index("grp") * D
    factor = -0.5 * 3.0 * (1.0 - COND_FLOOR)

    def plane_raw(z, carry):
        p = z + 3
        base = cover_y * inv_cover(base_z + z + jnp.zeros((8, 128), jnp.int32), 16 * D) * factor
        ra, rt = {}, {}
        last = None
        for k in range(NK):
            sl = tile_at(k)
            a, side, t = A_0[p, :, sl], A_1[p, :, sl], T[z + 1, :, sl]
            an = left_shift(lambda m: A_0[p, :, tile_at(m)], k, lane8, ra)
            tn = left_shift(lambda m: T[z + 1, :, tile_at(m)], k, lane8, rt)
            if k == NK - 1:
                an = jnp.where(lane8 == 127, 0.0, an)
                tn = jnp.where(lane8 == 127, 0.0, tn)
            px = (a - an) * (t - tn)
            back = pltpu.roll(px, 1, 1)
            pair = px + jnp.where(lane8 == 0, a * t if last is None else last, back)
            last = back
            edge = TH[z, :, sl]
            au, tu = jnp.where(row8 == 7, rot(side, -1), rot(a, -1)), jnp.where(row8 == 7, edge, rot(t, -1))
            ad, td = jnp.where(row8 == 0, rot(side, 1), rot(a, 1)), jnp.where(row8 == 0, edge, rot(t, 1))
            pair = pair + ((a - au) * (t - tu) + (a - ad) * (t - td))
            pair = pair + (a - A_0[p + 1, :, sl]) * (t - T[z + 2, :, sl])
            pair = pair + (a - A_0[p - 1, :, sl]) * (t - T[z, :, sl])
            s = s_ref[z, :, sl]
            switch = info[k // 2].astype(F32)
            scale = base * switch
            if k in (0, NK - 1):
                scale = scale * inv_cover(lane8 + 128 * k, X)
            else:
                scale = scale * (1.0 / float((RADIUS + 1) ** 2))
            R[pl.ds(pl.multiple_of(z * 8, 8), 8), sl] = pair * (s * s) * scale
        return carry

    lax.fori_loop(0, D, plane_raw, 0)

    i = lax.broadcasted_iota(jnp.int32, (512, 256), 0) - 128
    j = lax.broadcasted_iota(jnp.int32, (512, 256), 1)
    weights = jnp.maximum(RADIUS + 1 - jnp.abs(i - j), 0).astype(F32).astype(BF16)
    for n in range(X // 256):
        low, high = max(256 * n - 128, 0), min(256 * n + 384, X)
        x = R[:, low:high]
        w = weights[low - (256 * n - 128) : high - (256 * n - 128)]
        xh = x.astype(BF16)
        xl = (x - xh.astype(F32)).astype(BF16)
        y = jnp.dot(xh, w, preferred_element_type=F32) + jnp.dot(xl, w, preferred_element_type=F32)
        for h in range(2):
            part, m = y[:, 128 * h : 128 * h + 128], (2 * n + h) % HALF
            if n < X // 512:
                send[m] = part[0 : 4 * D]
                send[HALF + m] = part[4 * D :]
            else:
                late[m] = part
                layers = [part[8 * z : 8 * z + 8] for z in range(D)]
                sums[0, 8 * m : 8 * m + 8] = sum(layers)
                sums[1, 8 * m : 8 * m + 8] = sum(float(z) * layers[z] for z in range(1, D))


def filter_y(x_ref, out):
    i = lax.broadcasted_iota(jnp.int32, (128, 128), 0)
    j = lax.broadcasted_iota(jnp.int32, (128, 128), 1)
    w = jnp.maximum(RADIUS + 1 - jnp.abs(i - j), 0).astype(F32).astype(BF16)
    for z in range(D // 2):
        x = x_ref[:, 8 * z : 8 * z + 8, :].reshape(128, 128)
        xh = x.astype(BF16)
        xl = (x - xh.astype(F32)).astype(BF16)
        y = jnp.dot(w, xh, preferred_element_type=F32) + jnp.dot(w, xl, preferred_element_type=F32)
        out[:, 8 * z : 8 * z + 8, :] = y.reshape(16, 8, 128)


def whole_layer(ref, m, z):
    return ref[m, 8 * z : 8 * z + 8, :]


def split_layer(ref, m, z):
    return ref[HALF * (z // (D // 2)) + m, 8 * (z % (D // 2)) : 8 * (z % (D // 2)) + 8, :]


def layer_sums(x_ref, sums):
    def chunk(m, carry):
        layers = [split_layer(x_ref, m, z) for z in range(D)]
        sl = pl.ds(pl.multiple_of(m * 8, 8), 8)
        sums[0, sl] = sum(layers)
        sums[1, sl] = sum(float(z) * layers[z] for z in range(1, D))
        return carry

    lax.fori_loop(0, HALF, chunk, 0)


def filter_z(load, m, own, up, down, up2, down2, store):
    sl = pl.ds(pl.multiple_of(m * 8, 8), 8)
    u0, u1, d0, d1 = up[0, sl, :], up[1, sl, :], down[0, sl, :], down[1, sl, :]
    suffix = load(down2, m, D - 1)
    total = suffix
    far = [None] * D
    far[D - 1] = total
    for z in range(D - 2, -1, -1):
        suffix = suffix + load(down2, m, z)
        total = total + suffix
        far[z] = total
    sum_own = load(own, m, 0)
    distance = jnp.zeros_like(sum_own)
    for z in range(1, D):
        x = load(own, m, z)
        sum_own = sum_own + x
        distance = distance + float(z) * x
    near = (25.0 * (u0 + d0) + (d1 - u1)) + float(RADIUS + 1) * sum_own
    slope = u0 - d0
    prefix_own = jnp.zeros_like(sum_own)
    prefix_up = jnp.zeros_like(sum_own)
    total_up = jnp.zeros_like(sum_own)
    for z in range(D):
        prefix_up = prefix_up + load(up2, m, z)
        total_up = total_up + prefix_up
        store(z, (near - distance) + (total_up + far[z]))
        prefix_own = prefix_own + load(own, m, z)
        distance = distance + (2.0 * prefix_own - sum_own)
        near = near + slope


def filter_z_late(own, up, down, up2, down2, out):
    def chunk(m, carry):
        def store(z, value):
            out[HALF * (z // (D // 2)) + m, 8 * (z % (D // 2)) : 8 * (z % (D // 2)) + 8, :] = value

        filter_z(whole_layer, m, own, up, down, up2, down2, store)
        return carry

    lax.fori_loop(0, HALF, chunk, 0)


def finish(info, own, up, down, up2, down2, late, out):
    def chunk(m, carry):
        column = pl.ds(pl.multiple_of(m * 128, 128), 128)
        scale = REPORT_SCALE * info[m // 2].astype(F32)

        def store(z, value):
            out[z, :, column] = value * scale

        filter_z(split_layer, m, own, up, down, up2, down2, store)
        column = pl.ds(pl.multiple_of(m * 128 + X // 2, 128), 128)
        scale_late = REPORT_SCALE * info[HALF // 2 + m // 2].astype(F32)
        for z in range(D):
            out[z, :, column] = split_layer(late, m, z) * scale_late
        return carry

    lax.fori_loop(0, HALF, chunk, 0)


def kernel_call(body, ins, outs, scratch=(), scalars=0, limit=60):
    vmem = pl.BlockSpec(memory_space=pltpu.VMEM)
    smem = pl.BlockSpec(memory_space=pltpu.SMEM)
    return pl.pallas_call(
        body,
        out_shape=[jax.ShapeDtypeStruct(s, F32) for s in outs],
        in_specs=[smem] * scalars + [vmem] * (len(ins) - scalars),
        out_specs=[vmem] * len(outs),
        scratch_shapes=[pltpu.VMEM(s, F32) for s in scratch],
        compiler_params=pltpu.CompilerParams(vmem_limit_bytes=limit * MIB),
    )(*ins)


def moved(x, dz, dy):
    pairs = []
    for g in range(16):
        for b in range(16):
            if 0 <= g + dz < 16 and 0 <= b + dy < 16:
                pairs.append(((g + dz) * 16 + b + dy, g * 16 + b))
    return lax.ppermute(x, ("grp", "blk"), pairs)


def local(solid, thermal, target, coolant, switch):
    info = switch.reshape(8)
    block = (D, 8, X)
    near = tile_shape(D // 2)
    ylo, yhi, zlo, zhi = pl.pallas_call(
        pack_first,
        out_shape=[jax.ShapeDtypeStruct(shape, F32) for shape in (near, near, tile_shape(8), tile_shape(8))],
        in_specs=[pl.BlockSpec(memory_space=pltpu.HBM)] * 4,
        out_specs=[pl.BlockSpec(memory_space=pltpu.HBM)] * 4,
        scratch_shapes=[pltpu.VMEM(block, F32)] * 3
        + [pltpu.VMEM(near, F32)] * 2
        + [pltpu.VMEM(tile_shape(8), F32)] * 2
        + [pltpu.SemaphoreType.DMA((3, D // STEP)), pltpu.SemaphoreType.DMA((2,)), pltpu.SemaphoreType.DMA((3, D // STEP))],
        compiler_params=pltpu.CompilerParams(vmem_limit_bytes=60 * MIB),
    )(solid, thermal, target, coolant)
    yhi, ylo = moved(ylo, 0, 1), moved(yhi, 0, -1)
    zlo, zhi = moved(zhi, -1, 0), moved(zlo, 1, 0)
    ext, flat = (E, 8, X), (D * 8, X)
    c, b, fx, fz, dp, mlo, mhi, hlo, hhi = kernel_call(
        build_own, (solid, thermal, target, coolant, zlo, zhi),
        [ext] * 5 + [tile_shape(5)] * 2 + [tile_shape(9)] * 2, [(NK, D * 8, 128)] * 4, limit=10,
    )
    mhi, mlo = moved(mlo, 0, 1), moved(mhi, 0, -1)
    hlo, hhi, yhi, ylo = lax.optimization_barrier((hlo, hhi, yhi, ylo))
    hhi, hlo = moved(hlo, 0, 1), moved(hhi, 0, -1)
    a, y2lo, y2hi, w3lo, w3hi, z2lo, z2hi, *fields = kernel_call(
        sweeps_first, (c, b, fx, fz, dp, yhi, ylo, mhi, mlo),
        [block, tile_shape(6), tile_shape(6)] + [tile_shape(3)] * 4 + [ext] * 8, [ext] * 5, limit=14,
    )
    y2hi, y2lo = moved(y2lo, 0, 1), moved(y2hi, 0, -1)
    z2lo, z2hi = moved(z2hi, -1, 0), moved(z2lo, 1, 0)
    fy0, rd0, r0, fx1, fy1, fz1, rd1, r1 = fields
    rd1, fy1, th = kernel_call(unpack_third, (hhi, hlo, rd1, fy1), [ext, ext, block], limit=8)
    clo, chi = kernel_call(pack_corners_second, (z2lo, z2hi, w3lo, w3hi), [tile_shape(5)] * 2, limit=8)
    e_hi, e_lo = moved(clo, 0, 1), moved(chi, 0, -1)
    parts, wide, small = (2 * HALF, D * 4, 128), (HALF, D * 8, 128), (2, HALF * 8, 128)
    send, late, sums = kernel_call(
        sweeps_second,
        (info, solid, thermal, th, zlo, zhi, a, fx, fz, fy0, rd0, r0, fx1, fy1, fz1, rd1, r1,
         y2hi, y2lo, z2lo, z2hi, e_hi, e_lo),
        [parts, wide, small], [ext] * 4 + [(D + 2, 8, X), flat], scalars=1, limit=14,
    )

    def exchanged(x):
        return lax.all_to_all(x, "blk", split_axis=0, concat_axis=0, tiled=True)

    columns = exchanged(send)
    up2, down2 = moved(late, 2, 0), moved(late, -2, 0)
    up, down = moved(sums, 1, 0), moved(sums, -1, 0)
    (columns,) = kernel_call(filter_y, (columns,), [parts], limit=8)
    early = exchanged(columns)
    (late,) = kernel_call(filter_z_late, (late, up, down, up2, down2), [parts], limit=8)
    late = exchanged(late)
    up2, down2 = moved(early, 2, 0), moved(early, -2, 0)
    (sums,) = kernel_call(layer_sums, (early,), [small], limit=8)
    up, down = moved(sums, 1, 0), moved(sums, -1, 0)
    (late,) = kernel_call(filter_y, (late,), [parts], limit=8)
    late = exchanged(late)
    (out,) = kernel_call(finish, (info, early, up, down, up2, down2, late), [block], scalars=1, limit=8)
    return out


def tile_shape(n):
    return (n, 8, X)


def solution(mesh):
    spec = P("grp", "blk", None)
    return jax.shard_map(
        local, mesh=mesh, in_specs=(spec,) * 5, out_specs=spec, check_vma=False
    )
```

```python
import jax
import jax.numpy as jnp
from jax import lax
from jax.experimental import pallas as pl
from jax.experimental.pallas import tpu as pltpu
from jax.sharding import PartitionSpec as P

RADIUS = 48
COND_FLOOR = 0.001
REPORT_SCALE = 100.0
D, S, X = 24, 8, 2048
NK = X // 128
E = D + 6
STEP = 8
HALF = NK // 2
F32 = jnp.float32
BF16 = jnp.bfloat16
MIB = 1024 * 1024


def rows_of(shape):
    return lax.broadcasted_iota(jnp.int32, shape, 0)


def rot(tile, shift):
    shift = shift % 8
    return tile if shift == 0 else pltpu.roll(tile, shift, 0)


def conduct_of(solid):
    return COND_FLOOR + (1.0 - COND_FLOOR) * (solid * solid * solid)


def pack_first(s_hbm, t_hbm, b_hbm, k_hbm, ylo_hbm, yhi_hbm, zlo_hbm, zhi_hbm,
               s_ref, b_ref, k_ref, ylo, yhi, zlo, zhi, sems, edge_sems, out_sems):
    pairs = ((s_hbm, s_ref), (b_hbm, b_ref), (k_hbm, k_ref))
    copies = [
        [
            pltpu.make_async_copy(src.at[pl.ds(i * STEP, STEP)], dst.at[pl.ds(i * STEP, STEP)], sems.at[n, i])
            for n, (src, dst) in enumerate(pairs)
        ]
        for i in range(D // STEP)
    ]
    edges = [
        pltpu.make_async_copy(t_hbm.at[0], zlo.at[7], edge_sems.at[0]),
        pltpu.make_async_copy(t_hbm.at[D - 1], zhi.at[7], edge_sems.at[1]),
    ]
    for group in copies:
        for copy in group:
            copy.start()
    for copy in edges:
        copy.start()
    r = rows_of((8, X))
    outs = []
    for i, group in enumerate(copies):
        for copy in group:
            copy.wait()

        def two(m, carry):
            ce, co = conduct_of(s_ref[2 * m]), conduct_of(s_ref[2 * m + 1])
            be, bo, ke, ko = b_ref[2 * m], b_ref[2 * m + 1], k_ref[2 * m], k_ref[2 * m + 1]
            even = jnp.where(r < 2, ce, jnp.where(r == 2, rot(be, 2), rot(ke, 3)))
            odd = jnp.where(r < 6, rot(co, 4), jnp.where(r == 6, rot(bo, 6), rot(ko, 7)))
            ylo[m] = jnp.where(r < 4, even, odd)
            even = jnp.where(r > 1, rot(ce, 4), jnp.where(r == 1, rot(be, 2), rot(ke, 1)))
            odd = jnp.where(r > 5, co, jnp.where(r == 5, rot(bo, -2), rot(ko, -3)))
            yhi[m] = jnp.where(r < 4, even, odd)
            return carry

        half = STEP // 2
        lax.fori_loop(i * half, (i + 1) * half, two, 0)
        part = pl.ds(i * half, half)
        outs += [
            pltpu.make_async_copy(ylo.at[part], ylo_hbm.at[part], out_sems.at[0, i]),
            pltpu.make_async_copy(yhi.at[part], yhi_hbm.at[part], out_sems.at[1, i]),
        ]
        outs[-2].start()
        outs[-1].start()
    for copy in edges:
        copy.wait()
    for dst, at in ((zlo, lambda j: j), (zhi, lambda j: D - 1 - j)):
        for j in range(3):
            dst[j] = conduct_of(s_ref[at(j)])
        for j in range(2):
            dst[3 + j] = b_ref[at(j)]
            dst[5 + j] = k_ref[at(j)]
    outs += [
        pltpu.make_async_copy(zlo, zlo_hbm, out_sems.at[2, 0]),
        pltpu.make_async_copy(zhi, zhi_hbm, out_sems.at[2, 1]),
    ]
    outs[-2].start()
    outs[-1].start()
    for copy in outs:
        copy.wait()


def build_own(s_ref, b_ref, k_ref, zlo, zhi, C, B, FX, FZ, DP, mlo, mhi, RS, FS, AS):
    lane = lax.broadcasted_iota(jnp.int32, (8, 128), 1)
    row = lax.broadcasted_iota(jnp.int32, (8, 128), 0)

    def own(z, carry):
        C[z + 3] = conduct_of(s_ref[z])
        B[z + 3] = b_ref[z]
        DP[z + 3] = k_ref[z]
        return carry

    lax.fori_loop(0, D, own, 0)
    for src, at in ((zlo, lambda j: 2 - j), (zhi, lambda j: 27 + j)):
        for j in range(3):
            C[at(j)] = src[j]
        for j in range(2):
            B[at(j)] = src[3 + j]
            DP[at(j)] = src[5 + j]
    FZ[0] = C[0] + C[1]

    def plane(p, inner):
        rots, last = {}, None
        for k in range(NK):
            sl = tile_at(k)
            c = C[p, :, sl]
            nxt = left_shift(lambda m: C[p, :, tile_at(m)], k, lane, rots)
            fx = c + nxt
            if k == NK - 1:
                nxt = jnp.where(lane == 127, 0.0, nxt)
                fx = jnp.where(lane == 127, 0.0, fx)
            back = pltpu.roll(c, 1, 1)
            before = jnp.where(lane == 0, 0.0 if last is None else last, back)
            last = back
            up = jnp.where(row == 7, 0.0, pltpu.roll(c, 7, 0))
            down = jnp.where(row == 0, 0.0, pltpu.roll(c, 1, 0))
            cz = C[p + 1, :, sl]
            FX[p, :, sl] = fx
            FZ[p, :, sl] = c + cz
            coup = DP[p, :, sl]
            diag = coup + (3.0 * c + 0.5 * (nxt + before + up + down + cz + C[p - 1, :, sl]))
            diag = jnp.where(coup > 0.0, diag, 0.0)
            DP[p, :, sl] = diag
            if inner:
                at = pl.ds(pl.multiple_of((p - 3) * 8, 8), 8)
                rd = 1.0 / diag
                RS[k, at] = (1.0 / 3.0) * rd
                AS[k, at] = B[p, :, sl] * rd
                FS[k, at] = c + up

    def inside(p, carry):
        plane(p, True)
        return carry

    def outside(i, carry):
        plane(jnp.where(i < 2, 1 + i, 25 + i), False)
        return carry

    lax.fori_loop(3, E - 3, inside, 0, unroll=2)
    lax.fori_loop(0, 4, outside, 0)
    r = rows_of((8, X))
    for i, src in enumerate((zlo, zhi)):
        c1, c2, b1, k1 = src[0], src[1], src[3], src[5]
        mlo[i] = jnp.where(r < 2, c1, jnp.where(r == 2, rot(c2, 2), jnp.where(r == 3, rot(b1, 3), rot(k1, 4))))
        mhi[i] = jnp.where(r > 5, c1, jnp.where(r == 5, rot(c2, -2), jnp.where(r == 4, rot(b1, -3), rot(k1, -4))))
    for g in range(D // 8):
        for k in range(NK):
            sl = tile_at(k)
            mlo[2 + g, :, sl] = AS[k, pl.ds(64 * g + 1, 8, stride=8), :]
            mhi[2 + g, :, sl] = AS[k, pl.ds(64 * g + 6, 8, stride=8), :]


def pack_third(t_ref, RS, FS, hlo, hhi):
    r = rows_of((8, X))
    for g in range(D // 8):
        for k in range(NK):
            sl = tile_at(k)
            for n, (src, low, high) in enumerate(((RS, 1, 6), (FS, 1, 5))):
                hlo[3 * g + n, :, sl] = src[k, pl.ds(64 * g + low, 8, stride=8), :]
                hhi[3 * g + n, :, sl] = src[k, pl.ds(64 * g + high, 8, stride=8), :]
        low = high = t_ref[8 * g]
        high = rot(high, 1)
        for j in range(1, 8):
            t = t_ref[8 * g + j]
            low = jnp.where(r == j, rot(t, j), low)
            high = jnp.where(r == j, rot(t, j - 7), high)
        hlo[3 * g + 2] = low
        hhi[3 * g + 2] = high


def pack_corners_second(zlo, zhi, w3lo, w3hi, lo, hi):
    r = rows_of((8, X))
    for g in range(D // 8):
        lo[2 + g] = w3lo[g]
        hi[2 + g] = w3hi[g]
    for i, src in enumerate((zlo, zhi)):
        lo[i] = jnp.where(r < 2, src[0], rot(src[1], 2))
        hi[i] = jnp.where(r > 5, src[0], rot(src[1], -2))


def assemble(yhi, ylo, mhi, mlo, C, B, K):
    r = rows_of((8, X))
    zero = jnp.zeros((8, X), F32)

    def two(m, carry):
        h, l = yhi[m], ylo[m]
        p = 2 * m + 3
        C[p] = jnp.where(r < 2, h, jnp.where(r > 5, rot(l, 4), 0.0))
        B[p] = jnp.where(r == 0, rot(h, -2), jnp.where(r == 7, rot(l, 6), 0.0))
        K[p] = jnp.where(r == 0, rot(h, -3), jnp.where(r == 7, rot(l, 7), 0.0))
        C[p + 1] = jnp.where(r < 2, rot(h, -4), jnp.where(r > 5, l, 0.0))
        B[p + 1] = jnp.where(r == 0, rot(h, -6), jnp.where(r == 7, rot(l, 2), 0.0))
        K[p + 1] = jnp.where(r == 0, rot(h, -7), jnp.where(r == 7, rot(l, 3), 0.0))
        return carry

    lax.fori_loop(0, D // 2, two, 0)
    for i, at in ((0, lambda j: 2 - j), (1, lambda j: 27 + j)):
        h, l = mhi[i], mlo[i]
        C[at(0)] = jnp.where(r < 2, h, jnp.where(r > 5, l, 0.0))
        C[at(1)] = jnp.where(r == 0, rot(h, -2), jnp.where(r == 7, rot(l, 2), 0.0))
        C[at(2)] = zero
        B[at(0)] = jnp.where(r == 0, rot(h, -3), jnp.where(r == 7, rot(l, 3), 0.0))
        K[at(0)] = jnp.where(r == 0, rot(h, -4), jnp.where(r == 7, rot(l, 4), 0.0))
        B[at(1)] = zero
        K[at(1)] = zero


def tile_at(k):
    return slice(128 * k, 128 * k + 128)


def left_shift(load, k, lane, rots):
    for m in (k, (k + 1) % NK):
        if m not in rots:
            rots[m] = pltpu.roll(load(m), 127, 1)
    return jnp.where(lane == 127, rots[(k + 1) % NK], rots[k])


def build(C, B, DP, A, A0, RD, FX, FY, FZ):
    lane = lax.broadcasted_iota(jnp.int32, (8, 128), 1)
    row = lax.broadcasted_iota(jnp.int32, (8, 128), 0)
    top, bottom = row == 0, row == 7

    def plane(p, carry):
        rots, last = {}, None
        for k in range(NK):
            sl = tile_at(k)
            own, c = C[0][p, :, sl], C[1][p, :, sl]
            own_up, own_down = pltpu.roll(own, 7, 0), pltpu.roll(own, 1, 0)
            up, down = pltpu.roll(c, 7, 0), pltpu.roll(c, 1, 0)
            FY[0][p, :, sl] = own + jnp.where(bottom, up, own_up)
            beside = jnp.where(bottom, up, jnp.where(top, down, 0.0))
            up, down = jnp.where(bottom, own_up, up), jnp.where(top, own_down, down)
            FY[1][p, :, sl] = c + up
            part = DP[p, :, sl]
            rd = jnp.where(part > 0.0, 1.0 / jnp.where(part > 0.0, part + 0.5 * beside, 1.0), 0.0)
            a = B[p, :, sl] * rd
            A[0][p, :, sl] = a
            A0[0][p, :, sl] = (2.0 / 3.0) * a
            RD[0][p, :, sl] = (1.0 / 3.0) * rd

            nxt = left_shift(lambda m: C[1][p, :, tile_at(m)], k, lane, rots)
            fx = c + nxt
            if k == NK - 1:
                nxt = jnp.where(lane == 127, 0.0, nxt)
                fx = jnp.where(lane == 127, 0.0, fx)
            back = pltpu.roll(c, 1, 1)
            before = jnp.where(lane == 0, 0.0 if last is None else last, back)
            last = back
            cz = C[1][p + 1, :, sl]
            FX[1][p, :, sl] = fx
            FZ[1][p, :, sl] = c + cz
            coup = RD[1][p, :, sl]
            diag = coup + (3.0 * c + 0.5 * (nxt + before + up + down + cz + C[1][p - 1, :, sl]))
            rd = jnp.where(coup > 0.0, 1.0 / jnp.where(coup > 0.0, diag, 1.0), 0.0)
            a = A[1][p, :, sl] * rd
            A[1][p, :, sl] = a
            A0[1][p, :, sl] = (2.0 / 3.0) * a
            RD[1][p, :, sl] = (1.0 / 3.0) * rd
        return carry

    lax.fori_loop(1, E - 1, plane, 0, unroll=2)


def unpack_third(hhi, hlo, RD, FY, RDN, FYN, TH):
    r = rows_of((8, X))

    def group(g, carry):
        for j in range(8):
            p = 3 + 8 * g + j
            RDN[p] = jnp.where(r == 1, rot(hhi[3 * g], 1 - j), jnp.where(r == 6, rot(hlo[3 * g], 6 - j), RD[p]))
            FYN[p] = jnp.where(r == 1, rot(hhi[3 * g + 1], 1 - j), jnp.where(r == 5, rot(hlo[3 * g + 1], 5 - j), FY[p]))
            TH[8 * g + j] = jnp.where(r == 7, rot(hhi[3 * g + 2], 7 - j), rot(hlo[3 * g + 2], -j))
        return carry

    lax.fori_loop(0, D // 8, group, 0)
    for p in (0, 1, 2, 27, 28, 29):
        RDN[p] = RD[p]
        FYN[p] = FY[p]


def sweep(A, OUT, A0, RD, FX, FY, FZ, both):
    lane = lax.broadcasted_iota(jnp.int32, (8, 128), 1)
    row = lax.broadcasted_iota(jnp.int32, (8, 128), 0)
    first, last, top, bottom = lane == 0, lane == 127, row == 0, row == 7

    def plane(p, halves):
        ahead, back = {}, {}

        def shift(m):
            if m in ahead:
                return
            sl = tile_at(m)
            a = [A[h][p, :, sl] for h in range(halves)]
            ahead[m] = [pltpu.roll(x, 127, 1) for x in a]
            back[m] = [pltpu.roll(FX[h][p, :, sl] * a[h], 1, 1) for h in range(halves)]

        shift(NK - 1)
        shift(0)
        for k in range(NK):
            sl = tile_at(k)
            shift((k + 1) % NK)
            a = [A[h][p, :, sl] for h in (0, 1)]
            fy = [FY[h][p, :, sl] for h in (0, 1)]
            up = [pltpu.roll(x, 7, 0) for x in a]
            down = [pltpu.roll(f * x, 1, 0) for f, x in zip(fy, a)]
            for h in range(halves):
                flux = FX[h][p, :, sl] * jnp.where(last, ahead[(k + 1) % NK][h], ahead[k][h])
                flux = flux + jnp.where(first, back[(k - 1) % NK][h], back[k][h])
                flux = flux + (fy[h] * jnp.where(bottom, up[1 - h], up[h]) + jnp.where(top, down[1 - h], down[h]))
                flux = flux + (FZ[h][p, :, sl] * A[h][p + 1, :, sl] + FZ[h][p - 1, :, sl] * A[h][p - 1, :, sl])
                OUT[h][p, :, sl] = (1.0 / 3.0) * a[h] + (A0[h][p, :, sl] + RD[h][p, :, sl] * flux)

    low, high, halves = both

    group = 4 if (high - low) % 4 == 0 else 2

    def planes(i, carry):
        for q in range(group):
            plane(low + group * i + q, halves)
        return carry

    lax.fori_loop(0, (high - low) // group, planes, 0)
    if halves == 2:

        def ends(i, carry):
            plane(low - 1 + i * (high - low + 1), 1)
            return carry

        lax.fori_loop(0, 2, ends, 0)


def sweeps_first(C0, B0, FX0, FZ0, DP, yhi, ylo, mhi, mlo,
                 a_out, y2lo, y2hi, w3lo, w3hi, z2lo, z2hi, FY0, RD0, R0, FX1, FY1, FZ1, RD1, R1, C1, A_0, A_1, O_0, O_1):
    FX, FY, FZ, RD, A0, A, OUT = (FX0, FX1), (FY0, FY1), (FZ0, FZ1), (RD0, RD1), (R0, R1), (A_0, A_1), (O_0, O_1)
    assemble(yhi, ylo, mhi, mlo, C1, A_1, RD1)
    build((C0, C1), B0, DP, A, A0, RD, FX, FY, FZ)
    r = rows_of((8, X))

    def second_rows(g, carry):
        for j in range(8):
            p = 3 + 8 * g + j
            a = jnp.where(r == 1, rot(mhi[2 + g], 1 - j), jnp.where(r == 6, rot(mlo[2 + g], 6 - j), A_1[p]))
            A_1[p] = a
            R1[p] = (2.0 / 3.0) * a
        return carry

    lax.fori_loop(0, D // 8, second_rows, 0)
    sweep(A, OUT, A0, RD, FX, FY, FZ, (3, E - 3, 2))
    sweep(OUT, A, A0, RD, FX, FY, FZ, (3, E - 3, 1))
    A = A_0

    def copy(z, carry):
        a_out[z] = A[z + 3]
        return carry

    lax.fori_loop(0, D, copy, 0)

    def group(g, carry):
        for i in range(2):
            low, high = None, None
            for j in range(4):
                a = A[8 * g + 4 * i + j + 3]
                mask = (r >= 2 * j) & (r < 2 * j + 2)
                low = rot(a, 2 * j) if low is None else jnp.where(mask, rot(a, 2 * j), low)
                high = rot(a, 2 * j - 6) if high is None else jnp.where(mask, rot(a, 2 * j - 6), high)
            y2lo[2 * g + i] = low
            y2hi[2 * g + i] = high
        low, high = None, None
        for j in range(8):
            a = A[8 * g + j + 3]
            low = rot(a, j - 2) if low is None else jnp.where(r == j, rot(a, j - 2), low)
            high = rot(a, j - 5) if high is None else jnp.where(r == j, rot(a, j - 5), high)
        w3lo[g] = low
        w3hi[g] = high
        return carry

    lax.fori_loop(0, D // 8, group, 0)
    for j in range(3):
        z2lo[j] = A[3 + j]
        z2hi[j] = A[26 - j]


def tri(u):
    m = jnp.maximum(RADIUS - u, 0)
    return m * (m + 1) // 2


def inv_cover(position, length):
    total = (RADIUS + 1) ** 2 - tri(position) - tri(length - 1 - position)
    return 1.0 / total.astype(F32)


def sweeps_second(info, s_ref, t_ref, TH, zlo, zhi, a_in, FX0, FZ0, FY0, RD0, R0, FX1, FYN, FZ1, RDN, R1,
                  y2hi, y2lo, z2lo, z2hi, e_hi, e_lo, send, late, sums, A_0, A_1, O_0, O_1, T, R):
    r = rows_of((8, X))

    def group(g, carry):
        for j in range(8):
            z = 8 * g + j
            A_0[z + 3] = a_in[z]
            tile, at = 2 * g + j // 4, 2 * (j % 4)
            side = jnp.where(r < 2, rot(y2hi[tile], -at), jnp.where(r > 5, rot(y2lo[tile], 6 - at), 0.0))
            side = jnp.where(r == 2, rot(e_hi[2 + g], 2 - j), jnp.where(r == 5, rot(e_lo[2 + g], 5 - j), side))
            A_1[z + 3] = side
        return carry

    lax.fori_loop(0, 3, group, 0)
    for i, src, at in ((0, z2lo, lambda j: 2 - j), (1, z2hi, lambda j: 27 + j)):
        h, l = e_hi[i], e_lo[i]
        for j in range(3):
            A_0[at(j)] = src[j]
        A_1[at(0)] = jnp.where(r < 2, h, jnp.where(r > 5, l, 0.0))
        A_1[at(1)] = jnp.where(r == 0, rot(h, -2), jnp.where(r == 7, rot(l, 2), 0.0))

    FX, FY, FZ, RD, A0, A, B = (FX0, FX1), (FY0, FYN), (FZ0, FZ1), (RD0, RDN), (R0, R1), (A_0, A_1), (O_0, O_1)
    sweep(A, B, A0, RD, FX, FY, FZ, (2, E - 2, 2))
    sweep(B, A, A0, RD, FX, FY, FZ, (3, E - 3, 2))

    def plane_t(z, carry):
        T[z + 1] = t_ref[z]
        return carry

    lax.fori_loop(0, D, plane_t, 0)
    T[0] = zlo[7]
    T[D + 1] = zhi[7]

    lane8 = lax.broadcasted_iota(jnp.int32, (8, 128), 1)
    row8 = lax.broadcasted_iota(jnp.int32, (8, 128), 0)
    cover_y = inv_cover(lax.axis_index("blk") * S + row8, 16 * S)
    base_z = lax.axis_index("grp") * D
    factor = -0.5 * 3.0 * (1.0 - COND_FLOOR)

    def plane_raw(z, carry):
        p = z + 3
        base = cover_y * inv_cover(base_z + z + jnp.zeros((8, 128), jnp.int32), 16 * D) * factor
        ra, rt = {}, {}
        last = None
        for k in range(NK):
            sl = tile_at(k)
            a, side, t = A_0[p, :, sl], A_1[p, :, sl], T[z + 1, :, sl]
            an = left_shift(lambda m: A_0[p, :, tile_at(m)], k, lane8, ra)
            tn = left_shift(lambda m: T[z + 1, :, tile_at(m)], k, lane8, rt)
            if k == NK - 1:
                an = jnp.where(lane8 == 127, 0.0, an)
                tn = jnp.where(lane8 == 127, 0.0, tn)
            px = (a - an) * (t - tn)
            back = pltpu.roll(px, 1, 1)
            pair = px + jnp.where(lane8 == 0, a * t if last is None else last, back)
            last = back
            edge = TH[z, :, sl]
            au, tu = jnp.where(row8 == 7, rot(side, -1), rot(a, -1)), jnp.where(row8 == 7, edge, rot(t, -1))
            ad, td = jnp.where(row8 == 0, rot(side, 1), rot(a, 1)), jnp.where(row8 == 0, edge, rot(t, 1))
            pair = pair + ((a - au) * (t - tu) + (a - ad) * (t - td))
            pair = pair + (a - A_0[p + 1, :, sl]) * (t - T[z + 2, :, sl])
            pair = pair + (a - A_0[p - 1, :, sl]) * (t - T[z, :, sl])
            s = s_ref[z, :, sl]
            switch = info[k // 2].astype(F32)
            scale = base * switch
            if k in (0, NK - 1):
                scale = scale * inv_cover(lane8 + 128 * k, X)
            else:
                scale = scale * (1.0 / float((RADIUS + 1) ** 2))
            R[pl.ds(pl.multiple_of(z * 8, 8), 8), sl] = pair * (s * s) * scale
        return carry

    lax.fori_loop(0, D, plane_raw, 0, unroll=2)

    i = lax.broadcasted_iota(jnp.int32, (512, 256), 0) - 128
    j = lax.broadcasted_iota(jnp.int32, (512, 256), 1)
    weights = jnp.maximum(RADIUS + 1 - jnp.abs(i - j), 0).astype(F32).astype(BF16)
    for n in range(X // 256):
        low, high = max(256 * n - 128, 0), min(256 * n + 384, X)
        x = R[:, low:high]
        w = weights[low - (256 * n - 128) : high - (256 * n - 128)]
        xh = x.astype(BF16)
        xl = (x - xh.astype(F32)).astype(BF16)
        y = jnp.dot(xh, w, preferred_element_type=F32) + jnp.dot(xl, w, preferred_element_type=F32)
        for h in range(2):
            part, m = y[:, 128 * h : 128 * h + 128], (2 * n + h) % HALF
            if n < X // 512:
                send[m] = part[0 : 4 * D]
                send[HALF + m] = part[4 * D :]
            else:
                late[m] = part
                layers = [part[8 * z : 8 * z + 8] for z in range(D)]
                sums[0, 8 * m : 8 * m + 8] = sum(layers)
                sums[1, 8 * m : 8 * m + 8] = sum(float(z) * layers[z] for z in range(1, D))


def filter_y(x_ref, out):
    i = lax.broadcasted_iota(jnp.int32, (128, 128), 0)
    j = lax.broadcasted_iota(jnp.int32, (128, 128), 1)
    w = jnp.maximum(RADIUS + 1 - jnp.abs(i - j), 0).astype(F32).astype(BF16)
    for z in range(D // 2):
        x = x_ref[:, 8 * z : 8 * z + 8, :].reshape(128, 128)
        xh = x.astype(BF16)
        xl = (x - xh.astype(F32)).astype(BF16)
        y = jnp.dot(w, xh, preferred_element_type=F32) + jnp.dot(w, xl, preferred_element_type=F32)
        out[:, 8 * z : 8 * z + 8, :] = y.reshape(16, 8, 128)


def whole_layer(ref, m, z):
    return ref[m, 8 * z : 8 * z + 8, :]


def split_layer(ref, m, z):
    return ref[HALF * (z // (D // 2)) + m, 8 * (z % (D // 2)) : 8 * (z % (D // 2)) + 8, :]


def layer_sums(x_ref, sums):
    def chunk(m, carry):
        layers = [split_layer(x_ref, m, z) for z in range(D)]
        sl = pl.ds(pl.multiple_of(m * 8, 8), 8)
        sums[0, sl] = sum(layers)
        sums[1, sl] = sum(float(z) * layers[z] for z in range(1, D))
        return carry

    lax.fori_loop(0, HALF, chunk, 0)


def filter_z(load, m, own, up, down, up2, down2, store):
    sl = pl.ds(pl.multiple_of(m * 8, 8), 8)
    u0, u1, d0, d1 = up[0, sl, :], up[1, sl, :], down[0, sl, :], down[1, sl, :]
    suffix = load(down2, m, D - 1)
    total = suffix
    far = [None] * D
    far[D - 1] = total
    for z in range(D - 2, -1, -1):
        suffix = suffix + load(down2, m, z)
        total = total + suffix
        far[z] = total
    sum_own = load(own, m, 0)
    distance = jnp.zeros_like(sum_own)
    for z in range(1, D):
        x = load(own, m, z)
        sum_own = sum_own + x
        distance = distance + float(z) * x
    near = (25.0 * (u0 + d0) + (d1 - u1)) + float(RADIUS + 1) * sum_own
    slope = u0 - d0
    prefix_own = jnp.zeros_like(sum_own)
    prefix_up = jnp.zeros_like(sum_own)
    total_up = jnp.zeros_like(sum_own)
    for z in range(D):
        prefix_up = prefix_up + load(up2, m, z)
        total_up = total_up + prefix_up
        store(z, (near - distance) + (total_up + far[z]))
        prefix_own = prefix_own + load(own, m, z)
        distance = distance + (2.0 * prefix_own - sum_own)
        near = near + slope


def filter_z_late(own, up, down, up2, down2, out):
    def chunk(m, carry):
        def store(z, value):
            out[HALF * (z // (D // 2)) + m, 8 * (z % (D // 2)) : 8 * (z % (D // 2)) + 8, :] = value

        filter_z(whole_layer, m, own, up, down, up2, down2, store)
        return carry

    lax.fori_loop(0, HALF, chunk, 0)


def finish(info, own, up, down, up2, down2, late, out):
    def chunk(m, carry):
        column = pl.ds(pl.multiple_of(m * 128, 128), 128)
        scale = REPORT_SCALE * info[m // 2].astype(F32)

        def store(z, value):
            out[z, :, column] = value * scale

        filter_z(split_layer, m, own, up, down, up2, down2, store)
        column = pl.ds(pl.multiple_of(m * 128 + X // 2, 128), 128)
        scale_late = REPORT_SCALE * info[HALF // 2 + m // 2].astype(F32)
        for z in range(D):
            out[z, :, column] = split_layer(late, m, z) * scale_late
        return carry

    lax.fori_loop(0, HALF, chunk, 0)


def kernel_call(body, ins, outs, scratch=(), scalars=0, limit=60):
    vmem = pl.BlockSpec(memory_space=pltpu.VMEM)
    smem = pl.BlockSpec(memory_space=pltpu.SMEM)
    return pl.pallas_call(
        body,
        out_shape=[jax.ShapeDtypeStruct(s, F32) for s in outs],
        in_specs=[smem] * scalars + [vmem] * (len(ins) - scalars),
        out_specs=[vmem] * len(outs),
        scratch_shapes=[pltpu.VMEM(s, F32) for s in scratch],
        compiler_params=pltpu.CompilerParams(vmem_limit_bytes=limit * MIB),
    )(*ins)


def moved(x, dz, dy):
    pairs = []
    for g in range(16):
        for b in range(16):
            if 0 <= g + dz < 16 and 0 <= b + dy < 16:
                pairs.append(((g + dz) * 16 + b + dy, g * 16 + b))
    return lax.ppermute(x, ("grp", "blk"), pairs)


def local(solid, thermal, target, coolant, switch):
    info = switch.reshape(8)
    block = (D, 8, X)
    near = tile_shape(D // 2)
    ylo, yhi, zlo, zhi = pl.pallas_call(
        pack_first,
        out_shape=[jax.ShapeDtypeStruct(shape, F32) for shape in (near, near, tile_shape(8), tile_shape(8))],
        in_specs=[pl.BlockSpec(memory_space=pltpu.HBM)] * 4,
        out_specs=[pl.BlockSpec(memory_space=pltpu.HBM)] * 4,
        scratch_shapes=[pltpu.VMEM(block, F32)] * 3
        + [pltpu.VMEM(near, F32)] * 2
        + [pltpu.VMEM(tile_shape(8), F32)] * 2
        + [pltpu.SemaphoreType.DMA((3, D // STEP)), pltpu.SemaphoreType.DMA((2,)), pltpu.SemaphoreType.DMA((3, D // STEP))],
        compiler_params=pltpu.CompilerParams(vmem_limit_bytes=56 * MIB),
    )(solid, thermal, target, coolant)
    yhi, ylo = moved(ylo, 0, 1), moved(yhi, 0, -1)
    zlo, zhi = moved(zhi, -1, 0), moved(zlo, 1, 0)
    ext, flat = (E, 8, X), (D * 8, X)
    rows = (NK, D * 8, 128)
    c, b, fx, fz, dp, mlo, mhi, rs, fs = kernel_call(
        build_own, (solid, target, coolant, zlo, zhi),
        [ext] * 5 + [tile_shape(5)] * 2 + [rows] * 2, [rows], limit=8,
    )
    hlo, hhi = kernel_call(pack_third, (thermal, rs, fs), [tile_shape(9)] * 2, limit=8)
    mhi, mlo = moved(mlo, 0, 1), moved(mhi, 0, -1)
    hhi, hlo = moved(hlo, 0, 1), moved(hhi, 0, -1)
    a, y2lo, y2hi, w3lo, w3hi, z2lo, z2hi, *fields = kernel_call(
        sweeps_first, (c, b, fx, fz, dp, yhi, ylo, mhi, mlo),
        [block, tile_shape(6), tile_shape(6)] + [tile_shape(3)] * 4 + [ext] * 8, [ext] * 5, limit=14,
    )
    y2hi, y2lo = moved(y2lo, 0, 1), moved(y2hi, 0, -1)
    z2lo, z2hi = moved(z2hi, -1, 0), moved(z2lo, 1, 0)
    fy0, rd0, r0, fx1, fy1, fz1, rd1, r1 = fields
    rd1, fy1, th = kernel_call(unpack_third, (hhi, hlo, rd1, fy1), [ext, ext, block], limit=8)
    clo, chi = kernel_call(pack_corners_second, (z2lo, z2hi, w3lo, w3hi), [tile_shape(5)] * 2, limit=8)
    e_hi, e_lo = moved(clo, 0, 1), moved(chi, 0, -1)
    parts, wide, small = (2 * HALF, D * 4, 128), (HALF, D * 8, 128), (2, HALF * 8, 128)
    send, late, sums = kernel_call(
        sweeps_second,
        (info, solid, thermal, th, zlo, zhi, a, fx, fz, fy0, rd0, r0, fx1, fy1, fz1, rd1, r1,
         y2hi, y2lo, z2lo, z2hi, e_hi, e_lo),
        [parts, wide, small], [ext] * 4 + [(D + 2, 8, X), flat], scalars=1, limit=14,
    )

    def exchanged(x):
        return lax.all_to_all(x, "blk", split_axis=0, concat_axis=0, tiled=True)

    columns = exchanged(send)
    up2, down2 = moved(late, 2, 0), moved(late, -2, 0)
    up, down = moved(sums, 1, 0), moved(sums, -1, 0)
    (columns,) = kernel_call(filter_y, (columns,), [parts], limit=8)
    early = exchanged(columns)
    (late,) = kernel_call(filter_z_late, (late, up, down, up2, down2), [parts], limit=8)
    late = exchanged(late)
    up2, down2 = moved(early, 2, 0), moved(early, -2, 0)
    (sums,) = kernel_call(layer_sums, (early,), [small], limit=8)
    up, down = moved(sums, 1, 0), moved(sums, -1, 0)
    (late,) = kernel_call(filter_y, (late,), [parts], limit=8)
    late = exchanged(late)
    (out,) = kernel_call(finish, (info, early, up, down, up2, down2, late), [block], scalars=1, limit=8)
    return out


def tile_shape(n):
    return (n, 8, X)


def solution(mesh):
    spec = P("grp", "blk", None)
    return jax.shard_map(
        local, mesh=mesh, in_specs=(spec,) * 5, out_specs=spec, check_vma=False
    )
```

```python
import jax
import jax.numpy as jnp
from jax import lax
from jax.experimental import pallas as pl
from jax.experimental.pallas import tpu as pltpu
from jax.sharding import PartitionSpec as P

RADIUS = 48
COND_FLOOR = 0.001
REPORT_SCALE = 100.0
D, S, X = 24, 8, 2048
NK = X // 128
E = D + 6
STEP = 8
HALF = NK // 2
F32 = jnp.float32
BF16 = jnp.bfloat16
MIB = 1024 * 1024


def rows_of(shape):
    return lax.broadcasted_iota(jnp.int32, shape, 0)


def rot(tile, shift):
    shift = shift % 8
    return tile if shift == 0 else pltpu.roll(tile, shift, 0)


def conduct_of(solid):
    return COND_FLOOR + (1.0 - COND_FLOOR) * (solid * solid * solid)


def pack_first(s_hbm, t_hbm, b_hbm, k_hbm, ylo_hbm, yhi_hbm, zlo_hbm, zhi_hbm,
               s_ref, b_ref, k_ref, ylo, yhi, zlo, zhi, sems, edge_sems, out_sems):
    pairs = ((s_hbm, s_ref), (b_hbm, b_ref), (k_hbm, k_ref))
    copies = [
        [
            pltpu.make_async_copy(src.at[pl.ds(i * STEP, STEP)], dst.at[pl.ds(i * STEP, STEP)], sems.at[n, i])
            for n, (src, dst) in enumerate(pairs)
        ]
        for i in range(D // STEP)
    ]
    edges = [
        pltpu.make_async_copy(t_hbm.at[0], zlo.at[7], edge_sems.at[0]),
        pltpu.make_async_copy(t_hbm.at[D - 1], zhi.at[7], edge_sems.at[1]),
    ]
    for group in copies:
        for copy in group:
            copy.start()
    for copy in edges:
        copy.start()
    r = rows_of((8, X))
    outs = []
    for i, group in enumerate(copies):
        for copy in group:
            copy.wait()

        def two(m, carry):
            ce, co = conduct_of(s_ref[2 * m]), conduct_of(s_ref[2 * m + 1])
            be, bo, ke, ko = b_ref[2 * m], b_ref[2 * m + 1], k_ref[2 * m], k_ref[2 * m + 1]
            even = jnp.where(r < 2, ce, jnp.where(r == 2, rot(be, 2), rot(ke, 3)))
            odd = jnp.where(r < 6, rot(co, 4), jnp.where(r == 6, rot(bo, 6), rot(ko, 7)))
            ylo[m] = jnp.where(r < 4, even, odd)
            even = jnp.where(r > 1, rot(ce, 4), jnp.where(r == 1, rot(be, 2), rot(ke, 1)))
            odd = jnp.where(r > 5, co, jnp.where(r == 5, rot(bo, -2), rot(ko, -3)))
            yhi[m] = jnp.where(r < 4, even, odd)
            return carry

        half = STEP // 2
        lax.fori_loop(i * half, (i + 1) * half, two, 0)
        part = pl.ds(i * half, half)
        outs += [
            pltpu.make_async_copy(ylo.at[part], ylo_hbm.at[part], out_sems.at[0, i]),
            pltpu.make_async_copy(yhi.at[part], yhi_hbm.at[part], out_sems.at[1, i]),
        ]
        outs[-2].start()
        outs[-1].start()
    for copy in edges:
        copy.wait()
    for dst, at in ((zlo, lambda j: j), (zhi, lambda j: D - 1 - j)):
        for j in range(3):
            dst[j] = conduct_of(s_ref[at(j)])
        for j in range(2):
            dst[3 + j] = b_ref[at(j)]
            dst[5 + j] = k_ref[at(j)]
    outs += [
        pltpu.make_async_copy(zlo, zlo_hbm, out_sems.at[2, 0]),
        pltpu.make_async_copy(zhi, zhi_hbm, out_sems.at[2, 1]),
    ]
    outs[-2].start()
    outs[-1].start()
    for copy in outs:
        copy.wait()


def build_own(s_ref, b_ref, k_ref, zlo, zhi, C, B, FX, FZ, DP, mlo, mhi, RS, FS, AS):
    lane = lax.broadcasted_iota(jnp.int32, (8, 128), 1)
    row = lax.broadcasted_iota(jnp.int32, (8, 128), 0)

    def own(z, carry):
        C[z + 3] = conduct_of(s_ref[z])
        B[z + 3] = b_ref[z]
        DP[z + 3] = k_ref[z]
        return carry

    lax.fori_loop(0, D, own, 0)
    for src, at in ((zlo, lambda j: 2 - j), (zhi, lambda j: 27 + j)):
        for j in range(3):
            C[at(j)] = src[j]
        for j in range(2):
            B[at(j)] = src[3 + j]
            DP[at(j)] = src[5 + j]
    FZ[0] = C[0] + C[1]

    def plane(p, inner):
        rots, last = {}, None
        for k in range(NK):
            sl = tile_at(k)
            c = C[p, :, sl]
            nxt = left_shift(lambda m: C[p, :, tile_at(m)], k, lane, rots)
            fx = c + nxt
            if k == NK - 1:
                nxt = jnp.where(lane == 127, 0.0, nxt)
                fx = jnp.where(lane == 127, 0.0, fx)
            back = pltpu.roll(c, 1, 1)
            before = jnp.where(lane == 0, 0.0 if last is None else last, back)
            last = back
            up = jnp.where(row == 7, 0.0, pltpu.roll(c, 7, 0))
            down = jnp.where(row == 0, 0.0, pltpu.roll(c, 1, 0))
            cz = C[p + 1, :, sl]
            FX[p, :, sl] = fx
            FZ[p, :, sl] = c + cz
            coup = DP[p, :, sl]
            diag = coup + (3.0 * c + 0.5 * (nxt + before + up + down + cz + C[p - 1, :, sl]))
            diag = jnp.where(coup > 0.0, diag, 0.0)
            DP[p, :, sl] = diag
            if inner:
                at = pl.ds(pl.multiple_of((p - 3) * 8, 8), 8)
                rd = 1.0 / diag
                RS[k, at] = (1.0 / 3.0) * rd
                AS[k, at] = B[p, :, sl] * rd
                FS[k, at] = c + up

    def inside(p, carry):
        plane(p, True)
        return carry

    def outside(i, carry):
        plane(jnp.where(i < 2, 1 + i, 25 + i), False)
        return carry

    lax.fori_loop(3, E - 3, inside, 0, unroll=2)
    lax.fori_loop(0, 4, outside, 0)
    r = rows_of((8, X))
    for i, src in enumerate((zlo, zhi)):
        c1, c2, b1, k1 = src[0], src[1], src[3], src[5]
        mlo[i] = jnp.where(r < 2, c1, jnp.where(r == 2, rot(c2, 2), jnp.where(r == 3, rot(b1, 3), rot(k1, 4))))
        mhi[i] = jnp.where(r > 5, c1, jnp.where(r == 5, rot(c2, -2), jnp.where(r == 4, rot(b1, -3), rot(k1, -4))))
    for g in range(D // 8):
        for k in range(NK):
            sl = tile_at(k)
            mlo[2 + g, :, sl] = AS[k, pl.ds(64 * g + 1, 8, stride=8), :]
            mhi[2 + g, :, sl] = AS[k, pl.ds(64 * g + 6, 8, stride=8), :]


def pack_third(t_ref, RS, FS, hlo, hhi):
    r = rows_of((8, X))
    for g in range(D // 8):
        for k in range(NK):
            sl = tile_at(k)
            for n, (src, low, high) in enumerate(((RS, 1, 6), (FS, 1, 5))):
                hlo[3 * g + n, :, sl] = src[k, pl.ds(64 * g + low, 8, stride=8), :]
                hhi[3 * g + n, :, sl] = src[k, pl.ds(64 * g + high, 8, stride=8), :]
        low = high = t_ref[8 * g]
        high = rot(high, 1)
        for j in range(1, 8):
            t = t_ref[8 * g + j]
            low = jnp.where(r == j, rot(t, j), low)
            high = jnp.where(r == j, rot(t, j - 7), high)
        hlo[3 * g + 2] = low
        hhi[3 * g + 2] = high


def pack_corners_second(zlo, zhi, w3lo, w3hi, lo, hi):
    r = rows_of((8, X))
    for g in range(D // 8):
        lo[2 + g] = w3lo[g]
        hi[2 + g] = w3hi[g]
    for i, src in enumerate((zlo, zhi)):
        lo[i] = jnp.where(r < 2, src[0], rot(src[1], 2))
        hi[i] = jnp.where(r > 5, src[0], rot(src[1], -2))


def assemble(yhi, ylo, mhi, mlo, C, B, K):
    r = rows_of((8, X))
    zero = jnp.zeros((8, X), F32)

    def two(m, carry):
        h, l = yhi[m], ylo[m]
        p = 2 * m + 3
        C[p] = jnp.where(r < 2, h, jnp.where(r > 5, rot(l, 4), 0.0))
        B[p] = jnp.where(r == 0, rot(h, -2), jnp.where(r == 7, rot(l, 6), 0.0))
        K[p] = jnp.where(r == 0, rot(h, -3), jnp.where(r == 7, rot(l, 7), 0.0))
        C[p + 1] = jnp.where(r < 2, rot(h, -4), jnp.where(r > 5, l, 0.0))
        B[p + 1] = jnp.where(r == 0, rot(h, -6), jnp.where(r == 7, rot(l, 2), 0.0))
        K[p + 1] = jnp.where(r == 0, rot(h, -7), jnp.where(r == 7, rot(l, 3), 0.0))
        return carry

    lax.fori_loop(0, D // 2, two, 0)
    for i, at in ((0, lambda j: 2 - j), (1, lambda j: 27 + j)):
        h, l = mhi[i], mlo[i]
        C[at(0)] = jnp.where(r < 2, h, jnp.where(r > 5, l, 0.0))
        C[at(1)] = jnp.where(r == 0, rot(h, -2), jnp.where(r == 7, rot(l, 2), 0.0))
        C[at(2)] = zero
        B[at(0)] = jnp.where(r == 0, rot(h, -3), jnp.where(r == 7, rot(l, 3), 0.0))
        K[at(0)] = jnp.where(r == 0, rot(h, -4), jnp.where(r == 7, rot(l, 4), 0.0))
        B[at(1)] = zero
        K[at(1)] = zero


def tile_at(k):
    return slice(128 * k, 128 * k + 128)


def left_shift(load, k, lane, rots):
    for m in (k, (k + 1) % NK):
        if m not in rots:
            rots[m] = pltpu.roll(load(m), 127, 1)
    return jnp.where(lane == 127, rots[(k + 1) % NK], rots[k])


def build(C, B, DP, A, A0, RD, FX, FY, FZ):
    lane = lax.broadcasted_iota(jnp.int32, (8, 128), 1)
    row = lax.broadcasted_iota(jnp.int32, (8, 128), 0)
    top, bottom = row == 0, row == 7

    def plane(p, carry):
        rots, last = {}, None
        for k in range(NK):
            sl = tile_at(k)
            own, c = C[0][p, :, sl], C[1][p, :, sl]
            own_up, own_down = pltpu.roll(own, 7, 0), pltpu.roll(own, 1, 0)
            up, down = pltpu.roll(c, 7, 0), pltpu.roll(c, 1, 0)
            FY[0][p, :, sl] = own + jnp.where(bottom, up, own_up)
            beside = jnp.where(bottom, up, jnp.where(top, down, 0.0))
            up, down = jnp.where(bottom, own_up, up), jnp.where(top, own_down, down)
            FY[1][p, :, sl] = c + up
            part = DP[p, :, sl]
            rd = jnp.where(part > 0.0, 1.0 / jnp.where(part > 0.0, part + 0.5 * beside, 1.0), 0.0)
            a = B[p, :, sl] * rd
            A[0][p, :, sl] = a
            A0[0][p, :, sl] = (2.0 / 3.0) * a
            RD[0][p, :, sl] = (1.0 / 3.0) * rd

            nxt = left_shift(lambda m: C[1][p, :, tile_at(m)], k, lane, rots)
            fx = c + nxt
            if k == NK - 1:
                nxt = jnp.where(lane == 127, 0.0, nxt)
                fx = jnp.where(lane == 127, 0.0, fx)
            back = pltpu.roll(c, 1, 1)
            before = jnp.where(lane == 0, 0.0 if last is None else last, back)
            last = back
            cz = C[1][p + 1, :, sl]
            FX[1][p, :, sl] = fx
            FZ[1][p, :, sl] = c + cz
            coup = RD[1][p, :, sl]
            diag = coup + (3.0 * c + 0.5 * (nxt + before + up + down + cz + C[1][p - 1, :, sl]))
            rd = jnp.where(coup > 0.0, 1.0 / jnp.where(coup > 0.0, diag, 1.0), 0.0)
            a = A[1][p, :, sl] * rd
            A[1][p, :, sl] = a
            A0[1][p, :, sl] = (2.0 / 3.0) * a
            RD[1][p, :, sl] = (1.0 / 3.0) * rd
        return carry

    lax.fori_loop(1, E - 1, plane, 0, unroll=2)


def unpack_third(hhi, hlo, RD, FY, RDN, FYN, TH):
    r = rows_of((8, X))

    def group(g, carry):
        for j in range(8):
            p = 3 + 8 * g + j
            RDN[p] = jnp.where(r == 1, rot(hhi[3 * g], 1 - j), jnp.where(r == 6, rot(hlo[3 * g], 6 - j), RD[p]))
            FYN[p] = jnp.where(r == 1, rot(hhi[3 * g + 1], 1 - j), jnp.where(r == 5, rot(hlo[3 * g + 1], 5 - j), FY[p]))
            TH[8 * g + j] = jnp.where(r == 7, rot(hhi[3 * g + 2], 7 - j), rot(hlo[3 * g + 2], -j))
        return carry

    lax.fori_loop(0, D // 8, group, 0)
    for p in (0, 1, 2, 27, 28, 29):
        RDN[p] = RD[p]
        FYN[p] = FY[p]


def sweep(A, OUT, A0, RD, FX, FY, FZ, runs):
    lane = lax.broadcasted_iota(jnp.int32, (8, 128), 1)
    row = lax.broadcasted_iota(jnp.int32, (8, 128), 0)
    first, last, top, bottom = lane == 0, lane == 127, row == 0, row == 7

    def plane(p, tiles):
        ahead, back = {}, {}

        def shift(m):
            if (m, tiles[0]) in ahead:
                return
            sl = tile_at(m)
            for h in tiles:
                a = A[h][p, :, sl]
                ahead[m, h] = pltpu.roll(a, 127, 1)
                back[m, h] = pltpu.roll(FX[h][p, :, sl] * a, 1, 1)

        shift(NK - 1)
        shift(0)
        for k in range(NK):
            sl = tile_at(k)
            shift((k + 1) % NK)
            a = [A[h][p, :, sl] for h in (0, 1)]
            fy = [FY[h][p, :, sl] for h in (0, 1)]
            up = [pltpu.roll(x, 7, 0) for x in a]
            down = [pltpu.roll(f * x, 1, 0) for f, x in zip(fy, a)]
            for h in tiles:
                flux = FX[h][p, :, sl] * jnp.where(last, ahead[(k + 1) % NK, h], ahead[k, h])
                flux = flux + jnp.where(first, back[(k - 1) % NK, h], back[k, h])
                flux = flux + (fy[h] * jnp.where(bottom, up[1 - h], up[h]) + jnp.where(top, down[1 - h], down[h]))
                flux = flux + (FZ[h][p, :, sl] * A[h][p + 1, :, sl] + FZ[h][p - 1, :, sl] * A[h][p - 1, :, sl])
                OUT[h][p, :, sl] = (1.0 / 3.0) * a[h] + (A0[h][p, :, sl] + RD[h][p, :, sl] * flux)

    for tiles, low, count in runs:
        group = 4 if count % 4 == 0 else 2

        def planes(i, carry):
            for q in range(group):
                plane(low + group * i + q, tiles)
            return carry

        if isinstance(low, int):
            lax.fori_loop(0, count // group, planes, 0)
        else:

            def single(i, carry):
                plane(low(i), tiles)
                return carry

            lax.fori_loop(0, count, single, 0)


INNER = ((0, 1), 3, D)
OWN = ((0,), 3, D)
NEXT = ((0,), lambda i: 2 + (D + 1) * i, 2)


def sweeps_first(C0, B0, FX0, FZ0, DP, yhi, ylo, mhi, mlo,
                 a_out, y2lo, y2hi, w3lo, w3hi, z2lo, z2hi, FY0, RD0, R0, FX1, FY1, FZ1, RD1, R1, C1, A_0, A_1, O_0, O_1):
    FX, FY, FZ, RD, A0, A, OUT = (FX0, FX1), (FY0, FY1), (FZ0, FZ1), (RD0, RD1), (R0, R1), (A_0, A_1), (O_0, O_1)
    assemble(yhi, ylo, mhi, mlo, C1, A_1, RD1)
    build((C0, C1), B0, DP, A, A0, RD, FX, FY, FZ)
    r = rows_of((8, X))

    def second_rows(g, carry):
        for j in range(8):
            p = 3 + 8 * g + j
            a = jnp.where(r == 1, rot(mhi[2 + g], 1 - j), jnp.where(r == 6, rot(mlo[2 + g], 6 - j), A_1[p]))
            A_1[p] = a
            R1[p] = (2.0 / 3.0) * a
        return carry

    lax.fori_loop(0, D // 8, second_rows, 0)
    sweep(A, OUT, A0, RD, FX, FY, FZ, (INNER, NEXT))
    sweep(OUT, A, A0, RD, FX, FY, FZ, (OWN,))
    A = A_0

    def copy(z, carry):
        a_out[z] = A[z + 3]
        return carry

    lax.fori_loop(0, D, copy, 0)

    def group(g, carry):
        for i in range(2):
            low, high = None, None
            for j in range(4):
                a = A[8 * g + 4 * i + j + 3]
                mask = (r >= 2 * j) & (r < 2 * j + 2)
                low = rot(a, 2 * j) if low is None else jnp.where(mask, rot(a, 2 * j), low)
                high = rot(a, 2 * j - 6) if high is None else jnp.where(mask, rot(a, 2 * j - 6), high)
            y2lo[2 * g + i] = low
            y2hi[2 * g + i] = high
        low, high = None, None
        for j in range(8):
            a = A[8 * g + j + 3]
            low = rot(a, j - 2) if low is None else jnp.where(r == j, rot(a, j - 2), low)
            high = rot(a, j - 5) if high is None else jnp.where(r == j, rot(a, j - 5), high)
        w3lo[g] = low
        w3hi[g] = high
        return carry

    lax.fori_loop(0, D // 8, group, 0)
    for j in range(3):
        z2lo[j] = A[3 + j]
        z2hi[j] = A[26 - j]


def tri(u):
    m = jnp.maximum(RADIUS - u, 0)
    return m * (m + 1) // 2


def inv_cover(position, length):
    total = (RADIUS + 1) ** 2 - tri(position) - tri(length - 1 - position)
    return 1.0 / total.astype(F32)


def third_sweep_own(info, s_ref, t_ref, zlo, zhi, a_in, FX0, FZ0, FY0, FYN, RD0, R0, y2hi, y2lo, z2lo, z2hi,
                    A_0, A_1, B_0, T, DX, SC):
    r = rows_of((8, X))

    def group(g, carry):
        for j in range(8):
            z = 8 * g + j
            A_0[z + 3] = a_in[z]
            tile, at = 2 * g + j // 4, 2 * (j % 4)
            A_1[z + 3] = jnp.where(r < 2, rot(y2hi[tile], -at), jnp.where(r > 5, rot(y2lo[tile], 6 - at), 0.0))
        return carry

    lax.fori_loop(0, 3, group, 0)
    for src, at in ((z2lo, lambda j: 2 - j), (z2hi, lambda j: 27 + j)):
        for j in range(3):
            A_0[at(j)] = src[j]
    for p in (0, 1, 2, 27, 28, 29):
        A_1[p] = jnp.zeros((8, X), F32)
    sweep((A_0, A_1), (B_0,), (R0,), (RD0,), (FX0,), (FY0, FYN), (FZ0,), (OWN,))

    lane8 = lax.broadcasted_iota(jnp.int32, (8, 128), 1)
    row8 = lax.broadcasted_iota(jnp.int32, (8, 128), 0)
    cover_y = inv_cover(lax.axis_index("blk") * S + row8, 16 * S)
    base_z = lax.axis_index("grp") * D
    factor = -0.5 * 3.0 * (1.0 - COND_FLOOR)

    def plane_t(z, carry):
        base = cover_y * inv_cover(base_z + z + jnp.zeros((8, 128), jnp.int32), 16 * D) * factor
        rt = {}
        for k in range(NK):
            sl = tile_at(k)
            t = t_ref[z, :, sl]
            tn = left_shift(lambda m: t_ref[z, :, tile_at(m)], k, lane8, rt)
            if k == NK - 1:
                tn = jnp.where(lane8 == 127, 0.0, tn)
            T[z + 1, :, sl] = t
            DX[z, :, sl] = t - tn
            s = s_ref[z, :, sl]
            scale = base * info[k // 2].astype(F32)
            if k in (0, NK - 1):
                scale = scale * inv_cover(lane8 + 128 * k, X)
            else:
                scale = scale * (1.0 / float((RADIUS + 1) ** 2))
            SC[z, :, sl] = (s * s) * scale
        return carry

    lax.fori_loop(0, D, plane_t, 0, unroll=2)

    T[0] = zlo[7]
    T[D + 1] = zhi[7]


def sweeps_second(TH, A_0, A_in, B_in, T, DX, SC, FX0, FZ0, FY0, RD0, R0, FX1, FYN, FZ1, RDN, R1,
                  e_hi, e_lo, send, late, sums, A_1, B_0, B_1, O_0, R):
    O_1 = A_1
    r = rows_of((8, X))

    def group(g, carry):
        for j in range(8):
            p = 8 * g + j + 3
            A_1[p] = jnp.where(r == 2, rot(e_hi[2 + g], 2 - j), jnp.where(r == 5, rot(e_lo[2 + g], 5 - j), A_in[p]))
            B_0[p] = B_in[p]
        return carry

    lax.fori_loop(0, 3, group, 0)
    for i, at in ((0, lambda j: 2 - j), (1, lambda j: 27 + j)):
        h, l = e_hi[i], e_lo[i]
        A_1[at(0)] = jnp.where(r < 2, h, jnp.where(r > 5, l, 0.0))
        A_1[at(1)] = jnp.where(r == 0, rot(h, -2), jnp.where(r == 7, rot(l, 2), 0.0))
    FX, FY, FZ, RD, A0 = (FX0, FX1), (FY0, FYN), (FZ0, FZ1), (RD0, RDN), (R0, R1)
    outer = ((0,), lambda i: jnp.where(i < 2, 1 + i, 25 + i), 4)
    sweep((A_0, A_1), (B_0, B_1), A0, RD, FX, FY, FZ, (((1,), 2, D + 2), outer))
    sweep((B_0, B_1), (O_0, O_1), A0, RD, FX, FY, FZ, (INNER, NEXT))

    lane8 = lax.broadcasted_iota(jnp.int32, (8, 128), 1)
    row8 = lax.broadcasted_iota(jnp.int32, (8, 128), 0)

    def plane_raw(z, carry):
        p = z + 3
        ra = {}
        last = None
        for k in range(NK):
            sl = tile_at(k)
            a, side, t, edge = O_0[p, :, sl], O_1[p, :, sl], T[z + 1, :, sl], TH[z, :, sl]
            an = left_shift(lambda m: O_0[p, :, tile_at(m)], k, lane8, ra)
            if k == NK - 1:
                an = jnp.where(lane8 == 127, 0.0, an)
            px = (a - an) * DX[z, :, sl]
            back = pltpu.roll(px, 1, 1)
            pair = px + jnp.where(lane8 == 0, a * t if last is None else last, back)
            last = back
            au = jnp.where(row8 == 7, rot(side, -1), rot(a, -1))
            ad = jnp.where(row8 == 0, rot(side, 1), rot(a, 1))
            tu, td = jnp.where(row8 == 7, edge, rot(t, -1)), jnp.where(row8 == 0, edge, rot(t, 1))
            pair = pair + ((a - au) * (t - tu) + (a - ad) * (t - td))
            pair = pair + (a - O_0[p + 1, :, sl]) * (t - T[z + 2, :, sl])
            pair = pair + (a - O_0[p - 1, :, sl]) * (t - T[z, :, sl])
            R[pl.ds(pl.multiple_of(z * 8, 8), 8), sl] = pair * SC[z, :, sl]
        return carry

    lax.fori_loop(0, D, plane_raw, 0, unroll=2)

    i = lax.broadcasted_iota(jnp.int32, (512, 256), 0) - 128
    j = lax.broadcasted_iota(jnp.int32, (512, 256), 1)
    weights = jnp.maximum(RADIUS + 1 - jnp.abs(i - j), 0).astype(F32).astype(BF16)
    for n in range(X // 256):
        low, high = max(256 * n - 128, 0), min(256 * n + 384, X)
        x = R[:, low:high]
        w = weights[low - (256 * n - 128) : high - (256 * n - 128)]
        xh = x.astype(BF16)
        xl = (x - xh.astype(F32)).astype(BF16)
        y = jnp.dot(xh, w, preferred_element_type=F32) + jnp.dot(xl, w, preferred_element_type=F32)
        for h in range(2):
            part, m = y[:, 128 * h : 128 * h + 128], (2 * n + h) % HALF
            if n < X // 512:
                send[m] = part[0 : 4 * D]
                send[HALF + m] = part[4 * D :]
            else:
                late[m] = part
                layers = [part[8 * z : 8 * z + 8] for z in range(D)]
                sums[0, 8 * m : 8 * m + 8] = sum(layers)
                sums[1, 8 * m : 8 * m + 8] = sum(float(z) * layers[z] for z in range(1, D))


def filter_y(x_ref, out):
    i = lax.broadcasted_iota(jnp.int32, (128, 128), 0)
    j = lax.broadcasted_iota(jnp.int32, (128, 128), 1)
    w = jnp.maximum(RADIUS + 1 - jnp.abs(i - j), 0).astype(F32).astype(BF16)
    for z in range(D // 2):
        x = x_ref[:, 8 * z : 8 * z + 8, :].reshape(128, 128)
        xh = x.astype(BF16)
        xl = (x - xh.astype(F32)).astype(BF16)
        y = jnp.dot(w, xh, preferred_element_type=F32) + jnp.dot(w, xl, preferred_element_type=F32)
        out[:, 8 * z : 8 * z + 8, :] = y.reshape(16, 8, 128)


def whole_layer(ref, m, z):
    return ref[m, 8 * z : 8 * z + 8, :]


def split_layer(ref, m, z):
    return ref[HALF * (z // (D // 2)) + m, 8 * (z % (D // 2)) : 8 * (z % (D // 2)) + 8, :]


def layer_sums(x_ref, sums):
    def chunk(m, carry):
        layers = [split_layer(x_ref, m, z) for z in range(D)]
        sl = pl.ds(pl.multiple_of(m * 8, 8), 8)
        sums[0, sl] = sum(layers)
        sums[1, sl] = sum(float(z) * layers[z] for z in range(1, D))
        return carry

    lax.fori_loop(0, HALF, chunk, 0)


def filter_z(load, m, own, up, down, up2, down2, store):
    sl = pl.ds(pl.multiple_of(m * 8, 8), 8)
    u0, u1, d0, d1 = up[0, sl, :], up[1, sl, :], down[0, sl, :], down[1, sl, :]
    suffix = load(down2, m, D - 1)
    total = suffix
    far = [None] * D
    far[D - 1] = total
    for z in range(D - 2, -1, -1):
        suffix = suffix + load(down2, m, z)
        total = total + suffix
        far[z] = total
    sum_own = load(own, m, 0)
    distance = jnp.zeros_like(sum_own)
    for z in range(1, D):
        x = load(own, m, z)
        sum_own = sum_own + x
        distance = distance + float(z) * x
    near = (25.0 * (u0 + d0) + (d1 - u1)) + float(RADIUS + 1) * sum_own
    slope = u0 - d0
    prefix_own = jnp.zeros_like(sum_own)
    prefix_up = jnp.zeros_like(sum_own)
    total_up = jnp.zeros_like(sum_own)
    for z in range(D):
        prefix_up = prefix_up + load(up2, m, z)
        total_up = total_up + prefix_up
        store(z, (near - distance) + (total_up + far[z]))
        prefix_own = prefix_own + load(own, m, z)
        distance = distance + (2.0 * prefix_own - sum_own)
        near = near + slope


def filter_z_late(own, up, down, up2, down2, out):
    def chunk(m, carry):
        def store(z, value):
            out[HALF * (z // (D // 2)) + m, 8 * (z % (D // 2)) : 8 * (z % (D // 2)) + 8, :] = value

        filter_z(whole_layer, m, own, up, down, up2, down2, store)
        return carry

    lax.fori_loop(0, HALF, chunk, 0)


def finish(info, own, up, down, up2, down2, late, out):
    def chunk(m, carry):
        column = pl.ds(pl.multiple_of(m * 128, 128), 128)
        scale = REPORT_SCALE * info[m // 2].astype(F32)

        def store(z, value):
            out[z, :, column] = value * scale

        filter_z(split_layer, m, own, up, down, up2, down2, store)
        column = pl.ds(pl.multiple_of(m * 128 + X // 2, 128), 128)
        scale_late = REPORT_SCALE * info[HALF // 2 + m // 2].astype(F32)
        for z in range(D):
            out[z, :, column] = split_layer(late, m, z) * scale_late
        return carry

    lax.fori_loop(0, HALF, chunk, 0)


def kernel_call(body, ins, outs, scratch=(), scalars=0, limit=60):
    vmem = pl.BlockSpec(memory_space=pltpu.VMEM)
    smem = pl.BlockSpec(memory_space=pltpu.SMEM)
    return pl.pallas_call(
        body,
        out_shape=[jax.ShapeDtypeStruct(s, F32) for s in outs],
        in_specs=[smem] * scalars + [vmem] * (len(ins) - scalars),
        out_specs=[vmem] * len(outs),
        scratch_shapes=[pltpu.VMEM(s, F32) for s in scratch],
        compiler_params=pltpu.CompilerParams(vmem_limit_bytes=limit * MIB),
    )(*ins)


def moved(x, dz, dy):
    pairs = []
    for g in range(16):
        for b in range(16):
            if 0 <= g + dz < 16 and 0 <= b + dy < 16:
                pairs.append(((g + dz) * 16 + b + dy, g * 16 + b))
    return lax.ppermute(x, ("grp", "blk"), pairs)


def local(solid, thermal, target, coolant, switch):
    info = switch.reshape(8)
    block = (D, 8, X)
    near = tile_shape(D // 2)
    ylo, yhi, zlo, zhi = pl.pallas_call(
        pack_first,
        out_shape=[jax.ShapeDtypeStruct(shape, F32) for shape in (near, near, tile_shape(8), tile_shape(8))],
        in_specs=[pl.BlockSpec(memory_space=pltpu.HBM)] * 4,
        out_specs=[pl.BlockSpec(memory_space=pltpu.HBM)] * 4,
        scratch_shapes=[pltpu.VMEM(block, F32)] * 3
        + [pltpu.VMEM(near, F32)] * 2
        + [pltpu.VMEM(tile_shape(8), F32)] * 2
        + [pltpu.SemaphoreType.DMA((3, D // STEP)), pltpu.SemaphoreType.DMA((2,)), pltpu.SemaphoreType.DMA((3, D // STEP))],
        compiler_params=pltpu.CompilerParams(vmem_limit_bytes=56 * MIB),
    )(solid, thermal, target, coolant)
    yhi, ylo = moved(ylo, 0, 1), moved(yhi, 0, -1)
    zlo, zhi = moved(zhi, -1, 0), moved(zlo, 1, 0)
    ext, flat = (E, 8, X), (D * 8, X)
    rows = (NK, D * 8, 128)
    c, b, fx, fz, dp, mlo, mhi, rs, fs = kernel_call(
        build_own, (solid, target, coolant, zlo, zhi),
        [ext] * 5 + [tile_shape(5)] * 2 + [rows] * 2, [rows], limit=8,
    )
    hlo, hhi = kernel_call(pack_third, (thermal, rs, fs), [tile_shape(9)] * 2, limit=8)
    mhi, mlo = moved(mlo, 0, 1), moved(mhi, 0, -1)
    hhi, hlo = moved(hlo, 0, 1), moved(hhi, 0, -1)
    a, y2lo, y2hi, w3lo, w3hi, z2lo, z2hi, *fields = kernel_call(
        sweeps_first, (c, b, fx, fz, dp, yhi, ylo, mhi, mlo),
        [block, tile_shape(6), tile_shape(6)] + [tile_shape(3)] * 4 + [ext] * 8, [ext] * 5, limit=14,
    )
    y2hi, y2lo = moved(y2lo, 0, 1), moved(y2hi, 0, -1)
    z2lo, z2hi = moved(z2hi, -1, 0), moved(z2lo, 1, 0)
    fy0, rd0, r0, fx1, fy1, fz1, rd1, r1 = fields
    rd1, fy1, th = kernel_call(unpack_third, (hhi, hlo, rd1, fy1), [ext, ext, block], limit=8)
    clo, chi = kernel_call(pack_corners_second, (z2lo, z2hi, w3lo, w3hi), [tile_shape(5)] * 2, limit=8)
    e_hi, e_lo = moved(clo, 0, 1), moved(chi, 0, -1)
    parts, wide, small = (2 * HALF, D * 4, 128), (HALF, D * 8, 128), (2, HALF * 8, 128)
    a_0, a_1, b_0, *terms = kernel_call(
        third_sweep_own,
        (info, solid, thermal, zlo, zhi, a, fx, fz, fy0, fy1, rd0, r0, y2hi, y2lo, z2lo, z2hi),
        [ext] * 3 + [(D + 2, 8, X), block, block], scalars=1, limit=8,
    )
    send, late, sums = kernel_call(
        sweeps_second,
        (th, a_0, a_1, b_0, *terms, fx, fz, fy0, rd0, r0, fx1, fy1, fz1, rd1, r1, e_hi, e_lo),
        [parts, wide, small], [ext] * 4 + [flat], limit=13,
    )

    def exchanged(x):
        return lax.all_to_all(x, "blk", split_axis=0, concat_axis=0, tiled=True)

    columns = exchanged(send)
    up2, down2 = moved(late, 2, 0), moved(late, -2, 0)
    up, down = moved(sums, 1, 0), moved(sums, -1, 0)
    (columns,) = kernel_call(filter_y, (columns,), [parts], limit=8)
    early = exchanged(columns)
    (late,) = kernel_call(filter_z_late, (late, up, down, up2, down2), [parts], limit=8)
    late = exchanged(late)
    up2, down2 = moved(early, 2, 0), moved(early, -2, 0)
    (sums,) = kernel_call(layer_sums, (early,), [small], limit=8)
    up, down = moved(sums, 1, 0), moved(sums, -1, 0)
    (late,) = kernel_call(filter_y, (late,), [parts], limit=8)
    late = exchanged(late)
    (out,) = kernel_call(finish, (info, early, up, down, up2, down2, late), [block], scalars=1, limit=8)
    return out


def tile_shape(n):
    return (n, 8, X)


def solution(mesh):
    spec = P("grp", "blk", None)
    return jax.shard_map(
        local, mesh=mesh, in_specs=(spec,) * 5, out_specs=spec, check_vma=False
    )
```

```python
import jax
import jax.numpy as jnp
from jax import lax
from jax.experimental import pallas as pl
from jax.experimental.pallas import tpu as pltpu
from jax.sharding import PartitionSpec as P

RADIUS = 48
COND_FLOOR = 0.001
REPORT_SCALE = 100.0
D, S, X = 24, 8, 2048
NK = X // 128
E = D + 6
STEP = 8
HALF = NK // 2
F32 = jnp.float32
BF16 = jnp.bfloat16
MIB = 1024 * 1024


def rows_of(shape):
    return lax.broadcasted_iota(jnp.int32, shape, 0)


def rot(tile, shift):
    shift = shift % 8
    return tile if shift == 0 else pltpu.roll(tile, shift, 0)


def conduct_of(solid):
    return COND_FLOOR + (1.0 - COND_FLOOR) * (solid * solid * solid)


def pack_first(s_hbm, t_hbm, b_hbm, k_hbm, ylo_hbm, yhi_hbm, zlo_hbm, zhi_hbm,
               s_ref, b_ref, k_ref, ylo, yhi, zlo, zhi, sems, edge_sems, out_sems):
    pairs = ((s_hbm, s_ref), (b_hbm, b_ref), (k_hbm, k_ref))
    copies = [
        [
            pltpu.make_async_copy(src.at[pl.ds(i * STEP, STEP)], dst.at[pl.ds(i * STEP, STEP)], sems.at[n, i])
            for n, (src, dst) in enumerate(pairs)
        ]
        for i in range(D // STEP)
    ]
    edges = [
        pltpu.make_async_copy(t_hbm.at[0], zlo.at[7], edge_sems.at[0]),
        pltpu.make_async_copy(t_hbm.at[D - 1], zhi.at[7], edge_sems.at[1]),
    ]
    for group in copies:
        for copy in group:
            copy.start()
    for copy in edges:
        copy.start()
    r = rows_of((8, X))
    outs = []
    for i, group in enumerate(copies):
        for copy in group:
            copy.wait()

        def two(m, carry):
            ce, co = conduct_of(s_ref[2 * m]), conduct_of(s_ref[2 * m + 1])
            be, bo, ke, ko = b_ref[2 * m], b_ref[2 * m + 1], k_ref[2 * m], k_ref[2 * m + 1]
            even = jnp.where(r < 2, ce, jnp.where(r == 2, rot(be, 2), rot(ke, 3)))
            odd = jnp.where(r < 6, rot(co, 4), jnp.where(r == 6, rot(bo, 6), rot(ko, 7)))
            ylo[m] = jnp.where(r < 4, even, odd)
            even = jnp.where(r > 1, rot(ce, 4), jnp.where(r == 1, rot(be, 2), rot(ke, 1)))
            odd = jnp.where(r > 5, co, jnp.where(r == 5, rot(bo, -2), rot(ko, -3)))
            yhi[m] = jnp.where(r < 4, even, odd)
            return carry

        half = STEP // 2
        lax.fori_loop(i * half, (i + 1) * half, two, 0)
        part = pl.ds(i * half, half)
        outs += [
            pltpu.make_async_copy(ylo.at[part], ylo_hbm.at[part], out_sems.at[0, i]),
            pltpu.make_async_copy(yhi.at[part], yhi_hbm.at[part], out_sems.at[1, i]),
        ]
        outs[-2].start()
        outs[-1].start()
    for copy in edges:
        copy.wait()
    for dst, at in ((zlo, lambda j: j), (zhi, lambda j: D - 1 - j)):
        for j in range(3):
            dst[j] = conduct_of(s_ref[at(j)])
        for j in range(2):
            dst[3 + j] = b_ref[at(j)]
            dst[5 + j] = k_ref[at(j)]
    outs += [
        pltpu.make_async_copy(zlo, zlo_hbm, out_sems.at[2, 0]),
        pltpu.make_async_copy(zhi, zhi_hbm, out_sems.at[2, 1]),
    ]
    outs[-2].start()
    outs[-1].start()
    for copy in outs:
        copy.wait()


def build_own(s_ref, b_ref, k_ref, zlo, zhi, C, B, FX, FZ, DP, mlo, mhi, RS, FS, AS):
    lane = lax.broadcasted_iota(jnp.int32, (8, 128), 1)
    row = lax.broadcasted_iota(jnp.int32, (8, 128), 0)

    def own(z, carry):
        C[z + 3] = conduct_of(s_ref[z])
        B[z + 3] = b_ref[z]
        DP[z + 3] = k_ref[z]
        return carry

    lax.fori_loop(0, D, own, 0)
    for src, at in ((zlo, lambda j: 2 - j), (zhi, lambda j: 27 + j)):
        for j in range(3):
            C[at(j)] = src[j]
        for j in range(2):
            B[at(j)] = src[3 + j]
            DP[at(j)] = src[5 + j]
    FZ[0] = C[0] + C[1]

    def plane(p, inner):
        rots, last = {}, None
        for k in range(NK):
            sl = tile_at(k)
            c = C[p, :, sl]
            nxt = left_shift(lambda m: C[p, :, tile_at(m)], k, lane, rots)
            fx = c + nxt
            if k == NK - 1:
                nxt = jnp.where(lane == 127, 0.0, nxt)
                fx = jnp.where(lane == 127, 0.0, fx)
            back = pltpu.roll(c, 1, 1)
            before = jnp.where(lane == 0, 0.0 if last is None else last, back)
            last = back
            up = jnp.where(row == 7, 0.0, pltpu.roll(c, 7, 0))
            down = jnp.where(row == 0, 0.0, pltpu.roll(c, 1, 0))
            cz = C[p + 1, :, sl]
            FX[p, :, sl] = fx
            FZ[p, :, sl] = c + cz
            coup = DP[p, :, sl]
            diag = coup + (3.0 * c + 0.5 * (nxt + before + up + down + cz + C[p - 1, :, sl]))
            diag = jnp.where(coup > 0.0, diag, 0.0)
            DP[p, :, sl] = diag
            if inner:
                at = pl.ds(pl.multiple_of((p - 3) * 8, 8), 8)
                rd = 1.0 / diag
                RS[k, at] = (1.0 / 3.0) * rd
                AS[k, at] = B[p, :, sl] * rd
                FS[k, at] = c + up

    def inside(p, carry):
        plane(p, True)
        return carry

    def outside(i, carry):
        plane(jnp.where(i < 2, 1 + i, 25 + i), False)
        return carry

    lax.fori_loop(3, E - 3, inside, 0, unroll=2)
    lax.fori_loop(0, 4, outside, 0)
    r = rows_of((8, X))
    for i, src in enumerate((zlo, zhi)):
        c1, c2, b1, k1 = src[0], src[1], src[3], src[5]
        mlo[i] = jnp.where(r < 2, c1, jnp.where(r == 2, rot(c2, 2), jnp.where(r == 3, rot(b1, 3), rot(k1, 4))))
        mhi[i] = jnp.where(r > 5, c1, jnp.where(r == 5, rot(c2, -2), jnp.where(r == 4, rot(b1, -3), rot(k1, -4))))
    for g in range(D // 8):
        for k in range(NK):
            sl = tile_at(k)
            mlo[2 + g, :, sl] = AS[k, pl.ds(64 * g + 1, 8, stride=8), :]
            mhi[2 + g, :, sl] = AS[k, pl.ds(64 * g + 6, 8, stride=8), :]


def pack_third(t_ref, RS, FS, hlo, hhi):
    r = rows_of((8, X))
    for g in range(D // 8):
        for k in range(NK):
            sl = tile_at(k)
            for n, (src, low, high) in enumerate(((RS, 1, 6), (FS, 1, 5))):
                hlo[3 * g + n, :, sl] = src[k, pl.ds(64 * g + low, 8, stride=8), :]
                hhi[3 * g + n, :, sl] = src[k, pl.ds(64 * g + high, 8, stride=8), :]
        low = high = t_ref[8 * g]
        high = rot(high, 1)
        for j in range(1, 8):
            t = t_ref[8 * g + j]
            low = jnp.where(r == j, rot(t, j), low)
            high = jnp.where(r == j, rot(t, j - 7), high)
        hlo[3 * g + 2] = low
        hhi[3 * g + 2] = high


def pack_corners_second(zlo, zhi, w3lo, w3hi, lo, hi):
    r = rows_of((8, X))
    for g in range(D // 8):
        lo[2 + g] = w3lo[g]
        hi[2 + g] = w3hi[g]
    for i, src in enumerate((zlo, zhi)):
        lo[i] = jnp.where(r < 2, src[0], rot(src[1], 2))
        hi[i] = jnp.where(r > 5, src[0], rot(src[1], -2))


def assemble(yhi, ylo, mhi, mlo, C, B, K):
    r = rows_of((8, X))
    zero = jnp.zeros((8, X), F32)

    def two(m, carry):
        h, l = yhi[m], ylo[m]
        p = 2 * m + 3
        C[p] = jnp.where(r < 2, h, jnp.where(r > 5, rot(l, 4), 0.0))
        B[p] = jnp.where(r == 0, rot(h, -2), jnp.where(r == 7, rot(l, 6), 0.0))
        K[p] = jnp.where(r == 0, rot(h, -3), jnp.where(r == 7, rot(l, 7), 0.0))
        C[p + 1] = jnp.where(r < 2, rot(h, -4), jnp.where(r > 5, l, 0.0))
        B[p + 1] = jnp.where(r == 0, rot(h, -6), jnp.where(r == 7, rot(l, 2), 0.0))
        K[p + 1] = jnp.where(r == 0, rot(h, -7), jnp.where(r == 7, rot(l, 3), 0.0))
        return carry

    lax.fori_loop(0, D // 2, two, 0)
    for i, at in ((0, lambda j: 2 - j), (1, lambda j: 27 + j)):
        h, l = mhi[i], mlo[i]
        C[at(0)] = jnp.where(r < 2, h, jnp.where(r > 5, l, 0.0))
        C[at(1)] = jnp.where(r == 0, rot(h, -2), jnp.where(r == 7, rot(l, 2), 0.0))
        C[at(2)] = zero
        B[at(0)] = jnp.where(r == 0, rot(h, -3), jnp.where(r == 7, rot(l, 3), 0.0))
        K[at(0)] = jnp.where(r == 0, rot(h, -4), jnp.where(r == 7, rot(l, 4), 0.0))
        B[at(1)] = zero
        K[at(1)] = zero


def tile_at(k):
    return slice(128 * k, 128 * k + 128)


def left_shift(load, k, lane, rots):
    for m in (k, (k + 1) % NK):
        if m not in rots:
            rots[m] = pltpu.roll(load(m), 127, 1)
    return jnp.where(lane == 127, rots[(k + 1) % NK], rots[k])


def build(C, B, DP, A, A0, RD, FX, FY, FZ):
    lane = lax.broadcasted_iota(jnp.int32, (8, 128), 1)
    row = lax.broadcasted_iota(jnp.int32, (8, 128), 0)
    top, bottom = row == 0, row == 7

    def plane(p, carry):
        rots, last = {}, None
        for k in range(NK):
            sl = tile_at(k)
            own, c = C[0][p, :, sl], C[1][p, :, sl]
            own_up, own_down = pltpu.roll(own, 7, 0), pltpu.roll(own, 1, 0)
            up, down = pltpu.roll(c, 7, 0), pltpu.roll(c, 1, 0)
            FY[0][p, :, sl] = own + jnp.where(bottom, up, own_up)
            beside = jnp.where(bottom, up, jnp.where(top, down, 0.0))
            up, down = jnp.where(bottom, own_up, up), jnp.where(top, own_down, down)
            FY[1][p, :, sl] = c + up
            part = DP[p, :, sl]
            rd = jnp.where(part > 0.0, 1.0 / jnp.where(part > 0.0, part + 0.5 * beside, 1.0), 0.0)
            a = B[p, :, sl] * rd
            A[0][p, :, sl] = a
            A0[0][p, :, sl] = (2.0 / 3.0) * a
            RD[0][p, :, sl] = (1.0 / 3.0) * rd

            nxt = left_shift(lambda m: C[1][p, :, tile_at(m)], k, lane, rots)
            fx = c + nxt
            if k == NK - 1:
                nxt = jnp.where(lane == 127, 0.0, nxt)
                fx = jnp.where(lane == 127, 0.0, fx)
            back = pltpu.roll(c, 1, 1)
            before = jnp.where(lane == 0, 0.0 if last is None else last, back)
            last = back
            cz = C[1][p + 1, :, sl]
            FX[1][p, :, sl] = fx
            FZ[1][p, :, sl] = c + cz
            coup = RD[1][p, :, sl]
            diag = coup + (3.0 * c + 0.5 * (nxt + before + up + down + cz + C[1][p - 1, :, sl]))
            rd = jnp.where(coup > 0.0, 1.0 / jnp.where(coup > 0.0, diag, 1.0), 0.0)
            a = A[1][p, :, sl] * rd
            A[1][p, :, sl] = a
            A0[1][p, :, sl] = (2.0 / 3.0) * a
            RD[1][p, :, sl] = (1.0 / 3.0) * rd
        return carry

    lax.fori_loop(1, E - 1, plane, 0, unroll=2)


def unpack_third(hhi, hlo, RD, FY, RDN, FYN, TH):
    r = rows_of((8, X))

    def group(g, carry):
        for j in range(8):
            p = 3 + 8 * g + j
            RDN[p] = jnp.where(r == 1, rot(hhi[3 * g], 1 - j), jnp.where(r == 6, rot(hlo[3 * g], 6 - j), RD[p]))
            FYN[p] = jnp.where(r == 1, rot(hhi[3 * g + 1], 1 - j), jnp.where(r == 5, rot(hlo[3 * g + 1], 5 - j), FY[p]))
            TH[8 * g + j] = jnp.where(r == 7, rot(hhi[3 * g + 2], 7 - j), rot(hlo[3 * g + 2], -j))
        return carry

    lax.fori_loop(0, D // 8, group, 0)
    for p in (0, 1, 2, 27, 28, 29):
        RDN[p] = RD[p]
        FYN[p] = FY[p]


def sweep(A, OUT, A0, RD, FX, FY, FZ, runs):
    lane = lax.broadcasted_iota(jnp.int32, (8, 128), 1)
    row = lax.broadcasted_iota(jnp.int32, (8, 128), 0)
    first, last, top, bottom = lane == 0, lane == 127, row == 0, row == 7

    def plane(p, tiles):
        ahead, back = {}, {}

        def shift(m):
            if (m, tiles[0]) in ahead:
                return
            sl = tile_at(m)
            for h in tiles:
                a = A[h][p, :, sl]
                ahead[m, h] = pltpu.roll(a, 127, 1)
                back[m, h] = pltpu.roll(FX[h][p, :, sl] * a, 1, 1)

        shift(NK - 1)
        shift(0)
        for k in range(NK):
            sl = tile_at(k)
            shift((k + 1) % NK)
            a = [A[h][p, :, sl] for h in (0, 1)]
            fy = [FY[h][p, :, sl] for h in (0, 1)]
            up = [pltpu.roll(x, 7, 0) for x in a]
            down = [pltpu.roll(f * x, 1, 0) for f, x in zip(fy, a)]
            for h in tiles:
                flux = FX[h][p, :, sl] * jnp.where(last, ahead[(k + 1) % NK, h], ahead[k, h])
                flux = flux + jnp.where(first, back[(k - 1) % NK, h], back[k, h])
                flux = flux + (fy[h] * jnp.where(bottom, up[1 - h], up[h]) + jnp.where(top, down[1 - h], down[h]))
                flux = flux + (FZ[h][p, :, sl] * A[h][p + 1, :, sl] + FZ[h][p - 1, :, sl] * A[h][p - 1, :, sl])
                OUT[h][p, :, sl] = (1.0 / 3.0) * a[h] + (A0[h][p, :, sl] + RD[h][p, :, sl] * flux)

    for tiles, low, count in runs:
        group = 4 if count % 4 == 0 else 2

        def planes(i, carry):
            for q in range(group):
                plane(low + group * i + q, tiles)
            return carry

        if isinstance(low, int):
            lax.fori_loop(0, count // group, planes, 0)
        else:

            def single(i, carry):
                plane(low(i), tiles)
                return carry

            lax.fori_loop(0, count, single, 0)


INNER = ((0, 1), 3, D)
OWN = ((0,), 3, D)
NEXT = ((0,), lambda i: 2 + (D + 1) * i, 2)


def sweeps_first(C0, B0, FX0, FZ0, DP, yhi, ylo, mhi, mlo,
                 a_out, y2lo, y2hi, w3lo, w3hi, z2lo, z2hi, FY0, RD0, R0, FX1, FY1, FZ1, RD1, R1, C1, A_0, A_1, O_0, O_1):
    FX, FY, FZ, RD, A0, A, OUT = (FX0, FX1), (FY0, FY1), (FZ0, FZ1), (RD0, RD1), (R0, R1), (A_0, A_1), (O_0, O_1)
    assemble(yhi, ylo, mhi, mlo, C1, A_1, RD1)
    build((C0, C1), B0, DP, A, A0, RD, FX, FY, FZ)
    r = rows_of((8, X))

    def second_rows(g, carry):
        for j in range(8):
            p = 3 + 8 * g + j
            a = jnp.where(r == 1, rot(mhi[2 + g], 1 - j), jnp.where(r == 6, rot(mlo[2 + g], 6 - j), A_1[p]))
            A_1[p] = a
            R1[p] = (2.0 / 3.0) * a
        return carry

    lax.fori_loop(0, D // 8, second_rows, 0)
    sweep(A, OUT, A0, RD, FX, FY, FZ, (INNER, NEXT))
    sweep(OUT, A, A0, RD, FX, FY, FZ, (OWN,))
    A = A_0

    def copy(z, carry):
        a_out[z] = A[z + 3]
        return carry

    lax.fori_loop(0, D, copy, 0)

    def group(g, carry):
        for i in range(2):
            low, high = None, None
            for j in range(4):
                a = A[8 * g + 4 * i + j + 3]
                mask = (r >= 2 * j) & (r < 2 * j + 2)
                low = rot(a, 2 * j) if low is None else jnp.where(mask, rot(a, 2 * j), low)
                high = rot(a, 2 * j - 6) if high is None else jnp.where(mask, rot(a, 2 * j - 6), high)
            y2lo[2 * g + i] = low
            y2hi[2 * g + i] = high
        low, high = None, None
        for j in range(8):
            a = A[8 * g + j + 3]
            low = rot(a, j - 2) if low is None else jnp.where(r == j, rot(a, j - 2), low)
            high = rot(a, j - 5) if high is None else jnp.where(r == j, rot(a, j - 5), high)
        w3lo[g] = low
        w3hi[g] = high
        return carry

    lax.fori_loop(0, D // 8, group, 0)
    for j in range(3):
        z2lo[j] = A[3 + j]
        z2hi[j] = A[26 - j]


def tri(u):
    m = jnp.maximum(RADIUS - u, 0)
    return m * (m + 1) // 2


def inv_cover(position, length):
    total = (RADIUS + 1) ** 2 - tri(position) - tri(length - 1 - position)
    return 1.0 / total.astype(F32)


def third_sweep_own(info, s_ref, t_ref, zlo, zhi, a_in, FX0, FZ0, FY0, FYN, RD0, R0, y2hi, y2lo, z2lo, z2hi,
                    A_0, A_1, B_0, T, DX, SC):
    r = rows_of((8, X))

    def group(g, carry):
        for j in range(8):
            z = 8 * g + j
            A_0[z + 3] = a_in[z]
            tile, at = 2 * g + j // 4, 2 * (j % 4)
            A_1[z + 3] = jnp.where(r < 2, rot(y2hi[tile], -at), jnp.where(r > 5, rot(y2lo[tile], 6 - at), 0.0))
        return carry

    lax.fori_loop(0, 3, group, 0)
    for src, at in ((z2lo, lambda j: 2 - j), (z2hi, lambda j: 27 + j)):
        for j in range(3):
            A_0[at(j)] = src[j]
    for p in (0, 1, 2, 27, 28, 29):
        A_1[p] = jnp.zeros((8, X), F32)
    sweep((A_0, A_1), (B_0,), (R0,), (RD0,), (FX0,), (FY0, FYN), (FZ0,), (OWN,))

    lane8 = lax.broadcasted_iota(jnp.int32, (8, 128), 1)
    row8 = lax.broadcasted_iota(jnp.int32, (8, 128), 0)
    cover_y = inv_cover(lax.axis_index("blk") * S + row8, 16 * S)
    base_z = lax.axis_index("grp") * D
    factor = -0.5 * 3.0 * (1.0 - COND_FLOOR)

    def plane_t(z, carry):
        base = cover_y * inv_cover(base_z + z + jnp.zeros((8, 128), jnp.int32), 16 * D) * factor
        rt = {}
        for k in range(NK):
            sl = tile_at(k)
            t = t_ref[z, :, sl]
            tn = left_shift(lambda m: t_ref[z, :, tile_at(m)], k, lane8, rt)
            if k == NK - 1:
                tn = jnp.where(lane8 == 127, 0.0, tn)
            T[z + 1, :, sl] = t
            DX[z, :, sl] = t - tn
            s = s_ref[z, :, sl]
            scale = base * info[k // 2].astype(F32)
            if k in (0, NK - 1):
                scale = scale * inv_cover(lane8 + 128 * k, X)
            else:
                scale = scale * (1.0 / float((RADIUS + 1) ** 2))
            SC[z, :, sl] = (s * s) * scale
        return carry

    lax.fori_loop(0, D, plane_t, 0, unroll=2)

    T[0] = zlo[7]
    T[D + 1] = zhi[7]


def sweeps_second(TH, A_0, A_in, B_in, T, DX, SC, FX0, FZ0, FY0, RD0, R0, FX1, FYN, FZ1, RDN, R1,
                  e_hi, e_lo, send, late, sums, A_1, B_0, B_1, O_0, R):
    O_1 = A_1
    r = rows_of((8, X))

    def group(g, carry):
        for j in range(8):
            p = 8 * g + j + 3
            A_1[p] = jnp.where(r == 2, rot(e_hi[2 + g], 2 - j), jnp.where(r == 5, rot(e_lo[2 + g], 5 - j), A_in[p]))
            B_0[p] = B_in[p]
        return carry

    lax.fori_loop(0, 3, group, 0)
    for i, at in ((0, lambda j: 2 - j), (1, lambda j: 27 + j)):
        h, l = e_hi[i], e_lo[i]
        A_1[at(0)] = jnp.where(r < 2, h, jnp.where(r > 5, l, 0.0))
        A_1[at(1)] = jnp.where(r == 0, rot(h, -2), jnp.where(r == 7, rot(l, 2), 0.0))
    FX, FY, FZ, RD, A0 = (FX0, FX1), (FY0, FYN), (FZ0, FZ1), (RD0, RDN), (R0, R1)
    outer = ((0,), lambda i: jnp.where(i < 2, 1 + i, 25 + i), 4)
    sweep((A_0, A_1), (B_0, B_1), A0, RD, FX, FY, FZ, (((1,), 2, D + 2), outer))
    sweep((B_0, B_1), (O_0, O_1), A0, RD, FX, FY, FZ, (INNER, NEXT))

    lane8 = lax.broadcasted_iota(jnp.int32, (8, 128), 1)
    row8 = lax.broadcasted_iota(jnp.int32, (8, 128), 0)

    def plane_raw(z, carry):
        p = z + 3
        ra = {}
        last = None
        for k in range(NK):
            sl = tile_at(k)
            a, side, t, edge = O_0[p, :, sl], O_1[p, :, sl], T[z + 1, :, sl], TH[z, :, sl]
            an = left_shift(lambda m: O_0[p, :, tile_at(m)], k, lane8, ra)
            if k == NK - 1:
                an = jnp.where(lane8 == 127, 0.0, an)
            px = (a - an) * DX[z, :, sl]
            back = pltpu.roll(px, 1, 1)
            pair = px + jnp.where(lane8 == 0, a * t if last is None else last, back)
            last = back
            au = jnp.where(row8 == 7, rot(side, -1), rot(a, -1))
            ad = jnp.where(row8 == 0, rot(side, 1), rot(a, 1))
            tu, td = jnp.where(row8 == 7, edge, rot(t, -1)), jnp.where(row8 == 0, edge, rot(t, 1))
            pair = pair + ((a - au) * (t - tu) + (a - ad) * (t - td))
            pair = pair + (a - O_0[p + 1, :, sl]) * (t - T[z + 2, :, sl])
            pair = pair + (a - O_0[p - 1, :, sl]) * (t - T[z, :, sl])
            R[pl.ds(pl.multiple_of(z * 8, 8), 8), sl] = pair * SC[z, :, sl]
        return carry

    lax.fori_loop(0, D, plane_raw, 0, unroll=2)

    i = lax.broadcasted_iota(jnp.int32, (512, 256), 0) - 128
    j = lax.broadcasted_iota(jnp.int32, (512, 256), 1)
    weights = jnp.maximum(RADIUS + 1 - jnp.abs(i - j), 0).astype(F32).astype(BF16)
    for n in range(X // 256):
        low, high = max(256 * n - 128, 0), min(256 * n + 384, X)
        x = R[:, low:high]
        w = weights[low - (256 * n - 128) : high - (256 * n - 128)]
        xh = x.astype(BF16)
        xl = (x - xh.astype(F32)).astype(BF16)
        y = jnp.dot(xh, w, preferred_element_type=F32) + jnp.dot(xl, w, preferred_element_type=F32)
        for h in range(2):
            part, m = y[:, 128 * h : 128 * h + 128], (2 * n + h) % HALF
            if n < X // 512:
                send[m] = part[0 : 4 * D]
                send[HALF + m] = part[4 * D :]
            else:
                late[m] = part
                layers = [part[8 * z : 8 * z + 8] for z in range(D)]
                sums[0, 8 * m : 8 * m + 8] = sum(layers)
                sums[1, 8 * m : 8 * m + 8] = sum(float(z) * layers[z] for z in range(1, D))


def filter_y(x_ref, out):
    i = lax.broadcasted_iota(jnp.int32, (128, 128), 0)
    j = lax.broadcasted_iota(jnp.int32, (128, 128), 1)
    w = jnp.maximum(RADIUS + 1 - jnp.abs(i - j), 0).astype(F32).astype(BF16)
    for z in range(D // 2):
        x = x_ref[:, 8 * z : 8 * z + 8, :].reshape(128, 128)
        xh = x.astype(BF16)
        xl = (x - xh.astype(F32)).astype(BF16)
        y = jnp.dot(w, xh, preferred_element_type=F32) + jnp.dot(w, xl, preferred_element_type=F32)
        out[:, 8 * z : 8 * z + 8, :] = y.reshape(16, 8, 128)


def whole_layer(ref, m, z):
    return ref[m, 8 * z : 8 * z + 8, :]


def split_layer(ref, m, z):
    return ref[HALF * (z // (D // 2)) + m, 8 * (z % (D // 2)) : 8 * (z % (D // 2)) + 8, :]


def layer_sums(x_ref, sums):
    def chunk(m, carry):
        layers = [split_layer(x_ref, m, z) for z in range(D)]
        sl = pl.ds(pl.multiple_of(m * 8, 8), 8)
        sums[0, sl] = sum(layers)
        sums[1, sl] = sum(float(z) * layers[z] for z in range(1, D))
        return carry

    lax.fori_loop(0, HALF, chunk, 0)


def filter_z(load, m, own, up, down, up2, down2, store):
    sl = pl.ds(pl.multiple_of(m * 8, 8), 8)
    u0, u1, d0, d1 = up[0, sl, :], up[1, sl, :], down[0, sl, :], down[1, sl, :]
    suffix = load(down2, m, D - 1)
    total = suffix
    far = [None] * D
    far[D - 1] = total
    for z in range(D - 2, -1, -1):
        suffix = suffix + load(down2, m, z)
        total = total + suffix
        far[z] = total
    sum_own = load(own, m, 0)
    distance = jnp.zeros_like(sum_own)
    for z in range(1, D):
        x = load(own, m, z)
        sum_own = sum_own + x
        distance = distance + float(z) * x
    near = (25.0 * (u0 + d0) + (d1 - u1)) + float(RADIUS + 1) * sum_own
    slope = u0 - d0
    prefix_own = jnp.zeros_like(sum_own)
    prefix_up = jnp.zeros_like(sum_own)
    total_up = jnp.zeros_like(sum_own)
    for z in range(D):
        prefix_up = prefix_up + load(up2, m, z)
        total_up = total_up + prefix_up
        store(z, (near - distance) + (total_up + far[z]))
        prefix_own = prefix_own + load(own, m, z)
        distance = distance + (2.0 * prefix_own - sum_own)
        near = near + slope


def filter_z_late(own, up, down, up2, down2, out):
    def chunk(m, carry):
        def store(z, value):
            out[HALF * (z // (D // 2)) + m, 8 * (z % (D // 2)) : 8 * (z % (D // 2)) + 8, :] = value

        filter_z(whole_layer, m, own, up, down, up2, down2, store)
        return carry

    lax.fori_loop(0, HALF, chunk, 0)


def finish_early(info, own, up, down, up2, down2, out_hbm, out, sem):
    def chunk(m, carry):
        column = pl.ds(pl.multiple_of(m * 128, 128), 128)
        scale = REPORT_SCALE * info[m // 2].astype(F32)

        def store(z, value):
            out[z, :, column] = value * scale

        filter_z(split_layer, m, own, up, down, up2, down2, store)
        return carry

    lax.fori_loop(0, HALF, chunk, 0)
    copy = pltpu.make_async_copy(out, out_hbm.at[:, :, pl.ds(0, X // 2)], sem)
    copy.start()
    copy.wait()


def finish_late(info, late, half_done, out_hbm, out, sems):
    del half_done
    copies = []
    for part in range(2):
        for m in range(part * HALF // 2, (part + 1) * HALF // 2):
            scale = REPORT_SCALE * info[HALF // 2 + m // 2].astype(F32)
            for z in range(D):
                out[z, :, tile_at(m)] = split_layer(late, m, z) * scale
        column = pl.ds(part * X // 4, X // 4)
        target = pl.ds(X // 2 + part * X // 4, X // 4)
        copies.append(pltpu.make_async_copy(out.at[:, :, column], out_hbm.at[:, :, target], sems.at[part]))
        copies[-1].start()
    for copy in copies:
        copy.wait()


def kernel_call(body, ins, outs, scratch=(), scalars=0, limit=60):
    vmem = pl.BlockSpec(memory_space=pltpu.VMEM)
    smem = pl.BlockSpec(memory_space=pltpu.SMEM)
    return pl.pallas_call(
        body,
        out_shape=[jax.ShapeDtypeStruct(s, F32) for s in outs],
        in_specs=[smem] * scalars + [vmem] * (len(ins) - scalars),
        out_specs=[vmem] * len(outs),
        scratch_shapes=[pltpu.VMEM(s, F32) for s in scratch],
        compiler_params=pltpu.CompilerParams(vmem_limit_bytes=limit * MIB),
    )(*ins)


def moved(x, dz, dy):
    pairs = []
    for g in range(16):
        for b in range(16):
            if 0 <= g + dz < 16 and 0 <= b + dy < 16:
                pairs.append(((g + dz) * 16 + b + dy, g * 16 + b))
    return lax.ppermute(x, ("grp", "blk"), pairs)


def local(solid, thermal, target, coolant, switch):
    info = switch.reshape(8)
    block = (D, 8, X)
    near = tile_shape(D // 2)
    ylo, yhi, zlo, zhi = pl.pallas_call(
        pack_first,
        out_shape=[jax.ShapeDtypeStruct(shape, F32) for shape in (near, near, tile_shape(8), tile_shape(8))],
        in_specs=[pl.BlockSpec(memory_space=pltpu.HBM)] * 4,
        out_specs=[pl.BlockSpec(memory_space=pltpu.HBM)] * 4,
        scratch_shapes=[pltpu.VMEM(block, F32)] * 3
        + [pltpu.VMEM(near, F32)] * 2
        + [pltpu.VMEM(tile_shape(8), F32)] * 2
        + [pltpu.SemaphoreType.DMA((3, D // STEP)), pltpu.SemaphoreType.DMA((2,)), pltpu.SemaphoreType.DMA((3, D // STEP))],
        compiler_params=pltpu.CompilerParams(vmem_limit_bytes=56 * MIB),
    )(solid, thermal, target, coolant)
    yhi, ylo = moved(ylo, 0, 1), moved(yhi, 0, -1)
    zlo, zhi = moved(zhi, -1, 0), moved(zlo, 1, 0)
    ext, flat = (E, 8, X), (D * 8, X)
    rows = (NK, D * 8, 128)
    c, b, fx, fz, dp, mlo, mhi, rs, fs = kernel_call(
        build_own, (solid, target, coolant, zlo, zhi),
        [ext] * 5 + [tile_shape(5)] * 2 + [rows] * 2, [rows], limit=8,
    )
    hlo, hhi = kernel_call(pack_third, (thermal, rs, fs), [tile_shape(9)] * 2, limit=8)
    mhi, mlo = moved(mlo, 0, 1), moved(mhi, 0, -1)
    hhi, hlo = moved(hlo, 0, 1), moved(hhi, 0, -1)
    a, y2lo, y2hi, w3lo, w3hi, z2lo, z2hi, *fields = kernel_call(
        sweeps_first, (c, b, fx, fz, dp, yhi, ylo, mhi, mlo),
        [block, tile_shape(6), tile_shape(6)] + [tile_shape(3)] * 4 + [ext] * 8, [ext] * 5, limit=14,
    )
    y2hi, y2lo = moved(y2lo, 0, 1), moved(y2hi, 0, -1)
    z2lo, z2hi = moved(z2hi, -1, 0), moved(z2lo, 1, 0)
    fy0, rd0, r0, fx1, fy1, fz1, rd1, r1 = fields
    rd1, fy1, th = kernel_call(unpack_third, (hhi, hlo, rd1, fy1), [ext, ext, block], limit=8)
    clo, chi = kernel_call(pack_corners_second, (z2lo, z2hi, w3lo, w3hi), [tile_shape(5)] * 2, limit=8)
    e_hi, e_lo = moved(clo, 0, 1), moved(chi, 0, -1)
    parts, wide, small = (2 * HALF, D * 4, 128), (HALF, D * 8, 128), (2, HALF * 8, 128)
    a_0, a_1, b_0, *terms = kernel_call(
        third_sweep_own,
        (info, solid, thermal, zlo, zhi, a, fx, fz, fy0, fy1, rd0, r0, y2hi, y2lo, z2lo, z2hi),
        [ext] * 3 + [(D + 2, 8, X), block, block], scalars=1, limit=8,
    )
    send, late, sums = kernel_call(
        sweeps_second,
        (th, a_0, a_1, b_0, *terms, fx, fz, fy0, rd0, r0, fx1, fy1, fz1, rd1, r1, e_hi, e_lo),
        [parts, wide, small], [ext] * 4 + [flat], limit=13,
    )

    def exchanged(x):
        return lax.all_to_all(x, "blk", split_axis=0, concat_axis=0, tiled=True)

    columns = exchanged(send)
    up2, down2 = moved(late, 2, 0), moved(late, -2, 0)
    up, down = moved(sums, 1, 0), moved(sums, -1, 0)
    (columns,) = kernel_call(filter_y, (columns,), [parts], limit=8)
    early = exchanged(columns)
    (late,) = kernel_call(filter_z_late, (late, up, down, up2, down2), [parts], limit=8)
    late = exchanged(late)
    up2, down2 = moved(early, 2, 0), moved(early, -2, 0)
    (sums,) = kernel_call(layer_sums, (early,), [small], limit=8)
    up, down = moved(sums, 1, 0), moved(sums, -1, 0)
    (late,) = kernel_call(filter_y, (late,), [parts], limit=8)
    late = exchanged(late)
    smem, vmem, anywhere = (pl.BlockSpec(memory_space=space) for space in (pltpu.SMEM, pltpu.VMEM, pl.ANY))
    half = pltpu.VMEM((D, 8, X // 2), F32)
    out = pl.pallas_call(
        finish_early,
        out_shape=jax.ShapeDtypeStruct(block, F32),
        in_specs=[smem] + [vmem] * 5,
        out_specs=anywhere,
        scratch_shapes=[half, pltpu.SemaphoreType.DMA(())],
        compiler_params=pltpu.CompilerParams(vmem_limit_bytes=8 * MIB),
    )(info, early, up, down, up2, down2)
    return pl.pallas_call(
        finish_late,
        out_shape=jax.ShapeDtypeStruct(block, F32),
        in_specs=[smem, vmem, anywhere],
        out_specs=anywhere,
        scratch_shapes=[half, pltpu.SemaphoreType.DMA((2,))],
        input_output_aliases={2: 0},
        compiler_params=pltpu.CompilerParams(vmem_limit_bytes=8 * MIB),
    )(info, late, out)


def tile_shape(n):
    return (n, 8, X)


def solution(mesh):
    spec = P("grp", "blk", None)
    return jax.shard_map(
        local, mesh=mesh, in_specs=(spec,) * 5, out_specs=spec, check_vma=False
    )
```

```python
import jax
import jax.numpy as jnp
from jax import lax
from jax.experimental import pallas as pl
from jax.experimental.pallas import tpu as pltpu
from jax.sharding import PartitionSpec as P

RADIUS = 48
COND_FLOOR = 0.001
REPORT_SCALE = 100.0
D, S, X = 24, 8, 2048
NK = X // 128
E = D + 6
STEP = 8
HALF = NK // 2
F32 = jnp.float32
BF16 = jnp.bfloat16
MIB = 1024 * 1024


def rows_of(shape):
    return lax.broadcasted_iota(jnp.int32, shape, 0)


def rot(tile, shift):
    shift = shift % 8
    return tile if shift == 0 else pltpu.roll(tile, shift, 0)


def conduct_of(solid):
    return COND_FLOOR + (1.0 - COND_FLOOR) * (solid * solid * solid)


def pack_first(s_hbm, t_hbm, b_hbm, k_hbm, ylo_hbm, yhi_hbm, zlo_hbm, zhi_hbm,
               s_ref, b_ref, k_ref, ylo, yhi, zlo, zhi, sems, edge_sems, out_sems):
    pairs = ((s_hbm, s_ref), (b_hbm, b_ref), (k_hbm, k_ref))
    copies = [
        [
            pltpu.make_async_copy(src.at[pl.ds(i * STEP, STEP)], dst.at[pl.ds(i * STEP, STEP)], sems.at[n, i])
            for n, (src, dst) in enumerate(pairs)
        ]
        for i in range(D // STEP)
    ]
    edges = [
        pltpu.make_async_copy(t_hbm.at[0], zlo.at[7], edge_sems.at[0]),
        pltpu.make_async_copy(t_hbm.at[D - 1], zhi.at[7], edge_sems.at[1]),
    ]
    for group in copies:
        for copy in group:
            copy.start()
    for copy in edges:
        copy.start()
    r = rows_of((8, X))
    outs = []
    for i, group in enumerate(copies):
        for copy in group:
            copy.wait()

        def two(m, carry):
            ce, co = conduct_of(s_ref[2 * m]), conduct_of(s_ref[2 * m + 1])
            be, bo, ke, ko = b_ref[2 * m], b_ref[2 * m + 1], k_ref[2 * m], k_ref[2 * m + 1]
            even = jnp.where(r < 2, ce, jnp.where(r == 2, rot(be, 2), rot(ke, 3)))
            odd = jnp.where(r < 6, rot(co, 4), jnp.where(r == 6, rot(bo, 6), rot(ko, 7)))
            ylo[m] = jnp.where(r < 4, even, odd)
            even = jnp.where(r > 1, rot(ce, 4), jnp.where(r == 1, rot(be, 2), rot(ke, 1)))
            odd = jnp.where(r > 5, co, jnp.where(r == 5, rot(bo, -2), rot(ko, -3)))
            yhi[m] = jnp.where(r < 4, even, odd)
            return carry

        half = STEP // 2
        lax.fori_loop(i * half, (i + 1) * half, two, 0)
        part = pl.ds(i * half, half)
        outs += [
            pltpu.make_async_copy(ylo.at[part], ylo_hbm.at[part], out_sems.at[0, i]),
            pltpu.make_async_copy(yhi.at[part], yhi_hbm.at[part], out_sems.at[1, i]),
        ]
        outs[-2].start()
        outs[-1].start()
    for copy in edges:
        copy.wait()
    for dst, at in ((zlo, lambda j: j), (zhi, lambda j: D - 1 - j)):
        for j in range(3):
            dst[j] = conduct_of(s_ref[at(j)])
        for j in range(2):
            dst[3 + j] = b_ref[at(j)]
            dst[5 + j] = k_ref[at(j)]
    outs += [
        pltpu.make_async_copy(zlo, zlo_hbm, out_sems.at[2, 0]),
        pltpu.make_async_copy(zhi, zhi_hbm, out_sems.at[2, 1]),
    ]
    outs[-2].start()
    outs[-1].start()
    for copy in outs:
        copy.wait()


def build_own(s_ref, b_ref, k_ref, zlo, zhi, C, B, FX, FZ, DP, mlo, mhi, RS, FS, AS):
    lane = lax.broadcasted_iota(jnp.int32, (8, 128), 1)
    row = lax.broadcasted_iota(jnp.int32, (8, 128), 0)

    def own(z, carry):
        C[z + 3] = conduct_of(s_ref[z])
        B[z + 3] = b_ref[z]
        DP[z + 3] = k_ref[z]
        return carry

    lax.fori_loop(0, D, own, 0)
    for src, at in ((zlo, lambda j: 2 - j), (zhi, lambda j: 27 + j)):
        for j in range(3):
            C[at(j)] = src[j]
        for j in range(2):
            B[at(j)] = src[3 + j]
            DP[at(j)] = src[5 + j]
    FZ[0] = C[0] + C[1]

    def plane(p, inner):
        rots, last = {}, None
        for k in range(NK):
            sl = tile_at(k)
            c = C[p, :, sl]
            nxt = left_shift(lambda m: C[p, :, tile_at(m)], k, lane, rots)
            fx = c + nxt
            if k == NK - 1:
                nxt = jnp.where(lane == 127, 0.0, nxt)
                fx = jnp.where(lane == 127, 0.0, fx)
            back = pltpu.roll(c, 1, 1)
            before = jnp.where(lane == 0, 0.0 if last is None else last, back)
            last = back
            up = jnp.where(row == 7, 0.0, pltpu.roll(c, 7, 0))
            down = jnp.where(row == 0, 0.0, pltpu.roll(c, 1, 0))
            cz = C[p + 1, :, sl]
            FX[p, :, sl] = fx
            FZ[p, :, sl] = c + cz
            coup = DP[p, :, sl]
            diag = coup + (3.0 * c + 0.5 * (nxt + before + up + down + cz + C[p - 1, :, sl]))
            diag = jnp.where(coup > 0.0, diag, 0.0)
            DP[p, :, sl] = diag
            if inner:
                at = pl.ds(pl.multiple_of((p - 3) * 8, 8), 8)
                rd = 1.0 / diag
                RS[k, at] = (1.0 / 3.0) * rd
                AS[k, at] = B[p, :, sl] * rd
                FS[k, at] = c + up

    def inside(p, carry):
        plane(p, True)
        return carry

    def outside(i, carry):
        plane(jnp.where(i < 2, 1 + i, 25 + i), False)
        return carry

    lax.fori_loop(3, E - 3, inside, 0, unroll=2)
    lax.fori_loop(0, 4, outside, 0)
    r = rows_of((8, X))
    for i, src in enumerate((zlo, zhi)):
        c1, c2, b1, k1 = src[0], src[1], src[3], src[5]
        mlo[i] = jnp.where(r < 2, c1, jnp.where(r == 2, rot(c2, 2), jnp.where(r == 3, rot(b1, 3), rot(k1, 4))))
        mhi[i] = jnp.where(r > 5, c1, jnp.where(r == 5, rot(c2, -2), jnp.where(r == 4, rot(b1, -3), rot(k1, -4))))
    for g in range(D // 8):
        for k in range(NK):
            sl = tile_at(k)
            mlo[2 + g, :, sl] = AS[k, pl.ds(64 * g + 1, 8, stride=8), :]
            mhi[2 + g, :, sl] = AS[k, pl.ds(64 * g + 6, 8, stride=8), :]


def pack_third(t_ref, RS, FS, hlo, hhi):
    r = rows_of((8, X))
    for g in range(D // 8):
        for k in range(NK):
            sl = tile_at(k)
            for n, (src, low, high) in enumerate(((RS, 1, 6), (FS, 1, 5))):
                hlo[3 * g + n, :, sl] = src[k, pl.ds(64 * g + low, 8, stride=8), :]
                hhi[3 * g + n, :, sl] = src[k, pl.ds(64 * g + high, 8, stride=8), :]
        low = high = t_ref[8 * g]
        high = rot(high, 1)
        for j in range(1, 8):
            t = t_ref[8 * g + j]
            low = jnp.where(r == j, rot(t, j), low)
            high = jnp.where(r == j, rot(t, j - 7), high)
        hlo[3 * g + 2] = low
        hhi[3 * g + 2] = high


def pack_corners_second(zlo, zhi, w3lo, w3hi, lo, hi):
    r = rows_of((8, X))
    for g in range(D // 8):
        lo[2 + g] = w3lo[g]
        hi[2 + g] = w3hi[g]
    for i, src in enumerate((zlo, zhi)):
        lo[i] = jnp.where(r < 2, src[0], rot(src[1], 2))
        hi[i] = jnp.where(r > 5, src[0], rot(src[1], -2))


def assemble(yhi, ylo, mhi, mlo, C, B, K):
    r = rows_of((8, X))
    zero = jnp.zeros((8, X), F32)

    def two(m, carry):
        h, l = yhi[m], ylo[m]
        p = 2 * m + 3
        C[p] = jnp.where(r < 2, h, jnp.where(r > 5, rot(l, 4), 0.0))
        B[p] = jnp.where(r == 0, rot(h, -2), jnp.where(r == 7, rot(l, 6), 0.0))
        K[p] = jnp.where(r == 0, rot(h, -3), jnp.where(r == 7, rot(l, 7), 0.0))
        C[p + 1] = jnp.where(r < 2, rot(h, -4), jnp.where(r > 5, l, 0.0))
        B[p + 1] = jnp.where(r == 0, rot(h, -6), jnp.where(r == 7, rot(l, 2), 0.0))
        K[p + 1] = jnp.where(r == 0, rot(h, -7), jnp.where(r == 7, rot(l, 3), 0.0))
        return carry

    lax.fori_loop(0, D // 2, two, 0)
    for i, at in ((0, lambda j: 2 - j), (1, lambda j: 27 + j)):
        h, l = mhi[i], mlo[i]
        C[at(0)] = jnp.where(r < 2, h, jnp.where(r > 5, l, 0.0))
        C[at(1)] = jnp.where(r == 0, rot(h, -2), jnp.where(r == 7, rot(l, 2), 0.0))
        C[at(2)] = zero
        B[at(0)] = jnp.where(r == 0, rot(h, -3), jnp.where(r == 7, rot(l, 3), 0.0))
        K[at(0)] = jnp.where(r == 0, rot(h, -4), jnp.where(r == 7, rot(l, 4), 0.0))
        B[at(1)] = zero
        K[at(1)] = zero


def tile_at(k):
    return slice(128 * k, 128 * k + 128)


def left_shift(load, k, lane, rots):
    for m in (k, (k + 1) % NK):
        if m not in rots:
            rots[m] = pltpu.roll(load(m), 127, 1)
    return jnp.where(lane == 127, rots[(k + 1) % NK], rots[k])


def build(C, B, DP, A, A0, RD, FX, FY, FZ):
    lane = lax.broadcasted_iota(jnp.int32, (8, 128), 1)
    row = lax.broadcasted_iota(jnp.int32, (8, 128), 0)
    top, bottom = row == 0, row == 7

    def plane(p, carry):
        rots, last = {}, None
        for k in range(NK):
            sl = tile_at(k)
            own, c = C[0][p, :, sl], C[1][p, :, sl]
            own_up, own_down = pltpu.roll(own, 7, 0), pltpu.roll(own, 1, 0)
            up, down = pltpu.roll(c, 7, 0), pltpu.roll(c, 1, 0)
            FY[0][p, :, sl] = own + jnp.where(bottom, up, own_up)
            beside = jnp.where(bottom, up, jnp.where(top, down, 0.0))
            up, down = jnp.where(bottom, own_up, up), jnp.where(top, own_down, down)
            FY[1][p, :, sl] = c + up
            part = DP[p, :, sl]
            rd = jnp.where(part > 0.0, 1.0 / jnp.where(part > 0.0, part + 0.5 * beside, 1.0), 0.0)
            a = B[p, :, sl] * rd
            A[0][p, :, sl] = a
            A0[0][p, :, sl] = (2.0 / 3.0) * a
            RD[0][p, :, sl] = (1.0 / 3.0) * rd

            nxt = left_shift(lambda m: C[1][p, :, tile_at(m)], k, lane, rots)
            fx = c + nxt
            if k == NK - 1:
                nxt = jnp.where(lane == 127, 0.0, nxt)
                fx = jnp.where(lane == 127, 0.0, fx)
            back = pltpu.roll(c, 1, 1)
            before = jnp.where(lane == 0, 0.0 if last is None else last, back)
            last = back
            cz = C[1][p + 1, :, sl]
            FX[1][p, :, sl] = fx
            FZ[1][p, :, sl] = c + cz
            coup = RD[1][p, :, sl]
            diag = coup + (3.0 * c + 0.5 * (nxt + before + up + down + cz + C[1][p - 1, :, sl]))
            rd = jnp.where(coup > 0.0, 1.0 / jnp.where(coup > 0.0, diag, 1.0), 0.0)
            a = A[1][p, :, sl] * rd
            A[1][p, :, sl] = a
            A0[1][p, :, sl] = (2.0 / 3.0) * a
            RD[1][p, :, sl] = (1.0 / 3.0) * rd
        return carry

    lax.fori_loop(1, E - 1, plane, 0, unroll=2)


def unpack_third(hhi, hlo, RD, FY, RDN, FYN, TH):
    r = rows_of((8, X))

    def group(g, carry):
        for j in range(8):
            p = 3 + 8 * g + j
            RDN[p] = jnp.where(r == 1, rot(hhi[3 * g], 1 - j), jnp.where(r == 6, rot(hlo[3 * g], 6 - j), RD[p]))
            FYN[p] = jnp.where(r == 1, rot(hhi[3 * g + 1], 1 - j), jnp.where(r == 5, rot(hlo[3 * g + 1], 5 - j), FY[p]))
            TH[8 * g + j] = jnp.where(r == 7, rot(hhi[3 * g + 2], 7 - j), rot(hlo[3 * g + 2], -j))
        return carry

    lax.fori_loop(0, D // 8, group, 0)
    for p in (0, 1, 2, 27, 28, 29):
        RDN[p] = RD[p]
        FYN[p] = FY[p]


def sweep(A, OUT, A0, RD, FX, FY, FZ, runs):
    lane = lax.broadcasted_iota(jnp.int32, (8, 128), 1)
    row = lax.broadcasted_iota(jnp.int32, (8, 128), 0)
    first, last, top, bottom = lane == 0, lane == 127, row == 0, row == 7

    def plane(p, tiles):
        ahead, back = {}, {}

        def shift(m):
            if (m, tiles[0]) in ahead:
                return
            sl = tile_at(m)
            for h in tiles:
                a = A[h][p, :, sl]
                ahead[m, h] = pltpu.roll(a, 127, 1)
                back[m, h] = pltpu.roll(FX[h][p, :, sl] * a, 1, 1)

        shift(NK - 1)
        shift(0)
        for k in range(NK):
            sl = tile_at(k)
            shift((k + 1) % NK)
            a = [A[h][p, :, sl] for h in (0, 1)]
            fy = [FY[h][p, :, sl] for h in (0, 1)]
            up = [pltpu.roll(x, 7, 0) for x in a]
            down = [pltpu.roll(f * x, 1, 0) for f, x in zip(fy, a)]
            for h in tiles:
                flux = FX[h][p, :, sl] * jnp.where(last, ahead[(k + 1) % NK, h], ahead[k, h])
                flux = flux + jnp.where(first, back[(k - 1) % NK, h], back[k, h])
                flux = flux + (fy[h] * jnp.where(bottom, up[1 - h], up[h]) + jnp.where(top, down[1 - h], down[h]))
                flux = flux + (FZ[h][p, :, sl] * A[h][p + 1, :, sl] + FZ[h][p - 1, :, sl] * A[h][p - 1, :, sl])
                OUT[h][p, :, sl] = (1.0 / 3.0) * a[h] + (A0[h][p, :, sl] + RD[h][p, :, sl] * flux)

    for tiles, low, count in runs:
        group = 4 if count % 4 == 0 else 2

        def planes(i, carry):
            for q in range(group):
                plane(low + group * i + q, tiles)
            return carry

        if isinstance(low, int):
            lax.fori_loop(0, count // group, planes, 0)
        else:

            def single(i, carry):
                plane(low(i), tiles)
                return carry

            lax.fori_loop(0, count, single, 0)


INNER = ((0, 1), 3, D)
OWN = ((0,), 3, D)
NEXT = ((0,), lambda i: 2 + (D + 1) * i, 2)


def sweeps_first(C0, B0, FX0, FZ0, DP, yhi, ylo, mhi, mlo,
                 a_out, y2lo, y2hi, w3lo, w3hi, z2lo, z2hi, FY0, RD0, R0, FX1, FY1, FZ1, RD1, R1, C1, A_0, A_1, O_0, O_1):
    FX, FY, FZ, RD, A0, A, OUT = (FX0, FX1), (FY0, FY1), (FZ0, FZ1), (RD0, RD1), (R0, R1), (A_0, A_1), (O_0, O_1)
    assemble(yhi, ylo, mhi, mlo, C1, A_1, RD1)
    build((C0, C1), B0, DP, A, A0, RD, FX, FY, FZ)
    r = rows_of((8, X))

    def second_rows(g, carry):
        for j in range(8):
            p = 3 + 8 * g + j
            a = jnp.where(r == 1, rot(mhi[2 + g], 1 - j), jnp.where(r == 6, rot(mlo[2 + g], 6 - j), A_1[p]))
            A_1[p] = a
            R1[p] = (2.0 / 3.0) * a
        return carry

    lax.fori_loop(0, D // 8, second_rows, 0)
    sweep(A, OUT, A0, RD, FX, FY, FZ, (INNER, NEXT))
    sweep(OUT, A, A0, RD, FX, FY, FZ, (OWN,))
    A = A_0

    def copy(z, carry):
        a_out[z] = A[z + 3]
        return carry

    lax.fori_loop(0, D, copy, 0)

    def group(g, carry):
        for i in range(2):
            low, high = None, None
            for j in range(4):
                a = A[8 * g + 4 * i + j + 3]
                mask = (r >= 2 * j) & (r < 2 * j + 2)
                low = rot(a, 2 * j) if low is None else jnp.where(mask, rot(a, 2 * j), low)
                high = rot(a, 2 * j - 6) if high is None else jnp.where(mask, rot(a, 2 * j - 6), high)
            y2lo[2 * g + i] = low
            y2hi[2 * g + i] = high
        low, high = None, None
        for j in range(8):
            a = A[8 * g + j + 3]
            low = rot(a, j - 2) if low is None else jnp.where(r == j, rot(a, j - 2), low)
            high = rot(a, j - 5) if high is None else jnp.where(r == j, rot(a, j - 5), high)
        w3lo[g] = low
        w3hi[g] = high
        return carry

    lax.fori_loop(0, D // 8, group, 0)
    for j in range(3):
        z2lo[j] = A[3 + j]
        z2hi[j] = A[26 - j]


def tri(u):
    m = jnp.maximum(RADIUS - u, 0)
    return m * (m + 1) // 2


def inv_cover(position, length):
    total = (RADIUS + 1) ** 2 - tri(position) - tri(length - 1 - position)
    return 1.0 / total.astype(F32)


def third_sweep_own(info, s_ref, t_ref, zlo, zhi, a_in, FX0, FZ0, FY0, FYN, RD0, R0, y2hi, y2lo, z2lo, z2hi,
                    A_0, A_1, B_0, T, DX, SC):
    r = rows_of((8, X))

    def group(g, carry):
        for j in range(8):
            z = 8 * g + j
            A_0[z + 3] = a_in[z]
            tile, at = 2 * g + j // 4, 2 * (j % 4)
            A_1[z + 3] = jnp.where(r < 2, rot(y2hi[tile], -at), jnp.where(r > 5, rot(y2lo[tile], 6 - at), 0.0))
        return carry

    lax.fori_loop(0, 3, group, 0)
    for src, at in ((z2lo, lambda j: 2 - j), (z2hi, lambda j: 27 + j)):
        for j in range(3):
            A_0[at(j)] = src[j]
    for p in (0, 1, 2, 27, 28, 29):
        A_1[p] = jnp.zeros((8, X), F32)
    sweep((A_0, A_1), (B_0,), (R0,), (RD0,), (FX0,), (FY0, FYN), (FZ0,), (OWN,))

    lane8 = lax.broadcasted_iota(jnp.int32, (8, 128), 1)
    row8 = lax.broadcasted_iota(jnp.int32, (8, 128), 0)
    cover_y = inv_cover(lax.axis_index("blk") * S + row8, 16 * S)
    base_z = lax.axis_index("grp") * D
    factor = -0.5 * 3.0 * (1.0 - COND_FLOOR)

    def plane_t(z, carry):
        base = cover_y * inv_cover(base_z + z + jnp.zeros((8, 128), jnp.int32), 16 * D) * factor
        rt = {}
        for k in range(NK):
            sl = tile_at(k)
            t = t_ref[z, :, sl]
            tn = left_shift(lambda m: t_ref[z, :, tile_at(m)], k, lane8, rt)
            if k == NK - 1:
                tn = jnp.where(lane8 == 127, 0.0, tn)
            T[z + 1, :, sl] = t
            DX[z, :, sl] = t - tn
            s = s_ref[z, :, sl]
            scale = base * info[k // 2].astype(F32)
            if k in (0, NK - 1):
                scale = scale * inv_cover(lane8 + 128 * k, X)
            else:
                scale = scale * (1.0 / float((RADIUS + 1) ** 2))
            SC[z, :, sl] = (s * s) * scale
        return carry

    lax.fori_loop(0, D, plane_t, 0, unroll=2)

    T[0] = zlo[7]
    T[D + 1] = zhi[7]


def sweeps_second(TH, A_0, A_in, B_in, T, DX, SC, FX0, FZ0, FY0, RD0, R0, FX1, FYN, FZ1, RDN, R1,
                  e_hi, e_lo, send_any, late, sums, A_1, B_0, B_1, O_0, R, send, sems):
    O_1 = A_1
    r = rows_of((8, X))

    def group(g, carry):
        for j in range(8):
            p = 8 * g + j + 3
            A_1[p] = jnp.where(r == 2, rot(e_hi[2 + g], 2 - j), jnp.where(r == 5, rot(e_lo[2 + g], 5 - j), A_in[p]))
            B_0[p] = B_in[p]
        return carry

    lax.fori_loop(0, 3, group, 0)
    for i, at in ((0, lambda j: 2 - j), (1, lambda j: 27 + j)):
        h, l = e_hi[i], e_lo[i]
        A_1[at(0)] = jnp.where(r < 2, h, jnp.where(r > 5, l, 0.0))
        A_1[at(1)] = jnp.where(r == 0, rot(h, -2), jnp.where(r == 7, rot(l, 2), 0.0))
    FX, FY, FZ, RD, A0 = (FX0, FX1), (FY0, FYN), (FZ0, FZ1), (RD0, RDN), (R0, R1)
    outer = ((0,), lambda i: jnp.where(i < 2, 1 + i, 25 + i), 4)
    sweep((A_0, A_1), (B_0, B_1), A0, RD, FX, FY, FZ, (((1,), 2, D + 2), outer))
    sweep((B_0, B_1), (O_0, O_1), A0, RD, FX, FY, FZ, (INNER, NEXT))

    lane8 = lax.broadcasted_iota(jnp.int32, (8, 128), 1)
    row8 = lax.broadcasted_iota(jnp.int32, (8, 128), 0)

    def plane_raw(z, carry):
        p = z + 3
        ra = {}
        last = None
        for k in range(NK):
            sl = tile_at(k)
            a, side, t, edge = O_0[p, :, sl], O_1[p, :, sl], T[z + 1, :, sl], TH[z, :, sl]
            an = left_shift(lambda m: O_0[p, :, tile_at(m)], k, lane8, ra)
            if k == NK - 1:
                an = jnp.where(lane8 == 127, 0.0, an)
            px = (a - an) * DX[z, :, sl]
            back = pltpu.roll(px, 1, 1)
            pair = px + jnp.where(lane8 == 0, a * t if last is None else last, back)
            last = back
            au = jnp.where(row8 == 7, rot(side, -1), rot(a, -1))
            ad = jnp.where(row8 == 0, rot(side, 1), rot(a, 1))
            tu, td = jnp.where(row8 == 7, edge, rot(t, -1)), jnp.where(row8 == 0, edge, rot(t, 1))
            pair = pair + ((a - au) * (t - tu) + (a - ad) * (t - td))
            pair = pair + (a - O_0[p + 1, :, sl]) * (t - T[z + 2, :, sl])
            pair = pair + (a - O_0[p - 1, :, sl]) * (t - T[z, :, sl])
            R[pl.ds(pl.multiple_of(z * 8, 8), 8), sl] = pair * SC[z, :, sl]
        return carry

    lax.fori_loop(0, D, plane_raw, 0, unroll=2)

    i = lax.broadcasted_iota(jnp.int32, (512, 256), 0) - 128
    j = lax.broadcasted_iota(jnp.int32, (512, 256), 1)
    weights = jnp.maximum(RADIUS + 1 - jnp.abs(i - j), 0).astype(F32).astype(BF16)
    for n in range(X // 256):
        low, high = max(256 * n - 128, 0), min(256 * n + 384, X)
        x = R[:, low:high]
        w = weights[low - (256 * n - 128) : high - (256 * n - 128)]
        xh = x.astype(BF16)
        xl = (x - xh.astype(F32)).astype(BF16)
        y = jnp.dot(xh, w, preferred_element_type=F32) + jnp.dot(xl, w, preferred_element_type=F32)
        for h in range(2):
            part, m = y[:, 128 * h : 128 * h + 128], (2 * n + h) % HALF
            if n < X // 512:
                send[m] = part[0 : 4 * D]
                send[HALF + m] = part[4 * D :]
            else:
                late[m] = part
                layers = [part[8 * z : 8 * z + 8] for z in range(D)]
                sums[0, 8 * m : 8 * m + 8] = sum(layers)
                sums[1, 8 * m : 8 * m + 8] = sum(float(z) * layers[z] for z in range(1, D))
        if n == X // 512 - 1:
            copy = pltpu.make_async_copy(send, send_any, sems.at[0])
            copy.start()
    copy.wait()


def filter_y(x_ref, out_any, out, sems):
    i = lax.broadcasted_iota(jnp.int32, (128, 128), 0)
    j = lax.broadcasted_iota(jnp.int32, (128, 128), 1)
    w = jnp.maximum(RADIUS + 1 - jnp.abs(i - j), 0).astype(F32).astype(BF16)
    copies = []
    for z in range(D // 2):
        x = x_ref[:, 8 * z : 8 * z + 8, :].reshape(128, 128)
        xh = x.astype(BF16)
        xl = (x - xh.astype(F32)).astype(BF16)
        y = jnp.dot(w, xh, preferred_element_type=F32) + jnp.dot(w, xl, preferred_element_type=F32)
        out[:, 8 * z : 8 * z + 8, :] = y.reshape(16, 8, 128)
        if z % 4 == 3:
            part = pl.ds(8 * (z - 3), 32)
            copies.append(pltpu.make_async_copy(out.at[:, part], out_any.at[:, part], sems.at[z // 4]))
            copies[-1].start()
    for copy in copies:
        copy.wait()


def whole_layer(ref, m, z):
    return ref[m, 8 * z : 8 * z + 8, :]


def split_layer(ref, m, z):
    return ref[HALF * (z // (D // 2)) + m, 8 * (z % (D // 2)) : 8 * (z % (D // 2)) + 8, :]


def layer_sums(x_ref, sums):
    def chunk(m, carry):
        layers = [split_layer(x_ref, m, z) for z in range(D)]
        sl = pl.ds(pl.multiple_of(m * 8, 8), 8)
        sums[0, sl] = sum(layers)
        sums[1, sl] = sum(float(z) * layers[z] for z in range(1, D))
        return carry

    lax.fori_loop(0, HALF, chunk, 0)


def filter_z(load, m, own, up, down, up2, down2, store):
    sl = pl.ds(pl.multiple_of(m * 8, 8), 8)
    u0, u1, d0, d1 = up[0, sl, :], up[1, sl, :], down[0, sl, :], down[1, sl, :]
    suffix = load(down2, m, D - 1)
    total = suffix
    far = [None] * D
    far[D - 1] = total
    for z in range(D - 2, -1, -1):
        suffix = suffix + load(down2, m, z)
        total = total + suffix
        far[z] = total
    sum_own = load(own, m, 0)
    distance = jnp.zeros_like(sum_own)
    for z in range(1, D):
        x = load(own, m, z)
        sum_own = sum_own + x
        distance = distance + float(z) * x
    near = (25.0 * (u0 + d0) + (d1 - u1)) + float(RADIUS + 1) * sum_own
    slope = u0 - d0
    prefix_own = jnp.zeros_like(sum_own)
    prefix_up = jnp.zeros_like(sum_own)
    total_up = jnp.zeros_like(sum_own)
    for z in range(D):
        prefix_up = prefix_up + load(up2, m, z)
        total_up = total_up + prefix_up
        store(z, (near - distance) + (total_up + far[z]))
        prefix_own = prefix_own + load(own, m, z)
        distance = distance + (2.0 * prefix_own - sum_own)
        near = near + slope


def filter_z_late(own, up, down, up2, down2, out):
    def chunk(m, carry):
        def store(z, value):
            out[HALF * (z // (D // 2)) + m, 8 * (z % (D // 2)) : 8 * (z % (D // 2)) + 8, :] = value

        filter_z(whole_layer, m, own, up, down, up2, down2, store)
        return carry

    lax.fori_loop(0, HALF, chunk, 0)


def finish_early(info, own, up, down, up2, down2, out_hbm, out, sem):
    def chunk(m, carry):
        column = pl.ds(pl.multiple_of(m * 128, 128), 128)
        scale = REPORT_SCALE * info[m // 2].astype(F32)

        def store(z, value):
            out[z, :, column] = value * scale

        filter_z(split_layer, m, own, up, down, up2, down2, store)
        return carry

    lax.fori_loop(0, HALF, chunk, 0)
    copy = pltpu.make_async_copy(out, out_hbm.at[:, :, pl.ds(0, X // 2)], sem)
    copy.start()
    copy.wait()


def finish_late(info, late, half_done, out_hbm, out, sems):
    del half_done
    copies = []
    for part in range(2):
        for m in range(part * HALF // 2, (part + 1) * HALF // 2):
            scale = REPORT_SCALE * info[HALF // 2 + m // 2].astype(F32)
            for z in range(D):
                out[z, :, tile_at(m)] = split_layer(late, m, z) * scale
        column = pl.ds(part * X // 4, X // 4)
        target = pl.ds(X // 2 + part * X // 4, X // 4)
        copies.append(pltpu.make_async_copy(out.at[:, :, column], out_hbm.at[:, :, target], sems.at[part]))
        copies[-1].start()
    for copy in copies:
        copy.wait()


def kernel_call(body, ins, outs, scratch=(), scalars=0, limit=60, sems=0):
    vmem = pl.BlockSpec(memory_space=pltpu.VMEM)
    smem = pl.BlockSpec(memory_space=pltpu.SMEM)
    return pl.pallas_call(
        body,
        out_shape=[jax.ShapeDtypeStruct(s, F32) for s in outs],
        in_specs=[smem] * scalars + [vmem] * (len(ins) - scalars),
        out_specs=([pl.BlockSpec(memory_space=pl.ANY)] if sems else [vmem]) + [vmem] * (len(outs) - 1),
        scratch_shapes=[pltpu.VMEM(s, F32) for s in scratch] + ([pltpu.SemaphoreType.DMA((sems,))] if sems else []),
        compiler_params=pltpu.CompilerParams(vmem_limit_bytes=limit * MIB),
    )(*ins)


def moved(x, dz, dy):
    pairs = []
    for g in range(16):
        for b in range(16):
            if 0 <= g + dz < 16 and 0 <= b + dy < 16:
                pairs.append(((g + dz) * 16 + b + dy, g * 16 + b))
    return lax.ppermute(x, ("grp", "blk"), pairs)


def local(solid, thermal, target, coolant, switch):
    info = switch.reshape(8)
    block = (D, 8, X)
    near = tile_shape(D // 2)
    ylo, yhi, zlo, zhi = pl.pallas_call(
        pack_first,
        out_shape=[jax.ShapeDtypeStruct(shape, F32) for shape in (near, near, tile_shape(8), tile_shape(8))],
        in_specs=[pl.BlockSpec(memory_space=pltpu.HBM)] * 4,
        out_specs=[pl.BlockSpec(memory_space=pltpu.HBM)] * 4,
        scratch_shapes=[pltpu.VMEM(block, F32)] * 3
        + [pltpu.VMEM(near, F32)] * 2
        + [pltpu.VMEM(tile_shape(8), F32)] * 2
        + [pltpu.SemaphoreType.DMA((3, D // STEP)), pltpu.SemaphoreType.DMA((2,)), pltpu.SemaphoreType.DMA((3, D // STEP))],
        compiler_params=pltpu.CompilerParams(vmem_limit_bytes=52 * MIB),
    )(solid, thermal, target, coolant)
    yhi, ylo = moved(ylo, 0, 1), moved(yhi, 0, -1)
    zlo, zhi = moved(zhi, -1, 0), moved(zlo, 1, 0)
    ext, flat = (E, 8, X), (D * 8, X)
    rows = (NK, D * 8, 128)
    c, b, fx, fz, dp, mlo, mhi, rs, fs = kernel_call(
        build_own, (solid, target, coolant, zlo, zhi),
        [ext] * 5 + [tile_shape(5)] * 2 + [rows] * 2, [rows], limit=8,
    )
    hlo, hhi = kernel_call(pack_third, (thermal, rs, fs), [tile_shape(9)] * 2, limit=8)
    mhi, mlo = moved(mlo, 0, 1), moved(mhi, 0, -1)
    hhi, hlo = moved(hlo, 0, 1), moved(hhi, 0, -1)
    a, y2lo, y2hi, w3lo, w3hi, z2lo, z2hi, *fields = kernel_call(
        sweeps_first, (c, b, fx, fz, dp, yhi, ylo, mhi, mlo),
        [block, tile_shape(6), tile_shape(6)] + [tile_shape(3)] * 4 + [ext] * 8, [ext] * 5, limit=14,
    )
    y2hi, y2lo = moved(y2lo, 0, 1), moved(y2hi, 0, -1)
    z2lo, z2hi = moved(z2hi, -1, 0), moved(z2lo, 1, 0)
    fy0, rd0, r0, fx1, fy1, fz1, rd1, r1 = fields
    rd1, fy1, th = kernel_call(unpack_third, (hhi, hlo, rd1, fy1), [ext, ext, block], limit=8)
    clo, chi = kernel_call(pack_corners_second, (z2lo, z2hi, w3lo, w3hi), [tile_shape(5)] * 2, limit=8)
    e_hi, e_lo = moved(clo, 0, 1), moved(chi, 0, -1)
    parts, wide, small = (2 * HALF, D * 4, 128), (HALF, D * 8, 128), (2, HALF * 8, 128)
    a_0, a_1, b_0, *terms = kernel_call(
        third_sweep_own,
        (info, solid, thermal, zlo, zhi, a, fx, fz, fy0, fy1, rd0, r0, y2hi, y2lo, z2lo, z2hi),
        [ext] * 3 + [(D + 2, 8, X), block, block], scalars=1, limit=8,
    )
    send, late, sums = kernel_call(
        sweeps_second,
        (th, a_0, a_1, b_0, *terms, fx, fz, fy0, rd0, r0, fx1, fy1, fz1, rd1, r1, e_hi, e_lo),
        [parts, wide, small], [ext] * 4 + [flat, parts], limit=13, sems=1,
    )

    def exchanged(x):
        return lax.all_to_all(x, "blk", split_axis=0, concat_axis=0, tiled=True)

    columns = exchanged(send)
    up2, down2 = moved(late, 2, 0), moved(late, -2, 0)
    up, down = moved(sums, 1, 0), moved(sums, -1, 0)
    (columns,) = kernel_call(filter_y, (columns,), [parts], [parts], limit=8, sems=3)
    early = exchanged(columns)
    (late,) = kernel_call(filter_z_late, (late, up, down, up2, down2), [parts], limit=8)
    late = exchanged(late)
    up2, down2 = moved(early, 2, 0), moved(early, -2, 0)
    (sums,) = kernel_call(layer_sums, (early,), [small], limit=8)
    up, down = moved(sums, 1, 0), moved(sums, -1, 0)
    (late,) = kernel_call(filter_y, (late,), [parts], [parts], limit=8, sems=3)
    late = exchanged(late)
    smem, vmem, anywhere = (pl.BlockSpec(memory_space=space) for space in (pltpu.SMEM, pltpu.VMEM, pl.ANY))
    half = pltpu.VMEM((D, 8, X // 2), F32)
    out = pl.pallas_call(
        finish_early,
        out_shape=jax.ShapeDtypeStruct(block, F32),
        in_specs=[smem] + [vmem] * 5,
        out_specs=anywhere,
        scratch_shapes=[half, pltpu.SemaphoreType.DMA(())],
        compiler_params=pltpu.CompilerParams(vmem_limit_bytes=8 * MIB),
    )(info, early, up, down, up2, down2)
    return pl.pallas_call(
        finish_late,
        out_shape=jax.ShapeDtypeStruct(block, F32),
        in_specs=[smem, vmem, anywhere],
        out_specs=anywhere,
        scratch_shapes=[half, pltpu.SemaphoreType.DMA((2,))],
        input_output_aliases={2: 0},
        compiler_params=pltpu.CompilerParams(vmem_limit_bytes=8 * MIB),
    )(info, late, out)


def tile_shape(n):
    return (n, 8, X)


def solution(mesh):
    spec = P("grp", "blk", None)
    return jax.shard_map(
        local, mesh=mesh, in_specs=(spec,) * 5, out_specs=spec, check_vma=False
    )
```

```python
import jax
import jax.numpy as jnp
from jax import lax
from jax.experimental import pallas as pl
from jax.experimental.pallas import tpu as pltpu
from jax.sharding import PartitionSpec as P

RADIUS = 48
COND_FLOOR = 0.001
REPORT_SCALE = 100.0
D, S, X = 24, 8, 2048
NK = X // 128
E = D + 6
STEP = 8
HALF = NK // 2
F32 = jnp.float32
BF16 = jnp.bfloat16
MIB = 1024 * 1024


def rows_of(shape):
    return lax.broadcasted_iota(jnp.int32, shape, 0)


def rot(tile, shift):
    shift = shift % 8
    return tile if shift == 0 else pltpu.roll(tile, shift, 0)


def conduct_of(solid):
    return COND_FLOOR + (1.0 - COND_FLOOR) * (solid * solid * solid)


def pack_first(s_hbm, t_hbm, b_hbm, k_hbm, ylo_hbm, yhi_hbm, zlo_hbm, zhi_hbm,
               s_ref, b_ref, k_ref, ylo, yhi, zlo, zhi, sems, edge_sems, out_sems):
    pairs = ((s_hbm, s_ref), (b_hbm, b_ref), (k_hbm, k_ref))
    copies = [
        [
            pltpu.make_async_copy(src.at[pl.ds(i * STEP, STEP)], dst.at[pl.ds(i * STEP, STEP)], sems.at[n, i])
            for n, (src, dst) in enumerate(pairs)
        ]
        for i in range(D // STEP)
    ]
    edges = [
        pltpu.make_async_copy(t_hbm.at[0], zlo.at[7], edge_sems.at[0]),
        pltpu.make_async_copy(t_hbm.at[D - 1], zhi.at[7], edge_sems.at[1]),
    ]
    for group in copies:
        for copy in group:
            copy.start()
    for copy in edges:
        copy.start()
    r = rows_of((8, X))
    outs = []
    for i, group in enumerate(copies):
        for copy in group:
            copy.wait()

        def two(m, carry):
            ce, co = conduct_of(s_ref[2 * m]), conduct_of(s_ref[2 * m + 1])
            be, bo, ke, ko = b_ref[2 * m], b_ref[2 * m + 1], k_ref[2 * m], k_ref[2 * m + 1]
            even = jnp.where(r < 2, ce, jnp.where(r == 2, rot(be, 2), rot(ke, 3)))
            odd = jnp.where(r < 6, rot(co, 4), jnp.where(r == 6, rot(bo, 6), rot(ko, 7)))
            ylo[m] = jnp.where(r < 4, even, odd)
            even = jnp.where(r > 1, rot(ce, 4), jnp.where(r == 1, rot(be, 2), rot(ke, 1)))
            odd = jnp.where(r > 5, co, jnp.where(r == 5, rot(bo, -2), rot(ko, -3)))
            yhi[m] = jnp.where(r < 4, even, odd)
            return carry

        half = STEP // 2
        lax.fori_loop(i * half, (i + 1) * half, two, 0)
        part = pl.ds(i * half, half)
        outs += [
            pltpu.make_async_copy(ylo.at[part], ylo_hbm.at[part], out_sems.at[0, i]),
            pltpu.make_async_copy(yhi.at[part], yhi_hbm.at[part], out_sems.at[1, i]),
        ]
        outs[-2].start()
        outs[-1].start()
    for copy in edges:
        copy.wait()
    for dst, at in ((zlo, lambda j: j), (zhi, lambda j: D - 1 - j)):
        for j in range(3):
            dst[j] = conduct_of(s_ref[at(j)])
        for j in range(2):
            dst[3 + j] = b_ref[at(j)]
            dst[5 + j] = k_ref[at(j)]
    outs += [
        pltpu.make_async_copy(zlo, zlo_hbm, out_sems.at[2, 0]),
        pltpu.make_async_copy(zhi, zhi_hbm, out_sems.at[2, 1]),
    ]
    outs[-2].start()
    outs[-1].start()
    for copy in outs:
        copy.wait()


def build_own(s_ref, b_ref, k_ref, zlo, zhi, C, B, FX, FZ, DP, mlo, mhi, RS, FS, AS):
    lane = lax.broadcasted_iota(jnp.int32, (8, 128), 1)
    row = lax.broadcasted_iota(jnp.int32, (8, 128), 0)

    def own(z, carry):
        C[z + 3] = conduct_of(s_ref[z])
        B[z + 3] = b_ref[z]
        DP[z + 3] = k_ref[z]
        return carry

    lax.fori_loop(0, D, own, 0)
    for src, at in ((zlo, lambda j: 2 - j), (zhi, lambda j: 27 + j)):
        for j in range(3):
            C[at(j)] = src[j]
        for j in range(2):
            B[at(j)] = src[3 + j]
            DP[at(j)] = src[5 + j]
    FZ[0] = C[0] + C[1]

    def plane(p, inner):
        rots, last = {}, None
        for k in range(NK):
            sl = tile_at(k)
            c = C[p, :, sl]
            nxt = left_shift(lambda m: C[p, :, tile_at(m)], k, lane, rots)
            fx = c + nxt
            if k == NK - 1:
                nxt = jnp.where(lane == 127, 0.0, nxt)
                fx = jnp.where(lane == 127, 0.0, fx)
            back = pltpu.roll(c, 1, 1)
            before = jnp.where(lane == 0, 0.0 if last is None else last, back)
            last = back
            up = jnp.where(row == 7, 0.0, pltpu.roll(c, 7, 0))
            down = jnp.where(row == 0, 0.0, pltpu.roll(c, 1, 0))
            cz = C[p + 1, :, sl]
            FX[p, :, sl] = fx
            FZ[p, :, sl] = c + cz
            coup = DP[p, :, sl]
            diag = coup + (3.0 * c + 0.5 * (nxt + before + up + down + cz + C[p - 1, :, sl]))
            diag = jnp.where(coup > 0.0, diag, 0.0)
            DP[p, :, sl] = diag
            if inner:
                at = pl.ds(pl.multiple_of((p - 3) * 8, 8), 8)
                rd = 1.0 / diag
                RS[k, at] = (1.0 / 3.0) * rd
                AS[k, at] = B[p, :, sl] * rd
                FS[k, at] = c + up

    def inside(p, carry):
        plane(p, True)
        return carry

    def outside(i, carry):
        plane(jnp.where(i < 2, 1 + i, 25 + i), False)
        return carry

    lax.fori_loop(3, E - 3, inside, 0, unroll=2)
    lax.fori_loop(0, 4, outside, 0)
    r = rows_of((8, X))
    for i, src in enumerate((zlo, zhi)):
        c1, c2, b1, k1 = src[0], src[1], src[3], src[5]
        mlo[i] = jnp.where(r < 2, c1, jnp.where(r == 2, rot(c2, 2), jnp.where(r == 3, rot(b1, 3), rot(k1, 4))))
        mhi[i] = jnp.where(r > 5, c1, jnp.where(r == 5, rot(c2, -2), jnp.where(r == 4, rot(b1, -3), rot(k1, -4))))
    for g in range(D // 8):
        for k in range(NK):
            sl = tile_at(k)
            mlo[2 + g, :, sl] = AS[k, pl.ds(64 * g + 1, 8, stride=8), :]
            mhi[2 + g, :, sl] = AS[k, pl.ds(64 * g + 6, 8, stride=8), :]


def pack_third(t_ref, RS, FS, hlo, hhi):
    r = rows_of((8, X))
    for g in range(D // 8):
        for k in range(NK):
            sl = tile_at(k)
            for n, (src, low, high) in enumerate(((RS, 1, 6), (FS, 1, 5))):
                hlo[3 * g + n, :, sl] = src[k, pl.ds(64 * g + low, 8, stride=8), :]
                hhi[3 * g + n, :, sl] = src[k, pl.ds(64 * g + high, 8, stride=8), :]
        low = high = t_ref[8 * g]
        high = rot(high, 1)
        for j in range(1, 8):
            t = t_ref[8 * g + j]
            low = jnp.where(r == j, rot(t, j), low)
            high = jnp.where(r == j, rot(t, j - 7), high)
        hlo[3 * g + 2] = low
        hhi[3 * g + 2] = high


def pack_corners_second(zlo, zhi, w3lo, w3hi, lo, hi):
    r = rows_of((8, X))
    for g in range(D // 8):
        lo[2 + g] = w3lo[g]
        hi[2 + g] = w3hi[g]
    for i, src in enumerate((zlo, zhi)):
        lo[i] = jnp.where(r < 2, src[0], rot(src[1], 2))
        hi[i] = jnp.where(r > 5, src[0], rot(src[1], -2))


def assemble(yhi, ylo, mhi, mlo, C, B, K):
    r = rows_of((8, X))
    zero = jnp.zeros((8, X), F32)

    def two(m, carry):
        h, l = yhi[m], ylo[m]
        p = 2 * m + 3
        C[p] = jnp.where(r < 2, h, jnp.where(r > 5, rot(l, 4), 0.0))
        B[p] = jnp.where(r == 0, rot(h, -2), jnp.where(r == 7, rot(l, 6), 0.0))
        K[p] = jnp.where(r == 0, rot(h, -3), jnp.where(r == 7, rot(l, 7), 0.0))
        C[p + 1] = jnp.where(r < 2, rot(h, -4), jnp.where(r > 5, l, 0.0))
        B[p + 1] = jnp.where(r == 0, rot(h, -6), jnp.where(r == 7, rot(l, 2), 0.0))
        K[p + 1] = jnp.where(r == 0, rot(h, -7), jnp.where(r == 7, rot(l, 3), 0.0))
        return carry

    lax.fori_loop(0, D // 2, two, 0)
    for i, at in ((0, lambda j: 2 - j), (1, lambda j: 27 + j)):
        h, l = mhi[i], mlo[i]
        C[at(0)] = jnp.where(r < 2, h, jnp.where(r > 5, l, 0.0))
        C[at(1)] = jnp.where(r == 0, rot(h, -2), jnp.where(r == 7, rot(l, 2), 0.0))
        C[at(2)] = zero
        B[at(0)] = jnp.where(r == 0, rot(h, -3), jnp.where(r == 7, rot(l, 3), 0.0))
        K[at(0)] = jnp.where(r == 0, rot(h, -4), jnp.where(r == 7, rot(l, 4), 0.0))
        B[at(1)] = zero
        K[at(1)] = zero


def tile_at(k):
    return slice(128 * k, 128 * k + 128)


def left_shift(load, k, lane, rots):
    for m in (k, (k + 1) % NK):
        if m not in rots:
            rots[m] = pltpu.roll(load(m), 127, 1)
    return jnp.where(lane == 127, rots[(k + 1) % NK], rots[k])


def build(C, B, DP, A, A0, RD, FX, FY, FZ):
    lane = lax.broadcasted_iota(jnp.int32, (8, 128), 1)
    row = lax.broadcasted_iota(jnp.int32, (8, 128), 0)
    top, bottom = row == 0, row == 7

    def plane(p, carry):
        rots, last = {}, None
        for k in range(NK):
            sl = tile_at(k)
            own, c = C[0][p, :, sl], C[1][p, :, sl]
            own_up, own_down = pltpu.roll(own, 7, 0), pltpu.roll(own, 1, 0)
            up, down = pltpu.roll(c, 7, 0), pltpu.roll(c, 1, 0)
            FY[0][p, :, sl] = own + jnp.where(bottom, up, own_up)
            beside = jnp.where(bottom, up, jnp.where(top, down, 0.0))
            up, down = jnp.where(bottom, own_up, up), jnp.where(top, own_down, down)
            FY[1][p, :, sl] = c + up
            part = DP[p, :, sl]
            rd = jnp.where(part > 0.0, 1.0 / jnp.where(part > 0.0, part + 0.5 * beside, 1.0), 0.0)
            a = B[p, :, sl] * rd
            A[0][p, :, sl] = a
            A0[0][p, :, sl] = (2.0 / 3.0) * a
            RD[0][p, :, sl] = (1.0 / 3.0) * rd

            nxt = left_shift(lambda m: C[1][p, :, tile_at(m)], k, lane, rots)
            fx = c + nxt
            if k == NK - 1:
                nxt = jnp.where(lane == 127, 0.0, nxt)
                fx = jnp.where(lane == 127, 0.0, fx)
            back = pltpu.roll(c, 1, 1)
            before = jnp.where(lane == 0, 0.0 if last is None else last, back)
            last = back
            cz = C[1][p + 1, :, sl]
            FX[1][p, :, sl] = fx
            FZ[1][p, :, sl] = c + cz
            coup = RD[1][p, :, sl]
            diag = coup + (3.0 * c + 0.5 * (nxt + before + up + down + cz + C[1][p - 1, :, sl]))
            rd = jnp.where(coup > 0.0, 1.0 / jnp.where(coup > 0.0, diag, 1.0), 0.0)
            a = A[1][p, :, sl] * rd
            A[1][p, :, sl] = a
            A0[1][p, :, sl] = (2.0 / 3.0) * a
            RD[1][p, :, sl] = (1.0 / 3.0) * rd
        return carry

    lax.fori_loop(1, E - 1, plane, 0, unroll=4)


def unpack_third(hhi, hlo, RD, FY, RDN, FYN, TH):
    r = rows_of((8, X))

    def group(g, carry):
        for j in range(8):
            p = 3 + 8 * g + j
            RDN[p] = jnp.where(r == 1, rot(hhi[3 * g], 1 - j), jnp.where(r == 6, rot(hlo[3 * g], 6 - j), RD[p]))
            FYN[p] = jnp.where(r == 1, rot(hhi[3 * g + 1], 1 - j), jnp.where(r == 5, rot(hlo[3 * g + 1], 5 - j), FY[p]))
            TH[8 * g + j] = jnp.where(r == 7, rot(hhi[3 * g + 2], 7 - j), rot(hlo[3 * g + 2], -j))
        return carry

    lax.fori_loop(0, D // 8, group, 0)
    for p in (0, 1, 2, 27, 28, 29):
        RDN[p] = RD[p]
        FYN[p] = FY[p]


def sweep(A, OUT, A0, RD, FX, FY, FZ, runs):
    lane = lax.broadcasted_iota(jnp.int32, (8, 128), 1)
    row = lax.broadcasted_iota(jnp.int32, (8, 128), 0)
    first, last, top, bottom = lane == 0, lane == 127, row == 0, row == 7

    def plane(p, tiles):
        ahead, back = {}, {}

        def shift(m):
            if (m, tiles[0]) in ahead:
                return
            sl = tile_at(m)
            for h in tiles:
                a = A[h][p, :, sl]
                ahead[m, h] = pltpu.roll(a, 127, 1)
                back[m, h] = pltpu.roll(FX[h][p, :, sl] * a, 1, 1)

        shift(NK - 1)
        shift(0)
        for k in range(NK):
            sl = tile_at(k)
            shift((k + 1) % NK)
            a = [A[h][p, :, sl] for h in (0, 1)]
            fy = [FY[h][p, :, sl] for h in (0, 1)]
            up = [pltpu.roll(x, 7, 0) for x in a]
            down = [pltpu.roll(f * x, 1, 0) for f, x in zip(fy, a)]
            for h in tiles:
                flux = FX[h][p, :, sl] * jnp.where(last, ahead[(k + 1) % NK, h], ahead[k, h])
                flux = flux + jnp.where(first, back[(k - 1) % NK, h], back[k, h])
                flux = flux + (fy[h] * jnp.where(bottom, up[1 - h], up[h]) + jnp.where(top, down[1 - h], down[h]))
                flux = flux + (FZ[h][p, :, sl] * A[h][p + 1, :, sl] + FZ[h][p - 1, :, sl] * A[h][p - 1, :, sl])
                OUT[h][p, :, sl] = (1.0 / 3.0) * a[h] + (A0[h][p, :, sl] + RD[h][p, :, sl] * flux)

    for tiles, low, count in runs:
        group = 6 if count % 6 == 0 else 2

        def planes(i, carry):
            for q in range(group):
                plane(low + group * i + q, tiles)
            return carry

        if isinstance(low, int):
            lax.fori_loop(0, count // group, planes, 0)
        else:

            def single(i, carry):
                plane(low(i), tiles)
                return carry

            lax.fori_loop(0, count, single, 0)


INNER = ((0, 1), 3, D)
OWN = ((0,), 3, D)
NEXT = ((0,), lambda i: 2 + (D + 1) * i, 2)


def sweeps_first(C0, B0, FX0, FZ0, DP, yhi, ylo, mhi, mlo,
                 a_out, y2lo, y2hi, w3lo, w3hi, z2lo, z2hi, FY0, RD0, R0, FX1, FY1, FZ1, RD1, R1, C1, A_0, A_1, O_0, O_1):
    FX, FY, FZ, RD, A0, A, OUT = (FX0, FX1), (FY0, FY1), (FZ0, FZ1), (RD0, RD1), (R0, R1), (A_0, A_1), (O_0, O_1)
    assemble(yhi, ylo, mhi, mlo, C1, A_1, RD1)
    build((C0, C1), B0, DP, A, A0, RD, FX, FY, FZ)
    r = rows_of((8, X))

    def second_rows(g, carry):
        for j in range(8):
            p = 3 + 8 * g + j
            a = jnp.where(r == 1, rot(mhi[2 + g], 1 - j), jnp.where(r == 6, rot(mlo[2 + g], 6 - j), A_1[p]))
            A_1[p] = a
            R1[p] = (2.0 / 3.0) * a
        return carry

    lax.fori_loop(0, D // 8, second_rows, 0)
    sweep(A, OUT, A0, RD, FX, FY, FZ, (INNER, NEXT))
    sweep(OUT, A, A0, RD, FX, FY, FZ, (OWN,))
    A = A_0

    def copy(z, carry):
        a_out[z] = A[z + 3]
        return carry

    lax.fori_loop(0, D, copy, 0)

    def group(g, carry):
        for i in range(2):
            low, high = None, None
            for j in range(4):
                a = A[8 * g + 4 * i + j + 3]
                mask = (r >= 2 * j) & (r < 2 * j + 2)
                low = rot(a, 2 * j) if low is None else jnp.where(mask, rot(a, 2 * j), low)
                high = rot(a, 2 * j - 6) if high is None else jnp.where(mask, rot(a, 2 * j - 6), high)
            y2lo[2 * g + i] = low
            y2hi[2 * g + i] = high
        low, high = None, None
        for j in range(8):
            a = A[8 * g + j + 3]
            low = rot(a, j - 2) if low is None else jnp.where(r == j, rot(a, j - 2), low)
            high = rot(a, j - 5) if high is None else jnp.where(r == j, rot(a, j - 5), high)
        w3lo[g] = low
        w3hi[g] = high
        return carry

    lax.fori_loop(0, D // 8, group, 0)
    for j in range(3):
        z2lo[j] = A[3 + j]
        z2hi[j] = A[26 - j]


def tri(u):
    m = jnp.maximum(RADIUS - u, 0)
    return m * (m + 1) // 2


def inv_cover(position, length):
    total = (RADIUS + 1) ** 2 - tri(position) - tri(length - 1 - position)
    return 1.0 / total.astype(F32)


def third_sweep_own(info, s_ref, t_ref, zlo, zhi, a_in, FX0, FZ0, FY0, FYN, RD0, R0, y2hi, y2lo, z2lo, z2hi,
                    A_0, A_1, B_0, T, DX, SC):
    r = rows_of((8, X))

    def group(g, carry):
        for j in range(8):
            z = 8 * g + j
            A_0[z + 3] = a_in[z]
            tile, at = 2 * g + j // 4, 2 * (j % 4)
            A_1[z + 3] = jnp.where(r < 2, rot(y2hi[tile], -at), jnp.where(r > 5, rot(y2lo[tile], 6 - at), 0.0))
        return carry

    lax.fori_loop(0, 3, group, 0)
    for src, at in ((z2lo, lambda j: 2 - j), (z2hi, lambda j: 27 + j)):
        for j in range(3):
            A_0[at(j)] = src[j]
    for p in (0, 1, 2, 27, 28, 29):
        A_1[p] = jnp.zeros((8, X), F32)
    sweep((A_0, A_1), (B_0,), (R0,), (RD0,), (FX0,), (FY0, FYN), (FZ0,), (OWN,))

    lane8 = lax.broadcasted_iota(jnp.int32, (8, 128), 1)
    row8 = lax.broadcasted_iota(jnp.int32, (8, 128), 0)
    cover_y = inv_cover(lax.axis_index("blk") * S + row8, 16 * S)
    base_z = lax.axis_index("grp") * D
    factor = -0.5 * 3.0 * (1.0 - COND_FLOOR)

    def plane_t(z, carry):
        base = cover_y * inv_cover(base_z + z + jnp.zeros((8, 128), jnp.int32), 16 * D) * factor
        rt = {}
        for k in range(NK):
            sl = tile_at(k)
            t = t_ref[z, :, sl]
            tn = left_shift(lambda m: t_ref[z, :, tile_at(m)], k, lane8, rt)
            if k == NK - 1:
                tn = jnp.where(lane8 == 127, 0.0, tn)
            T[z + 1, :, sl] = t
            DX[z, :, sl] = t - tn
            s = s_ref[z, :, sl]
            scale = base * info[k // 2].astype(F32)
            if k in (0, NK - 1):
                scale = scale * inv_cover(lane8 + 128 * k, X)
            else:
                scale = scale * (1.0 / float((RADIUS + 1) ** 2))
            SC[z, :, sl] = (s * s) * scale
        return carry

    lax.fori_loop(0, D, plane_t, 0, unroll=2)

    T[0] = zlo[7]
    T[D + 1] = zhi[7]


def sweeps_second(TH, A_0, A_in, B_in, T, DX, SC, FX0, FZ0, FY0, RD0, R0, FX1, FYN, FZ1, RDN, R1,
                  e_hi, e_lo, send_any, late, sums, A_1, B_0, B_1, O_0, R, send, sems):
    O_1 = A_1
    r = rows_of((8, X))

    def group(g, carry):
        for j in range(8):
            p = 8 * g + j + 3
            A_1[p] = jnp.where(r == 2, rot(e_hi[2 + g], 2 - j), jnp.where(r == 5, rot(e_lo[2 + g], 5 - j), A_in[p]))
            B_0[p] = B_in[p]
        return carry

    lax.fori_loop(0, 3, group, 0)
    for i, at in ((0, lambda j: 2 - j), (1, lambda j: 27 + j)):
        h, l = e_hi[i], e_lo[i]
        A_1[at(0)] = jnp.where(r < 2, h, jnp.where(r > 5, l, 0.0))
        A_1[at(1)] = jnp.where(r == 0, rot(h, -2), jnp.where(r == 7, rot(l, 2), 0.0))
    FX, FY, FZ, RD, A0 = (FX0, FX1), (FY0, FYN), (FZ0, FZ1), (RD0, RDN), (R0, R1)
    outer = ((0,), lambda i: jnp.where(i < 2, 1 + i, 25 + i), 4)
    sweep((A_0, A_1), (B_0, B_1), A0, RD, FX, FY, FZ, (((1,), 2, D + 2), outer))
    sweep((B_0, B_1), (O_0, O_1), A0, RD, FX, FY, FZ, (INNER, NEXT))

    lane8 = lax.broadcasted_iota(jnp.int32, (8, 128), 1)
    row8 = lax.broadcasted_iota(jnp.int32, (8, 128), 0)

    def plane_raw(z, carry):
        p = z + 3
        ra = {}
        last = None
        for k in range(NK):
            sl = tile_at(k)
            a, side, t, edge = O_0[p, :, sl], O_1[p, :, sl], T[z + 1, :, sl], TH[z, :, sl]
            an = left_shift(lambda m: O_0[p, :, tile_at(m)], k, lane8, ra)
            if k == NK - 1:
                an = jnp.where(lane8 == 127, 0.0, an)
            px = (a - an) * DX[z, :, sl]
            back = pltpu.roll(px, 1, 1)
            pair = px + jnp.where(lane8 == 0, a * t if last is None else last, back)
            last = back
            au = jnp.where(row8 == 7, rot(side, -1), rot(a, -1))
            ad = jnp.where(row8 == 0, rot(side, 1), rot(a, 1))
            tu, td = jnp.where(row8 == 7, edge, rot(t, -1)), jnp.where(row8 == 0, edge, rot(t, 1))
            pair = pair + ((a - au) * (t - tu) + (a - ad) * (t - td))
            pair = pair + (a - O_0[p + 1, :, sl]) * (t - T[z + 2, :, sl])
            pair = pair + (a - O_0[p - 1, :, sl]) * (t - T[z, :, sl])
            R[pl.ds(pl.multiple_of(z * 8, 8), 8), sl] = pair * SC[z, :, sl]
        return carry

    lax.fori_loop(0, D, plane_raw, 0, unroll=2)

    i = lax.broadcasted_iota(jnp.int32, (512, 256), 0) - 128
    j = lax.broadcasted_iota(jnp.int32, (512, 256), 1)
    weights = jnp.maximum(RADIUS + 1 - jnp.abs(i - j), 0).astype(F32).astype(BF16)
    for n in range(X // 256):
        low, high = max(256 * n - 128, 0), min(256 * n + 384, X)
        x = R[:, low:high]
        w = weights[low - (256 * n - 128) : high - (256 * n - 128)]
        xh = x.astype(BF16)
        xl = (x - xh.astype(F32)).astype(BF16)
        y = jnp.dot(xh, w, preferred_element_type=F32) + jnp.dot(xl, w, preferred_element_type=F32)
        for h in range(2):
            part, m = y[:, 128 * h : 128 * h + 128], (2 * n + h) % HALF
            if n < X // 512:
                send[m] = part[0 : 4 * D]
                send[HALF + m] = part[4 * D :]
            else:
                late[m] = part
                layers = [part[8 * z : 8 * z + 8] for z in range(D)]
                sums[0, 8 * m : 8 * m + 8] = sum(layers)
                sums[1, 8 * m : 8 * m + 8] = sum(float(z) * layers[z] for z in range(1, D))
        if n == X // 512 - 1:
            copy = pltpu.make_async_copy(send, send_any, sems.at[0])
            copy.start()
    copy.wait()


def filter_y(x_ref, out_any, out, sems):
    i = lax.broadcasted_iota(jnp.int32, (128, 128), 0)
    j = lax.broadcasted_iota(jnp.int32, (128, 128), 1)
    w = jnp.maximum(RADIUS + 1 - jnp.abs(i - j), 0).astype(F32).astype(BF16)
    copies = []
    for z in range(D // 2):
        x = x_ref[:, 8 * z : 8 * z + 8, :].reshape(128, 128)
        xh = x.astype(BF16)
        xl = (x - xh.astype(F32)).astype(BF16)
        y = jnp.dot(w, xh, preferred_element_type=F32) + jnp.dot(w, xl, preferred_element_type=F32)
        out[:, 8 * z : 8 * z + 8, :] = y.reshape(16, 8, 128)
        if z % 4 == 3:
            part = pl.ds(8 * (z - 3), 32)
            copies.append(pltpu.make_async_copy(out.at[:, part], out_any.at[:, part], sems.at[z // 4]))
            copies[-1].start()
    for copy in copies:
        copy.wait()


def whole_layer(ref, m, z):
    return ref[m, 8 * z : 8 * z + 8, :]


def split_layer(ref, m, z):
    return ref[HALF * (z // (D // 2)) + m, 8 * (z % (D // 2)) : 8 * (z % (D // 2)) + 8, :]


def layer_sums(x_ref, sums):
    def chunk(m, carry):
        layers = [split_layer(x_ref, m, z) for z in range(D)]
        sl = pl.ds(pl.multiple_of(m * 8, 8), 8)
        sums[0, sl] = sum(layers)
        sums[1, sl] = sum(float(z) * layers[z] for z in range(1, D))
        return carry

    lax.fori_loop(0, HALF, chunk, 0)


def filter_z(load, m, own, up, down, up2, down2, store):
    sl = pl.ds(pl.multiple_of(m * 8, 8), 8)
    u0, u1, d0, d1 = up[0, sl, :], up[1, sl, :], down[0, sl, :], down[1, sl, :]
    suffix = load(down2, m, D - 1)
    total = suffix
    far = [None] * D
    far[D - 1] = total
    for z in range(D - 2, -1, -1):
        suffix = suffix + load(down2, m, z)
        total = total + suffix
        far[z] = total
    sum_own = load(own, m, 0)
    distance = jnp.zeros_like(sum_own)
    for z in range(1, D):
        x = load(own, m, z)
        sum_own = sum_own + x
        distance = distance + float(z) * x
    near = (25.0 * (u0 + d0) + (d1 - u1)) + float(RADIUS + 1) * sum_own
    slope = u0 - d0
    prefix_own = jnp.zeros_like(sum_own)
    prefix_up = jnp.zeros_like(sum_own)
    total_up = jnp.zeros_like(sum_own)
    for z in range(D):
        prefix_up = prefix_up + load(up2, m, z)
        total_up = total_up + prefix_up
        store(z, (near - distance) + (total_up + far[z]))
        prefix_own = prefix_own + load(own, m, z)
        distance = distance + (2.0 * prefix_own - sum_own)
        near = near + slope


def filter_z_late(own, up, down, up2, down2, out):
    def chunk(m, carry):
        def store(z, value):
            out[HALF * (z // (D // 2)) + m, 8 * (z % (D // 2)) : 8 * (z % (D // 2)) + 8, :] = value

        filter_z(whole_layer, m, own, up, down, up2, down2, store)
        return carry

    lax.fori_loop(0, HALF, chunk, 0)


def finish_early(info, own, up, down, up2, down2, out_hbm, out, sem):
    def chunk(m, carry):
        column = pl.ds(pl.multiple_of(m * 128, 128), 128)
        scale = REPORT_SCALE * info[m // 2].astype(F32)

        def store(z, value):
            out[z, :, column] = value * scale

        filter_z(split_layer, m, own, up, down, up2, down2, store)
        return carry

    lax.fori_loop(0, HALF, chunk, 0)
    copy = pltpu.make_async_copy(out, out_hbm.at[:, :, pl.ds(0, X // 2)], sem)
    copy.start()
    copy.wait()


def finish_late(info, late, half_done, out_hbm, out, sems):
    del half_done
    copies = []
    for part in range(2):
        for m in range(part * HALF // 2, (part + 1) * HALF // 2):
            scale = REPORT_SCALE * info[HALF // 2 + m // 2].astype(F32)
            for z in range(D):
                out[z, :, tile_at(m)] = split_layer(late, m, z) * scale
        column = pl.ds(part * X // 4, X // 4)
        target = pl.ds(X // 2 + part * X // 4, X // 4)
        copies.append(pltpu.make_async_copy(out.at[:, :, column], out_hbm.at[:, :, target], sems.at[part]))
        copies[-1].start()
    for copy in copies:
        copy.wait()


def kernel_call(body, ins, outs, scratch=(), scalars=0, limit=60, sems=0):
    vmem = pl.BlockSpec(memory_space=pltpu.VMEM)
    smem = pl.BlockSpec(memory_space=pltpu.SMEM)
    return pl.pallas_call(
        body,
        out_shape=[jax.ShapeDtypeStruct(s, F32) for s in outs],
        in_specs=[smem] * scalars + [vmem] * (len(ins) - scalars),
        out_specs=([pl.BlockSpec(memory_space=pl.ANY)] if sems else [vmem]) + [vmem] * (len(outs) - 1),
        scratch_shapes=[pltpu.VMEM(s, F32) for s in scratch] + ([pltpu.SemaphoreType.DMA((sems,))] if sems else []),
        compiler_params=pltpu.CompilerParams(vmem_limit_bytes=limit * MIB),
    )(*ins)


def moved(x, dz, dy):
    pairs = []
    for g in range(16):
        for b in range(16):
            if 0 <= g + dz < 16 and 0 <= b + dy < 16:
                pairs.append(((g + dz) * 16 + b + dy, g * 16 + b))
    return lax.ppermute(x, ("grp", "blk"), pairs)


def local(solid, thermal, target, coolant, switch):
    info = switch.reshape(8)
    block = (D, 8, X)
    near = tile_shape(D // 2)
    ylo, yhi, zlo, zhi = pl.pallas_call(
        pack_first,
        out_shape=[jax.ShapeDtypeStruct(shape, F32) for shape in (near, near, tile_shape(8), tile_shape(8))],
        in_specs=[pl.BlockSpec(memory_space=pltpu.HBM)] * 4,
        out_specs=[pl.BlockSpec(memory_space=pltpu.HBM)] * 4,
        scratch_shapes=[pltpu.VMEM(block, F32)] * 3
        + [pltpu.VMEM(near, F32)] * 2
        + [pltpu.VMEM(tile_shape(8), F32)] * 2
        + [pltpu.SemaphoreType.DMA((3, D // STEP)), pltpu.SemaphoreType.DMA((2,)), pltpu.SemaphoreType.DMA((3, D // STEP))],
        compiler_params=pltpu.CompilerParams(vmem_limit_bytes=52 * MIB),
    )(solid, thermal, target, coolant)
    yhi, ylo = moved(ylo, 0, 1), moved(yhi, 0, -1)
    zlo, zhi = moved(zhi, -1, 0), moved(zlo, 1, 0)
    ext, flat = (E, 8, X), (D * 8, X)
    rows = (NK, D * 8, 128)
    c, b, fx, fz, dp, mlo, mhi, rs, fs = kernel_call(
        build_own, (solid, target, coolant, zlo, zhi),
        [ext] * 5 + [tile_shape(5)] * 2 + [rows] * 2, [rows], limit=8,
    )
    hlo, hhi = kernel_call(pack_third, (thermal, rs, fs), [tile_shape(9)] * 2, limit=8)
    mhi, mlo = moved(mlo, 0, 1), moved(mhi, 0, -1)
    hhi, hlo = moved(hlo, 0, 1), moved(hhi, 0, -1)
    a, y2lo, y2hi, w3lo, w3hi, z2lo, z2hi, *fields = kernel_call(
        sweeps_first, (c, b, fx, fz, dp, yhi, ylo, mhi, mlo),
        [block, tile_shape(6), tile_shape(6)] + [tile_shape(3)] * 4 + [ext] * 8, [ext] * 5, limit=14,
    )
    y2hi, y2lo = moved(y2lo, 0, 1), moved(y2hi, 0, -1)
    z2lo, z2hi = moved(z2hi, -1, 0), moved(z2lo, 1, 0)
    fy0, rd0, r0, fx1, fy1, fz1, rd1, r1 = fields
    rd1, fy1, th = kernel_call(unpack_third, (hhi, hlo, rd1, fy1), [ext, ext, block], limit=8)
    clo, chi = kernel_call(pack_corners_second, (z2lo, z2hi, w3lo, w3hi), [tile_shape(5)] * 2, limit=8)
    e_hi, e_lo = moved(clo, 0, 1), moved(chi, 0, -1)
    parts, wide, small = (2 * HALF, D * 4, 128), (HALF, D * 8, 128), (2, HALF * 8, 128)
    a_0, a_1, b_0, *terms = kernel_call(
        third_sweep_own,
        (info, solid, thermal, zlo, zhi, a, fx, fz, fy0, fy1, rd0, r0, y2hi, y2lo, z2lo, z2hi),
        [ext] * 3 + [(D + 2, 8, X), block, block], scalars=1, limit=8,
    )
    send, late, sums = kernel_call(
        sweeps_second,
        (th, a_0, a_1, b_0, *terms, fx, fz, fy0, rd0, r0, fx1, fy1, fz1, rd1, r1, e_hi, e_lo),
        [parts, wide, small], [ext] * 4 + [flat, parts], limit=13, sems=1,
    )

    def exchanged(x):
        return lax.all_to_all(x, "blk", split_axis=0, concat_axis=0, tiled=True)

    columns = exchanged(send)
    up2, down2 = moved(late, 2, 0), moved(late, -2, 0)
    up, down = moved(sums, 1, 0), moved(sums, -1, 0)
    (columns,) = kernel_call(filter_y, (columns,), [parts], [parts], limit=8, sems=3)
    early = exchanged(columns)
    (late,) = kernel_call(filter_z_late, (late, up, down, up2, down2), [parts], limit=8)
    late = exchanged(late)
    up2, down2 = moved(early, 2, 0), moved(early, -2, 0)
    (sums,) = kernel_call(layer_sums, (early,), [small], limit=8)
    up, down = moved(sums, 1, 0), moved(sums, -1, 0)
    (late,) = kernel_call(filter_y, (late,), [parts], [parts], limit=8, sems=3)
    late = exchanged(late)
    smem, vmem, anywhere = (pl.BlockSpec(memory_space=space) for space in (pltpu.SMEM, pltpu.VMEM, pl.ANY))
    half = pltpu.VMEM((D, 8, X // 2), F32)
    out = pl.pallas_call(
        finish_early,
        out_shape=jax.ShapeDtypeStruct(block, F32),
        in_specs=[smem] + [vmem] * 5,
        out_specs=anywhere,
        scratch_shapes=[half, pltpu.SemaphoreType.DMA(())],
        compiler_params=pltpu.CompilerParams(vmem_limit_bytes=8 * MIB),
    )(info, early, up, down, up2, down2)
    return pl.pallas_call(
        finish_late,
        out_shape=jax.ShapeDtypeStruct(block, F32),
        in_specs=[smem, vmem, anywhere],
        out_specs=anywhere,
        scratch_shapes=[half, pltpu.SemaphoreType.DMA((2,))],
        input_output_aliases={2: 0},
        compiler_params=pltpu.CompilerParams(vmem_limit_bytes=8 * MIB),
    )(info, late, out)


def tile_shape(n):
    return (n, 8, X)


def solution(mesh):
    spec = P("grp", "blk", None)
    return jax.shard_map(
        local, mesh=mesh, in_specs=(spec,) * 5, out_specs=spec, check_vma=False
    )
```

```python
import jax
import jax.numpy as jnp
from jax import lax
from jax.experimental import pallas as pl
from jax.experimental.pallas import tpu as pltpu
from jax.sharding import PartitionSpec as P

RADIUS = 48
COND_FLOOR = 0.001
REPORT_SCALE = 100.0
D, S, X = 24, 8, 2048
NK = X // 128
E = D + 6
STEP = 4
HALF = NK // 2
F32 = jnp.float32
BF16 = jnp.bfloat16
MIB = 1024 * 1024


def rows_of(shape):
    return lax.broadcasted_iota(jnp.int32, shape, 0)


def rot(tile, shift):
    shift = shift % 8
    return tile if shift == 0 else pltpu.roll(tile, shift, 0)


def conduct_of(solid):
    return COND_FLOOR + (1.0 - COND_FLOOR) * (solid * solid * solid)


def pack_first(s_hbm, t_hbm, b_hbm, k_hbm, ylo_hbm, yhi_hbm, zlo_hbm, zhi_hbm,
               s_ref, b_ref, k_ref, ylo, yhi, zlo, zhi, sems, edge_sems, out_sems):
    pairs = ((s_hbm, s_ref), (b_hbm, b_ref), (k_hbm, k_ref))
    copies = [
        [
            pltpu.make_async_copy(src.at[pl.ds(i * STEP, STEP)], dst.at[pl.ds(i * STEP, STEP)], sems.at[n, i])
            for n, (src, dst) in enumerate(pairs)
        ]
        for i in range(D // STEP)
    ]
    edges = [
        pltpu.make_async_copy(t_hbm.at[0], zlo.at[7], edge_sems.at[0]),
        pltpu.make_async_copy(t_hbm.at[D - 1], zhi.at[7], edge_sems.at[1]),
    ]
    for group in copies:
        for copy in group:
            copy.start()
    for copy in edges:
        copy.start()
    r = rows_of((8, X))
    outs = []
    for i, group in enumerate(copies):
        for copy in group:
            copy.wait()

        def two(m, carry):
            ce, co = conduct_of(s_ref[2 * m]), conduct_of(s_ref[2 * m + 1])
            be, bo, ke, ko = b_ref[2 * m], b_ref[2 * m + 1], k_ref[2 * m], k_ref[2 * m + 1]
            even = jnp.where(r < 2, ce, jnp.where(r == 2, rot(be, 2), rot(ke, 3)))
            odd = jnp.where(r < 6, rot(co, 4), jnp.where(r == 6, rot(bo, 6), rot(ko, 7)))
            ylo[m] = jnp.where(r < 4, even, odd)
            even = jnp.where(r > 1, rot(ce, 4), jnp.where(r == 1, rot(be, 2), rot(ke, 1)))
            odd = jnp.where(r > 5, co, jnp.where(r == 5, rot(bo, -2), rot(ko, -3)))
            yhi[m] = jnp.where(r < 4, even, odd)
            return carry

        half = STEP // 2
        lax.fori_loop(i * half, (i + 1) * half, two, 0)
        part = pl.ds(i * half, half)
        outs += [
            pltpu.make_async_copy(ylo.at[part], ylo_hbm.at[part], out_sems.at[0, i]),
            pltpu.make_async_copy(yhi.at[part], yhi_hbm.at[part], out_sems.at[1, i]),
        ]
        outs[-2].start()
        outs[-1].start()
    for copy in edges:
        copy.wait()
    for dst, at in ((zlo, lambda j: j), (zhi, lambda j: D - 1 - j)):
        for j in range(3):
            dst[j] = conduct_of(s_ref[at(j)])
        for j in range(2):
            dst[3 + j] = b_ref[at(j)]
            dst[5 + j] = k_ref[at(j)]
    outs += [
        pltpu.make_async_copy(zlo, zlo_hbm, out_sems.at[2, 0]),
        pltpu.make_async_copy(zhi, zhi_hbm, out_sems.at[2, 1]),
    ]
    outs[-2].start()
    outs[-1].start()
    for copy in outs:
        copy.wait()


def build_own(s_ref, b_ref, k_ref, zlo, zhi, C, B, FX, FZ, DP, mlo, mhi, RS, FS, AS):
    lane = lax.broadcasted_iota(jnp.int32, (8, 128), 1)
    row = lax.broadcasted_iota(jnp.int32, (8, 128), 0)

    def own(z, carry):
        C[z + 3] = conduct_of(s_ref[z])
        B[z + 3] = b_ref[z]
        DP[z + 3] = k_ref[z]
        return carry

    lax.fori_loop(0, D, own, 0)
    for src, at in ((zlo, lambda j: 2 - j), (zhi, lambda j: 27 + j)):
        for j in range(3):
            C[at(j)] = src[j]
        for j in range(2):
            B[at(j)] = src[3 + j]
            DP[at(j)] = src[5 + j]
    FZ[0] = C[0] + C[1]

    def plane(p, inner):
        rots, last = {}, None
        for k in range(NK):
            sl = tile_at(k)
            c = C[p, :, sl]
            nxt = left_shift(lambda m: C[p, :, tile_at(m)], k, lane, rots)
            fx = c + nxt
            if k == NK - 1:
                nxt = jnp.where(lane == 127, 0.0, nxt)
                fx = jnp.where(lane == 127, 0.0, fx)
            back = pltpu.roll(c, 1, 1)
            before = jnp.where(lane == 0, 0.0 if last is None else last, back)
            last = back
            up = jnp.where(row == 7, 0.0, pltpu.roll(c, 7, 0))
            down = jnp.where(row == 0, 0.0, pltpu.roll(c, 1, 0))
            cz = C[p + 1, :, sl]
            FX[p, :, sl] = fx
            FZ[p, :, sl] = c + cz
            coup = DP[p, :, sl]
            diag = coup + (3.0 * c + 0.5 * (nxt + before + up + down + cz + C[p - 1, :, sl]))
            diag = jnp.where(coup > 0.0, diag, 0.0)
            DP[p, :, sl] = diag
            if inner:
                at = pl.ds(pl.multiple_of((p - 3) * 8, 8), 8)
                rd = 1.0 / diag
                RS[k, at] = (1.0 / 3.0) * rd
                AS[k, at] = B[p, :, sl] * rd
                FS[k, at] = c + up

    def inside(p, carry):
        plane(p, True)
        return carry

    def outside(i, carry):
        plane(jnp.where(i < 2, 1 + i, 25 + i), False)
        return carry

    lax.fori_loop(3, E - 3, inside, 0, unroll=2)
    lax.fori_loop(0, 4, outside, 0)
    r = rows_of((8, X))
    for i, src in enumerate((zlo, zhi)):
        c1, c2, b1, k1 = src[0], src[1], src[3], src[5]
        mlo[i] = jnp.where(r < 2, c1, jnp.where(r == 2, rot(c2, 2), jnp.where(r == 3, rot(b1, 3), rot(k1, 4))))
        mhi[i] = jnp.where(r > 5, c1, jnp.where(r == 5, rot(c2, -2), jnp.where(r == 4, rot(b1, -3), rot(k1, -4))))
    for g in range(D // 8):
        for k in range(NK):
            sl = tile_at(k)
            mlo[2 + g, :, sl] = AS[k, pl.ds(64 * g + 1, 8, stride=8), :]
            mhi[2 + g, :, sl] = AS[k, pl.ds(64 * g + 6, 8, stride=8), :]


def pack_third(t_ref, RS, FS, hlo, hhi):
    r = rows_of((8, X))
    for g in range(D // 8):
        for k in range(NK):
            sl = tile_at(k)
            for n, (src, low, high) in enumerate(((RS, 1, 6), (FS, 1, 5))):
                hlo[3 * g + n, :, sl] = src[k, pl.ds(64 * g + low, 8, stride=8), :]
                hhi[3 * g + n, :, sl] = src[k, pl.ds(64 * g + high, 8, stride=8), :]
        low = high = t_ref[8 * g]
        high = rot(high, 1)
        for j in range(1, 8):
            t = t_ref[8 * g + j]
            low = jnp.where(r == j, rot(t, j), low)
            high = jnp.where(r == j, rot(t, j - 7), high)
        hlo[3 * g + 2] = low
        hhi[3 * g + 2] = high


def pack_corners_second(zlo, zhi, w3lo, w3hi, lo, hi):
    r = rows_of((8, X))
    for g in range(D // 8):
        lo[2 + g] = w3lo[g]
        hi[2 + g] = w3hi[g]
    for i, src in enumerate((zlo, zhi)):
        lo[i] = jnp.where(r < 2, src[0], rot(src[1], 2))
        hi[i] = jnp.where(r > 5, src[0], rot(src[1], -2))


def assemble(yhi, ylo, mhi, mlo, C, B, K):
    r = rows_of((8, X))
    zero = jnp.zeros((8, X), F32)

    def two(m, carry):
        h, l = yhi[m], ylo[m]
        p = 2 * m + 3
        C[p] = jnp.where(r < 2, h, jnp.where(r > 5, rot(l, 4), 0.0))
        B[p] = jnp.where(r == 0, rot(h, -2), jnp.where(r == 7, rot(l, 6), 0.0))
        K[p] = jnp.where(r == 0, rot(h, -3), jnp.where(r == 7, rot(l, 7), 0.0))
        C[p + 1] = jnp.where(r < 2, rot(h, -4), jnp.where(r > 5, l, 0.0))
        B[p + 1] = jnp.where(r == 0, rot(h, -6), jnp.where(r == 7, rot(l, 2), 0.0))
        K[p + 1] = jnp.where(r == 0, rot(h, -7), jnp.where(r == 7, rot(l, 3), 0.0))
        return carry

    lax.fori_loop(0, D // 2, two, 0)
    for i, at in ((0, lambda j: 2 - j), (1, lambda j: 27 + j)):
        h, l = mhi[i], mlo[i]
        C[at(0)] = jnp.where(r < 2, h, jnp.where(r > 5, l, 0.0))
        C[at(1)] = jnp.where(r == 0, rot(h, -2), jnp.where(r == 7, rot(l, 2), 0.0))
        C[at(2)] = zero
        B[at(0)] = jnp.where(r == 0, rot(h, -3), jnp.where(r == 7, rot(l, 3), 0.0))
        K[at(0)] = jnp.where(r == 0, rot(h, -4), jnp.where(r == 7, rot(l, 4), 0.0))
        B[at(1)] = zero
        K[at(1)] = zero


def tile_at(k):
    return slice(128 * k, 128 * k + 128)


def left_shift(load, k, lane, rots):
    for m in (k, (k + 1) % NK):
        if m not in rots:
            rots[m] = pltpu.roll(load(m), 127, 1)
    return jnp.where(lane == 127, rots[(k + 1) % NK], rots[k])


def build(C, B, DP, A, A0, RD, FX, FY, FZ):
    lane = lax.broadcasted_iota(jnp.int32, (8, 128), 1)
    row = lax.broadcasted_iota(jnp.int32, (8, 128), 0)
    top, bottom = row == 0, row == 7

    def plane(p, carry):
        rots, last = {}, None
        for k in range(NK):
            sl = tile_at(k)
            own, c = C[0][p, :, sl], C[1][p, :, sl]
            own_up, own_down = pltpu.roll(own, 7, 0), pltpu.roll(own, 1, 0)
            up, down = pltpu.roll(c, 7, 0), pltpu.roll(c, 1, 0)
            FY[0][p, :, sl] = own + jnp.where(bottom, up, own_up)
            beside = jnp.where(bottom, up, jnp.where(top, down, 0.0))
            up, down = jnp.where(bottom, own_up, up), jnp.where(top, own_down, down)
            FY[1][p, :, sl] = c + up
            part = DP[p, :, sl]
            rd = jnp.where(part > 0.0, 1.0 / jnp.where(part > 0.0, part + 0.5 * beside, 1.0), 0.0)
            a = B[p, :, sl] * rd
            A[0][p, :, sl] = a
            A0[0][p, :, sl] = (2.0 / 3.0) * a
            RD[0][p, :, sl] = (1.0 / 3.0) * rd

            nxt = left_shift(lambda m: C[1][p, :, tile_at(m)], k, lane, rots)
            fx = c + nxt
            if k == NK - 1:
                nxt = jnp.where(lane == 127, 0.0, nxt)
                fx = jnp.where(lane == 127, 0.0, fx)
            back = pltpu.roll(c, 1, 1)
            before = jnp.where(lane == 0, 0.0 if last is None else last, back)
            last = back
            cz = C[1][p + 1, :, sl]
            FX[1][p, :, sl] = fx
            FZ[1][p, :, sl] = c + cz
            coup = RD[1][p, :, sl]
            diag = coup + (3.0 * c + 0.5 * (nxt + before + up + down + cz + C[1][p - 1, :, sl]))
            rd = jnp.where(coup > 0.0, 1.0 / jnp.where(coup > 0.0, diag, 1.0), 0.0)
            a = A[1][p, :, sl] * rd
            A[1][p, :, sl] = a
            A0[1][p, :, sl] = (2.0 / 3.0) * a
            RD[1][p, :, sl] = (1.0 / 3.0) * rd
        return carry

    lax.fori_loop(1, E - 1, plane, 0, unroll=4)


def unpack_third(hhi, hlo, RD, FY, RDN, FYN, TH):
    r = rows_of((8, X))

    def group(g, carry):
        for j in range(8):
            p = 3 + 8 * g + j
            RDN[p] = jnp.where(r == 1, rot(hhi[3 * g], 1 - j), jnp.where(r == 6, rot(hlo[3 * g], 6 - j), RD[p]))
            FYN[p] = jnp.where(r == 1, rot(hhi[3 * g + 1], 1 - j), jnp.where(r == 5, rot(hlo[3 * g + 1], 5 - j), FY[p]))
            TH[8 * g + j] = jnp.where(r == 7, rot(hhi[3 * g + 2], 7 - j), rot(hlo[3 * g + 2], -j))
        return carry

    lax.fori_loop(0, D // 8, group, 0)
    for p in (0, 1, 2, 27, 28, 29):
        RDN[p] = RD[p]
        FYN[p] = FY[p]


def sweep(A, OUT, A0, RD, FX, FY, FZ, runs):
    lane = lax.broadcasted_iota(jnp.int32, (8, 128), 1)
    row = lax.broadcasted_iota(jnp.int32, (8, 128), 0)
    first, last, top, bottom = lane == 0, lane == 127, row == 0, row == 7

    def plane(p, tiles):
        ahead, back = {}, {}

        def shift(m):
            if (m, tiles[0]) in ahead:
                return
            sl = tile_at(m)
            for h in tiles:
                a = A[h][p, :, sl]
                ahead[m, h] = pltpu.roll(a, 127, 1)
                back[m, h] = pltpu.roll(FX[h][p, :, sl] * a, 1, 1)

        shift(NK - 1)
        shift(0)
        for k in range(NK):
            sl = tile_at(k)
            shift((k + 1) % NK)
            a = [A[h][p, :, sl] for h in (0, 1)]
            fy = [FY[h][p, :, sl] for h in (0, 1)]
            up = [pltpu.roll(x, 7, 0) for x in a]
            down = [pltpu.roll(f * x, 1, 0) for f, x in zip(fy, a)]
            for h in tiles:
                flux = FX[h][p, :, sl] * jnp.where(last, ahead[(k + 1) % NK, h], ahead[k, h])
                flux = flux + jnp.where(first, back[(k - 1) % NK, h], back[k, h])
                flux = flux + (fy[h] * jnp.where(bottom, up[1 - h], up[h]) + jnp.where(top, down[1 - h], down[h]))
                flux = flux + (FZ[h][p, :, sl] * A[h][p + 1, :, sl] + FZ[h][p - 1, :, sl] * A[h][p - 1, :, sl])
                OUT[h][p, :, sl] = (1.0 / 3.0) * a[h] + (A0[h][p, :, sl] + RD[h][p, :, sl] * flux)

    for tiles, low, count in runs:
        group = 6 if count % 6 == 0 else 2

        def planes(i, carry):
            for q in range(group):
                plane(low + group * i + q, tiles)
            return carry

        if isinstance(low, int):
            lax.fori_loop(0, count // group, planes, 0)
        else:

            def single(i, carry):
                plane(low(i), tiles)
                return carry

            lax.fori_loop(0, count, single, 0)


INNER = ((0, 1), 3, D)
OWN = ((0,), 3, D)
NEXT = ((0,), lambda i: 2 + (D + 1) * i, 2)


def sweeps_first(C0, B0, FX0, FZ0, DP, yhi, ylo, mhi, mlo,
                 a_out, y2lo, y2hi, w3lo, w3hi, z2lo, z2hi, FY0, RD0, R0, FX1, FY1, FZ1, RD1, R1, C1, A_0, A_1, O_0, O_1):
    FX, FY, FZ, RD, A0, A, OUT = (FX0, FX1), (FY0, FY1), (FZ0, FZ1), (RD0, RD1), (R0, R1), (A_0, A_1), (O_0, O_1)
    assemble(yhi, ylo, mhi, mlo, C1, A_1, RD1)
    build((C0, C1), B0, DP, A, A0, RD, FX, FY, FZ)
    r = rows_of((8, X))

    def second_rows(g, carry):
        for j in range(8):
            p = 3 + 8 * g + j
            a = jnp.where(r == 1, rot(mhi[2 + g], 1 - j), jnp.where(r == 6, rot(mlo[2 + g], 6 - j), A_1[p]))
            A_1[p] = a
            R1[p] = (2.0 / 3.0) * a
        return carry

    lax.fori_loop(0, D // 8, second_rows, 0)
    sweep(A, OUT, A0, RD, FX, FY, FZ, (INNER, NEXT))
    sweep(OUT, A, A0, RD, FX, FY, FZ, (OWN,))
    A = A_0

    def copy(z, carry):
        a_out[z] = A[z + 3]
        return carry

    lax.fori_loop(0, D, copy, 0)

    def group(g, carry):
        for i in range(2):
            low, high = None, None
            for j in range(4):
                a = A[8 * g + 4 * i + j + 3]
                mask = (r >= 2 * j) & (r < 2 * j + 2)
                low = rot(a, 2 * j) if low is None else jnp.where(mask, rot(a, 2 * j), low)
                high = rot(a, 2 * j - 6) if high is None else jnp.where(mask, rot(a, 2 * j - 6), high)
            y2lo[2 * g + i] = low
            y2hi[2 * g + i] = high
        low, high = None, None
        for j in range(8):
            a = A[8 * g + j + 3]
            low = rot(a, j - 2) if low is None else jnp.where(r == j, rot(a, j - 2), low)
            high = rot(a, j - 5) if high is None else jnp.where(r == j, rot(a, j - 5), high)
        w3lo[g] = low
        w3hi[g] = high
        return carry

    lax.fori_loop(0, D // 8, group, 0)
    for j in range(3):
        z2lo[j] = A[3 + j]
        z2hi[j] = A[26 - j]


def tri(u):
    m = jnp.maximum(RADIUS - u, 0)
    return m * (m + 1) // 2


def inv_cover(position, length):
    total = (RADIUS + 1) ** 2 - tri(position) - tri(length - 1 - position)
    return 1.0 / total.astype(F32)


def third_sweep_own(info, s_ref, t_ref, zlo, zhi, a_in, FX0, FZ0, FY0, FYN, RD0, R0, y2hi, y2lo, z2lo, z2hi,
                    A_0, A_1, B_0, T, DX, SC):
    r = rows_of((8, X))

    def group(g, carry):
        for j in range(8):
            z = 8 * g + j
            A_0[z + 3] = a_in[z]
            tile, at = 2 * g + j // 4, 2 * (j % 4)
            A_1[z + 3] = jnp.where(r < 2, rot(y2hi[tile], -at), jnp.where(r > 5, rot(y2lo[tile], 6 - at), 0.0))
        return carry

    lax.fori_loop(0, 3, group, 0)
    for src, at in ((z2lo, lambda j: 2 - j), (z2hi, lambda j: 27 + j)):
        for j in range(3):
            A_0[at(j)] = src[j]
    for p in (0, 1, 2, 27, 28, 29):
        A_1[p] = jnp.zeros((8, X), F32)
    sweep((A_0, A_1), (B_0,), (R0,), (RD0,), (FX0,), (FY0, FYN), (FZ0,), (OWN,))

    lane8 = lax.broadcasted_iota(jnp.int32, (8, 128), 1)
    row8 = lax.broadcasted_iota(jnp.int32, (8, 128), 0)
    cover_y = inv_cover(lax.axis_index("blk") * S + row8, 16 * S)
    base_z = lax.axis_index("grp") * D
    factor = -0.5 * 3.0 * (1.0 - COND_FLOOR)

    def plane_t(z, carry):
        base = cover_y * inv_cover(base_z + z + jnp.zeros((8, 128), jnp.int32), 16 * D) * factor
        rt = {}
        for k in range(NK):
            sl = tile_at(k)
            t = t_ref[z, :, sl]
            tn = left_shift(lambda m: t_ref[z, :, tile_at(m)], k, lane8, rt)
            if k == NK - 1:
                tn = jnp.where(lane8 == 127, 0.0, tn)
            T[z + 1, :, sl] = t
            DX[z, :, sl] = t - tn
            s = s_ref[z, :, sl]
            scale = base * info[k // 2].astype(F32)
            if k in (0, NK - 1):
                scale = scale * inv_cover(lane8 + 128 * k, X)
            else:
                scale = scale * (1.0 / float((RADIUS + 1) ** 2))
            SC[z, :, sl] = (s * s) * scale
        return carry

    lax.fori_loop(0, D, plane_t, 0, unroll=2)

    T[0] = zlo[7]
    T[D + 1] = zhi[7]


def sweeps_second(TH, A_0, A_in, B_in, T, DX, SC, FX0, FZ0, FY0, RD0, R0, FX1, FYN, FZ1, RDN, R1,
                  e_hi, e_lo, send_any, late, sums, A_1, B_0, B_1, O_0, R, send, sems):
    O_1 = A_1
    r = rows_of((8, X))

    def group(g, carry):
        for j in range(8):
            p = 8 * g + j + 3
            A_1[p] = jnp.where(r == 2, rot(e_hi[2 + g], 2 - j), jnp.where(r == 5, rot(e_lo[2 + g], 5 - j), A_in[p]))
            B_0[p] = B_in[p]
        return carry

    lax.fori_loop(0, 3, group, 0)
    for i, at in ((0, lambda j: 2 - j), (1, lambda j: 27 + j)):
        h, l = e_hi[i], e_lo[i]
        A_1[at(0)] = jnp.where(r < 2, h, jnp.where(r > 5, l, 0.0))
        A_1[at(1)] = jnp.where(r == 0, rot(h, -2), jnp.where(r == 7, rot(l, 2), 0.0))
    FX, FY, FZ, RD, A0 = (FX0, FX1), (FY0, FYN), (FZ0, FZ1), (RD0, RDN), (R0, R1)
    outer = ((0,), lambda i: jnp.where(i < 2, 1 + i, 25 + i), 4)
    sweep((A_0, A_1), (B_0, B_1), A0, RD, FX, FY, FZ, (((1,), 2, D + 2), outer))
    sweep((B_0, B_1), (O_0, O_1), A0, RD, FX, FY, FZ, (INNER, NEXT))

    lane8 = lax.broadcasted_iota(jnp.int32, (8, 128), 1)
    row8 = lax.broadcasted_iota(jnp.int32, (8, 128), 0)

    def plane_raw(z, carry):
        p = z + 3
        ra = {}
        last = None
        for k in range(NK):
            sl = tile_at(k)
            a, side, t, edge = O_0[p, :, sl], O_1[p, :, sl], T[z + 1, :, sl], TH[z, :, sl]
            an = left_shift(lambda m: O_0[p, :, tile_at(m)], k, lane8, ra)
            if k == NK - 1:
                an = jnp.where(lane8 == 127, 0.0, an)
            px = (a - an) * DX[z, :, sl]
            back = pltpu.roll(px, 1, 1)
            pair = px + jnp.where(lane8 == 0, a * t if last is None else last, back)
            last = back
            au = jnp.where(row8 == 7, rot(side, -1), rot(a, -1))
            ad = jnp.where(row8 == 0, rot(side, 1), rot(a, 1))
            tu, td = jnp.where(row8 == 7, edge, rot(t, -1)), jnp.where(row8 == 0, edge, rot(t, 1))
            pair = pair + ((a - au) * (t - tu) + (a - ad) * (t - td))
            pair = pair + (a - O_0[p + 1, :, sl]) * (t - T[z + 2, :, sl])
            pair = pair + (a - O_0[p - 1, :, sl]) * (t - T[z, :, sl])
            R[pl.ds(pl.multiple_of(z * 8, 8), 8), sl] = pair * SC[z, :, sl]
        return carry

    lax.fori_loop(0, D, plane_raw, 0, unroll=2)

    i = lax.broadcasted_iota(jnp.int32, (512, 256), 0) - 128
    j = lax.broadcasted_iota(jnp.int32, (512, 256), 1)
    weights = jnp.maximum(RADIUS + 1 - jnp.abs(i - j), 0).astype(F32).astype(BF16)
    for n in range(X // 256):
        low, high = max(256 * n - 128, 0), min(256 * n + 384, X)
        x = R[:, low:high]
        w = weights[low - (256 * n - 128) : high - (256 * n - 128)]
        xh = x.astype(BF16)
        xl = (x - xh.astype(F32)).astype(BF16)
        y = jnp.dot(xh, w, preferred_element_type=F32) + jnp.dot(xl, w, preferred_element_type=F32)
        for h in range(2):
            part, m = y[:, 128 * h : 128 * h + 128], (2 * n + h) % HALF
            if n < X // 512:
                send[m] = part[0 : 4 * D]
                send[HALF + m] = part[4 * D :]
            else:
                late[m] = part
                layers = [part[8 * z : 8 * z + 8] for z in range(D)]
                sums[0, 8 * m : 8 * m + 8] = sum(layers)
                sums[1, 8 * m : 8 * m + 8] = sum(float(z) * layers[z] for z in range(1, D))
        if n == X // 512 - 1:
            copy = pltpu.make_async_copy(send, send_any, sems.at[0])
            copy.start()
    copy.wait()


def filter_y(x_ref, out_any, out, sems):
    i = lax.broadcasted_iota(jnp.int32, (128, 128), 0)
    j = lax.broadcasted_iota(jnp.int32, (128, 128), 1)
    w = jnp.maximum(RADIUS + 1 - jnp.abs(i - j), 0).astype(F32).astype(BF16)
    copies = []
    for z in range(D // 2):
        x = x_ref[:, 8 * z : 8 * z + 8, :].reshape(128, 128)
        xh = x.astype(BF16)
        xl = (x - xh.astype(F32)).astype(BF16)
        y = jnp.dot(w, xh, preferred_element_type=F32) + jnp.dot(w, xl, preferred_element_type=F32)
        out[:, 8 * z : 8 * z + 8, :] = y.reshape(16, 8, 128)
        if z % 4 == 3:
            part = pl.ds(8 * (z - 3), 32)
            copies.append(pltpu.make_async_copy(out.at[:, part], out_any.at[:, part], sems.at[z // 4]))
            copies[-1].start()
    for copy in copies:
        copy.wait()


def whole_layer(ref, m, z):
    return ref[m, 8 * z : 8 * z + 8, :]


def split_layer(ref, m, z):
    return ref[HALF * (z // (D // 2)) + m, 8 * (z % (D // 2)) : 8 * (z % (D // 2)) + 8, :]


def layer_sums(x_ref, sums):
    def chunk(m, carry):
        layers = [split_layer(x_ref, m, z) for z in range(D)]
        sl = pl.ds(pl.multiple_of(m * 8, 8), 8)
        sums[0, sl] = sum(layers)
        sums[1, sl] = sum(float(z) * layers[z] for z in range(1, D))
        return carry

    lax.fori_loop(0, HALF, chunk, 0)


def filter_z(load, m, own, up, down, up2, down2, store):
    sl = pl.ds(pl.multiple_of(m * 8, 8), 8)
    u0, u1, d0, d1 = up[0, sl, :], up[1, sl, :], down[0, sl, :], down[1, sl, :]
    suffix = load(down2, m, D - 1)
    total = suffix
    far = [None] * D
    far[D - 1] = total
    for z in range(D - 2, -1, -1):
        suffix = suffix + load(down2, m, z)
        total = total + suffix
        far[z] = total
    sum_own = load(own, m, 0)
    distance = jnp.zeros_like(sum_own)
    for z in range(1, D):
        x = load(own, m, z)
        sum_own = sum_own + x
        distance = distance + float(z) * x
    near = (25.0 * (u0 + d0) + (d1 - u1)) + float(RADIUS + 1) * sum_own
    slope = u0 - d0
    prefix_own = jnp.zeros_like(sum_own)
    prefix_up = jnp.zeros_like(sum_own)
    total_up = jnp.zeros_like(sum_own)
    for z in range(D):
        prefix_up = prefix_up + load(up2, m, z)
        total_up = total_up + prefix_up
        store(z, (near - distance) + (total_up + far[z]))
        prefix_own = prefix_own + load(own, m, z)
        distance = distance + (2.0 * prefix_own - sum_own)
        near = near + slope


def filter_z_late(own, up, down, up2, down2, out):
    def chunk(m, carry):
        def store(z, value):
            out[HALF * (z // (D // 2)) + m, 8 * (z % (D // 2)) : 8 * (z % (D // 2)) + 8, :] = value

        filter_z(whole_layer, m, own, up, down, up2, down2, store)
        return carry

    lax.fori_loop(0, HALF, chunk, 0)


def finish_early(info, own, up, down, up2, down2, out_hbm, out, sem):
    def chunk(m, carry):
        column = pl.ds(pl.multiple_of(m * 128, 128), 128)
        scale = REPORT_SCALE * info[m // 2].astype(F32)

        def store(z, value):
            out[z, :, column] = value * scale

        filter_z(split_layer, m, own, up, down, up2, down2, store)
        return carry

    lax.fori_loop(0, HALF, chunk, 0)
    copy = pltpu.make_async_copy(out, out_hbm.at[:, :, pl.ds(0, X // 2)], sem)
    copy.start()
    copy.wait()


def finish_late(info, late, half_done, out_hbm, out, sems):
    del half_done
    copies = []
    for part in range(2):
        for m in range(part * HALF // 2, (part + 1) * HALF // 2):
            scale = REPORT_SCALE * info[HALF // 2 + m // 2].astype(F32)
            for z in range(D):
                out[z, :, tile_at(m)] = split_layer(late, m, z) * scale
        column = pl.ds(part * X // 4, X // 4)
        target = pl.ds(X // 2 + part * X // 4, X // 4)
        copies.append(pltpu.make_async_copy(out.at[:, :, column], out_hbm.at[:, :, target], sems.at[part]))
        copies[-1].start()
    for copy in copies:
        copy.wait()


def kernel_call(body, ins, outs, scratch=(), scalars=0, limit=60, sems=0):
    vmem = pl.BlockSpec(memory_space=pltpu.VMEM)
    smem = pl.BlockSpec(memory_space=pltpu.SMEM)
    return pl.pallas_call(
        body,
        out_shape=[jax.ShapeDtypeStruct(s, F32) for s in outs],
        in_specs=[smem] * scalars + [vmem] * (len(ins) - scalars),
        out_specs=([pl.BlockSpec(memory_space=pl.ANY)] if sems else [vmem]) + [vmem] * (len(outs) - 1),
        scratch_shapes=[pltpu.VMEM(s, F32) for s in scratch] + ([pltpu.SemaphoreType.DMA((sems,))] if sems else []),
        compiler_params=pltpu.CompilerParams(vmem_limit_bytes=limit * MIB),
    )(*ins)


def moved(x, dz, dy):
    pairs = []
    for g in range(16):
        for b in range(16):
            if 0 <= g + dz < 16 and 0 <= b + dy < 16:
                pairs.append(((g + dz) * 16 + b + dy, g * 16 + b))
    return lax.ppermute(x, ("grp", "blk"), pairs)


def local(solid, thermal, target, coolant, switch):
    info = switch.reshape(8)
    block = (D, 8, X)
    near = tile_shape(D // 2)
    ylo, yhi, zlo, zhi = pl.pallas_call(
        pack_first,
        out_shape=[jax.ShapeDtypeStruct(shape, F32) for shape in (near, near, tile_shape(8), tile_shape(8))],
        in_specs=[pl.BlockSpec(memory_space=pltpu.HBM)] * 4,
        out_specs=[pl.BlockSpec(memory_space=pltpu.HBM)] * 4,
        scratch_shapes=[pltpu.VMEM(block, F32)] * 3
        + [pltpu.VMEM(near, F32)] * 2
        + [pltpu.VMEM(tile_shape(8), F32)] * 2
        + [pltpu.SemaphoreType.DMA((3, D // STEP)), pltpu.SemaphoreType.DMA((2,)), pltpu.SemaphoreType.DMA((3, D // STEP))],
        compiler_params=pltpu.CompilerParams(vmem_limit_bytes=52 * MIB),
    )(solid, thermal, target, coolant)
    yhi, ylo = moved(ylo, 0, 1), moved(yhi, 0, -1)
    zlo, zhi = moved(zhi, -1, 0), moved(zlo, 1, 0)
    ext, flat = (E, 8, X), (D * 8, X)
    rows = (NK, D * 8, 128)
    c, b, fx, fz, dp, mlo, mhi, rs, fs = kernel_call(
        build_own, (solid, target, coolant, zlo, zhi),
        [ext] * 5 + [tile_shape(5)] * 2 + [rows] * 2, [rows], limit=8,
    )
    hlo, hhi = kernel_call(pack_third, (thermal, rs, fs), [tile_shape(9)] * 2, limit=8)
    mhi, mlo = moved(mlo, 0, 1), moved(mhi, 0, -1)
    hhi, hlo = moved(hlo, 0, 1), moved(hhi, 0, -1)
    a, y2lo, y2hi, w3lo, w3hi, z2lo, z2hi, *fields = kernel_call(
        sweeps_first, (c, b, fx, fz, dp, yhi, ylo, mhi, mlo),
        [block, tile_shape(6), tile_shape(6)] + [tile_shape(3)] * 4 + [ext] * 8, [ext] * 5, limit=14,
    )
    y2hi, y2lo = moved(y2lo, 0, 1), moved(y2hi, 0, -1)
    z2lo, z2hi = moved(z2hi, -1, 0), moved(z2lo, 1, 0)
    fy0, rd0, r0, fx1, fy1, fz1, rd1, r1 = fields
    rd1, fy1, th = kernel_call(unpack_third, (hhi, hlo, rd1, fy1), [ext, ext, block], limit=8)
    clo, chi = kernel_call(pack_corners_second, (z2lo, z2hi, w3lo, w3hi), [tile_shape(5)] * 2, limit=8)
    e_hi, e_lo = moved(clo, 0, 1), moved(chi, 0, -1)
    parts, wide, small = (2 * HALF, D * 4, 128), (HALF, D * 8, 128), (2, HALF * 8, 128)
    a_0, a_1, b_0, *terms = kernel_call(
        third_sweep_own,
        (info, solid, thermal, zlo, zhi, a, fx, fz, fy0, fy1, rd0, r0, y2hi, y2lo, z2lo, z2hi),
        [ext] * 3 + [(D + 2, 8, X), block, block], scalars=1, limit=8,
    )
    send, late, sums = kernel_call(
        sweeps_second,
        (th, a_0, a_1, b_0, *terms, fx, fz, fy0, rd0, r0, fx1, fy1, fz1, rd1, r1, e_hi, e_lo),
        [parts, wide, small], [ext] * 4 + [flat, parts], limit=13, sems=1,
    )

    def exchanged(x):
        return lax.all_to_all(x, "blk", split_axis=0, concat_axis=0, tiled=True)

    columns = exchanged(send)
    up2, down2 = moved(late, 2, 0), moved(late, -2, 0)
    up, down = moved(sums, 1, 0), moved(sums, -1, 0)
    (columns,) = kernel_call(filter_y, (columns,), [parts], [parts], limit=8, sems=3)
    early = exchanged(columns)
    (late,) = kernel_call(filter_z_late, (late, up, down, up2, down2), [parts], limit=8)
    late = exchanged(late)
    up2, down2 = moved(early, 2, 0), moved(early, -2, 0)
    (sums,) = kernel_call(layer_sums, (early,), [small], limit=8)
    up, down = moved(sums, 1, 0), moved(sums, -1, 0)
    (late,) = kernel_call(filter_y, (late,), [parts], [parts], limit=8, sems=3)
    late = exchanged(late)
    smem, vmem, anywhere = (pl.BlockSpec(memory_space=space) for space in (pltpu.SMEM, pltpu.VMEM, pl.ANY))
    half = pltpu.VMEM((D, 8, X // 2), F32)
    out = pl.pallas_call(
        finish_early,
        out_shape=jax.ShapeDtypeStruct(block, F32),
        in_specs=[smem] + [vmem] * 5,
        out_specs=anywhere,
        scratch_shapes=[half, pltpu.SemaphoreType.DMA(())],
        compiler_params=pltpu.CompilerParams(vmem_limit_bytes=8 * MIB),
    )(info, early, up, down, up2, down2)
    return pl.pallas_call(
        finish_late,
        out_shape=jax.ShapeDtypeStruct(block, F32),
        in_specs=[smem, vmem, anywhere],
        out_specs=anywhere,
        scratch_shapes=[half, pltpu.SemaphoreType.DMA((2,))],
        input_output_aliases={2: 0},
        compiler_params=pltpu.CompilerParams(vmem_limit_bytes=8 * MIB),
    )(info, late, out)


def tile_shape(n):
    return (n, 8, X)


def solution(mesh):
    spec = P("grp", "blk", None)
    return jax.shard_map(
        local, mesh=mesh, in_specs=(spec,) * 5, out_specs=spec, check_vma=False
    )
```
